256 devices in a mesh: pipe: 16 (over z_lo, x, core), ctx: 16 (over y, z_hi).
Axes of the slice: x: 4, y: 4, z: 8 (z_hi: 4, z_lo: 2; z = z_hi * 2 + z_lo), core: 2. Of those that a mesh axis runs over, the one named last changes fastest.
Arguments:
- queries: bfloat16 [2, 16, 2048, 2560], P(None, 'pipe', 'ctx'), may hold values from -80 to 80
- keys: bfloat16 [2, 16, 2048, 512], P(None, 'pipe', 'ctx'), may hold values from -25 to 25
- values: bfloat16 [2, 16, 2048, 512], P(None, 'pipe', 'ctx'), may hold values from -6 to 6
- grad_a: bfloat16 [16, 2048, 2560], P('pipe', 'ctx'), may hold values from -96 to 96
- grad_b: bfloat16 [16, 2048, 2560], P('pipe', 'ctx'), may hold values from -48 to 48
- imports: int32 [2, 16, 16, 16], P(None, 'pipe'), may hold values from 0 to 1, as said below
- block_ids: int32 [2, 16, 16], P(None, 'pipe'), may hold values from 0 to 15, each once within a row
Outputs:
- dq_a: bfloat16 [16, 2048, 2560], P('pipe', 'ctx')
- dq_b: bfloat16 [16, 2048, 2560], P('pipe', 'ctx')
- kv_grads: bfloat16 [2, 16, 2048, 1024], P(None, 'pipe', 'ctx')
The draws below stay inside these ranges and needn't reach their ends.
Inputs may be any that keep to these rules, and one draw needn't show every extreme that they name: Every file block sees itself and imports at most 7 other blocks; in each micro-batch and section some block imports exactly 7.
All inputs are finite; a program needn't handle non-finite values.
Results may differ from the reference program's by a relative error of at most 0.015.
Values may be sent and summed in bfloat16 or wider, within the bound.
A program may use at most 64 MiB of HBM per device.

```python
import math
import jax
import jax.numpy as jnp
from jax import lax

QUERY_HEADS = 20
KEY_VALUE_HEADS = 4
HEAD_DIMENSION = 128
FILE_BLOCK_SIZE = 128
BPD = 1
MICRO_BATCHES = 2
FILE_BLOCKS = 16
MICRO_LENGTH = 2048
IMP = 7
N_PIPE = 16
N_CTX = 16


def pair_fields(key):
    base_key = jax.random.fold_in(key, 7)
    key_query, key_random_keys = jax.random.split(base_key, 2)
    query_part = jax.random.normal(key_query, (MICRO_BATCHES, N_PIPE, FILE_BLOCKS, FILE_BLOCK_SIZE, QUERY_HEADS, HEAD_DIMENSION), jnp.float32)
    key_portion = jax.random.normal(key_random_keys, (MICRO_BATCHES, N_PIPE, FILE_BLOCKS, FILE_BLOCK_SIZE, KEY_VALUE_HEADS, HEAD_DIMENSION), jnp.float32)
    return (query_part, key_portion)


def draw_queries(key, part):
    query_part, key_portion = pair_fields(key)
    return jnp.clip(query_part, -80.0, 80.0).reshape(MICRO_BATCHES, N_PIPE, MICRO_LENGTH, QUERY_HEADS * HEAD_DIMENSION).astype(jnp.bfloat16)


def draw_keys(key, part):
    query_part, key_portion = pair_fields(key)
    return jnp.clip(key_portion, -25.0, 25.0).reshape(MICRO_BATCHES, N_PIPE, MICRO_LENGTH, KEY_VALUE_HEADS * HEAD_DIMENSION).astype(jnp.bfloat16)


def draw_imports(key, part):
    base_key = jax.random.fold_in(key, 29)
    key_first, key_second, key_pick, key_rank = jax.random.split(base_key, 4)
    lead_shape = (MICRO_BATCHES, N_PIPE)
    first_draw = jax.random.randint(key_first, lead_shape + (FILE_BLOCKS,), 0, IMP + 1)
    second_draw = jax.random.randint(key_second, lead_shape + (FILE_BLOCKS,), 0, IMP + 1)
    counts = first_draw * second_draw // IMP
    chosen = jax.random.randint(key_pick, lead_shape + (1,), 0, FILE_BLOCKS)
    column = jnp.arange(FILE_BLOCKS, dtype=jnp.int32)
    counts = jnp.where(column[None, None, :] == chosen, IMP, counts)
    ranking = jax.random.randint(key_rank, lead_shape + (FILE_BLOCKS, FILE_BLOCKS), 0, 4096) * FILE_BLOCKS + column
    diagonal = column[:, None] == column[None, :]
    ranking = jnp.where(diagonal, 4096 * FILE_BLOCKS + FILE_BLOCKS, ranking)
    sort_order = jnp.argsort(ranking, axis=-1, stable=True)
    position = jnp.argsort(sort_order, axis=-1, stable=True)
    selected_entries = (position < counts[..., None]) | diagonal
    return selected_entries.astype(jnp.int32)


def shard_levels(rng, extent, shards, least, largest):
    gain, own = 1.0, jax.random.fold_in(rng, 6)
    for dim, blocks in shards:
        draws = jnp.exp(jax.random.uniform(jax.random.fold_in(own, dim), (blocks,), jnp.float32, least / len(shards), largest / len(shards)))
        gain = gain * jnp.repeat(draws, extent[dim] // blocks).reshape([-1 if axis == dim else 1 for axis in range(len(extent))])
    return gain


def bell_draw(key, extent, deviation, reach, cuts=(), kind=jnp.bfloat16):
    drawn = jax.random.normal(key, extent, jnp.float32) * deviation
    if len(cuts) > 0:
        drawn = shard_levels(key, extent, cuts, -0.22, 0.18) * drawn
    return jnp.clip(drawn, min=-reach, max=reach).astype(kind)


def setup_inputs(seed: int = 0) -> dict:
    seeds = jax.random.split(jax.random.key(seed), 8)
    queries = draw_queries(jax.random.fold_in(seeds[7], 71), 0)
    keys = draw_keys(jax.random.fold_in(seeds[7], 71), 0)
    values = bell_draw(seeds[2], (MICRO_BATCHES, N_PIPE, MICRO_LENGTH, KEY_VALUE_HEADS * HEAD_DIMENSION), 1.0, 6.0, ((1, 16), (2, 16)))
    grad_a = bell_draw(seeds[3], (N_PIPE, MICRO_LENGTH, QUERY_HEADS * HEAD_DIMENSION), 16.0, 96.0, ((0, 16), (1, 16)))
    grad_b = bell_draw(seeds[4], (N_PIPE, MICRO_LENGTH, QUERY_HEADS * HEAD_DIMENSION), 8.0, 48.0, ((0, 16), (1, 16)))
    imports = draw_imports(jax.random.fold_in(seeds[7], 71), 0)
    block_ids = jax.vmap(lambda own: jax.random.permutation(own, FILE_BLOCKS))(jax.random.split(seeds[6], MICRO_BATCHES * N_PIPE)).reshape((MICRO_BATCHES, N_PIPE, FILE_BLOCKS)).astype(jnp.int32)
    return dict(queries=queries, keys=keys, values=values, grad_a=grad_a, grad_b=grad_b, imports=imports, block_ids=block_ids)


negative_large = -1e+30

def lowered(values_in):
    return lax.optimization_barrier(values_in.astype(jnp.bfloat16)).astype(jnp.float32)

def slot_table(import_mask, block_order):
    onehot = (block_order[:, None] == jnp.arange(FILE_BLOCKS, dtype=jnp.int32)[None, :]).astype(jnp.float32)
    mapped = jnp.dot(onehot, import_mask.astype(jnp.float32), precision=lax.Precision.HIGHEST)
    return jnp.dot(mapped, onehot.T, precision=lax.Precision.HIGHEST)

def block_grads(query_row_tensor, gradient_rows, selected_keys, selected_values, key_slots, key_live, slot_index, softmax_scale):
    query_group_width = QUERY_HEADS // KEY_VALUE_HEADS
    selected_entries = key_slots.shape[0]
    query_head_tensor = query_row_tensor.astype(jnp.float32).reshape(FILE_BLOCK_SIZE, KEY_VALUE_HEADS, query_group_width, HEAD_DIMENSION)
    gradient_heads = gradient_rows.astype(jnp.float32).reshape(FILE_BLOCK_SIZE, KEY_VALUE_HEADS, query_group_width, HEAD_DIMENSION)
    flattened_keys = selected_keys.astype(jnp.float32).reshape(selected_entries * FILE_BLOCK_SIZE, KEY_VALUE_HEADS, HEAD_DIMENSION)
    flattened_values = selected_values.astype(jnp.float32).reshape(selected_entries * FILE_BLOCK_SIZE, KEY_VALUE_HEADS, HEAD_DIMENSION)
    column_slot = jnp.repeat(key_slots, FILE_BLOCK_SIZE)
    column_place = jnp.tile(jnp.arange(FILE_BLOCK_SIZE, dtype=jnp.int32), selected_entries)
    column_live = jnp.repeat(key_live, FILE_BLOCK_SIZE)
    row_place = jnp.arange(FILE_BLOCK_SIZE, dtype=jnp.int32)
    allowed = column_live[None, :] & ((column_slot != slot_index)[None, :] | (column_place[None, :] <= row_place[:, None]))
    scores = jnp.einsum('rhgd,khd->hgrk', query_head_tensor, flattened_keys) * softmax_scale
    masked = jnp.where(allowed, scores, negative_large)
    row_max = lax.optimization_barrier(jnp.max(masked, axis=-1))
    expo = jnp.where(allowed, jnp.exp(masked - row_max[..., None]), 0.0)
    row_sum = lax.optimization_barrier(jnp.sum(expo, axis=-1))
    weighted = jnp.einsum('hgrk,khd->rhgd', lowered(expo), flattened_values)
    attended = weighted / jnp.transpose(row_sum, (2, 0, 1))[..., None]
    log_total = row_max + jnp.log(row_sum)
    delta = jnp.transpose(lax.optimization_barrier(jnp.sum(gradient_heads * attended, axis=-1)), (1, 2, 0))
    probs = jnp.where(allowed, jnp.exp(jnp.where(allowed, scores - log_total[..., None], negative_large)), 0.0)
    value_gradient = jnp.einsum('hgrk,rhgd->khd', lowered(probs), gradient_heads)
    prob_grad = jnp.einsum('rhgd,khd->hgrk', gradient_heads, flattened_values)
    score_grad = lowered(probs * (prob_grad - delta[..., None]))
    q_grad = jnp.einsum('hgrk,khd->rhgd', score_grad, flattened_keys) * softmax_scale
    key_gradient = jnp.einsum('hgrk,rhgd->khd', score_grad, query_head_tensor) * softmax_scale
    key_value_block = jnp.concatenate([key_gradient.reshape(selected_entries * FILE_BLOCK_SIZE, KEY_VALUE_HEADS * HEAD_DIMENSION), value_gradient.reshape(selected_entries * FILE_BLOCK_SIZE, KEY_VALUE_HEADS * HEAD_DIMENSION)], axis=1)
    return (q_grad.reshape(FILE_BLOCK_SIZE, QUERY_HEADS * HEAD_DIMENSION), key_value_block)

def section_micro(query_all, every_key, every_value, incoming_gradient, import_mask, block_order, softmax_scale):
    slot_mask = slot_table(import_mask, block_order)
    column_counts = 2 * KEY_VALUE_HEADS * HEAD_DIMENSION
    key_block_list = every_key.reshape(FILE_BLOCKS, FILE_BLOCK_SIZE, KEY_VALUE_HEADS, HEAD_DIMENSION)
    value_block_list = every_value.reshape(FILE_BLOCKS, FILE_BLOCK_SIZE, KEY_VALUE_HEADS, HEAD_DIMENSION)

    def device_turn(carried, device):
        partial_sum = jnp.zeros((FILE_BLOCKS, FILE_BLOCK_SIZE, column_counts), jnp.float32)
        q_parts = []
        for local_index in range(BPD):
            slot_index = (device * BPD + local_index).astype(jnp.int32)
            query_row_tensor = lax.dynamic_slice_in_dim(query_all, slot_index * FILE_BLOCK_SIZE, FILE_BLOCK_SIZE, 0)
            gradient_rows = lax.dynamic_slice_in_dim(incoming_gradient, slot_index * FILE_BLOCK_SIZE, FILE_BLOCK_SIZE, 0)
            reachable = lax.dynamic_index_in_dim(slot_mask, slot_index, 0, keepdims=False)
            live_keys = (reachable > 0.5).astype(jnp.int32)
            sort_order = jnp.argsort(1 - live_keys, stable=True)[:IMP + 1].astype(jnp.int32)
            key_live = jnp.take(live_keys, sort_order) > 0
            q_grad, key_value_block = block_grads(query_row_tensor, gradient_rows, key_block_list[sort_order], value_block_list[sort_order], sort_order, key_live, slot_index, softmax_scale)
            partial_sum = partial_sum.at[sort_order].add(key_value_block.reshape(IMP + 1, FILE_BLOCK_SIZE, column_counts))
            q_parts.append(q_grad)
        rounded = lowered(partial_sum).reshape(MICRO_LENGTH, column_counts)
        return (carried + rounded, jnp.concatenate(q_parts, axis=0))
    totals, q_grads = lax.scan(device_turn, jnp.zeros((MICRO_LENGTH, column_counts), jnp.float32), jnp.arange(N_CTX, dtype=jnp.int32))
    return (q_grads.reshape(MICRO_LENGTH, QUERY_HEADS * HEAD_DIMENSION), totals)

def reference(queries, keys, values, grad_a, grad_b, imports, block_ids):
    softmax_scale = 1.0 / math.sqrt(HEAD_DIMENSION)

    def section_fn(section_args):
        query_all, every_key, every_value, incoming_gradient, import_mask, block_order = section_args
        return section_micro(query_all, every_key, every_value, incoming_gradient, import_mask, block_order, softmax_scale)
    q_first, kv_first = lax.map(section_fn, (queries[0], keys[0], values[0], grad_a, imports[0], block_ids[0]))
    dq_a = q_first.astype(jnp.bfloat16)
    arrived = jnp.concatenate([dq_a[1:], jnp.zeros_like(dq_a[:1])], axis=0)
    upstream_b = (grad_b.astype(jnp.float32) + arrived.astype(jnp.float32)).astype(jnp.bfloat16)
    q_second, kv_second = lax.map(section_fn, (queries[1], keys[1], values[1], upstream_b, imports[1], block_ids[1]))
    kv_grads = jnp.stack([kv_first, kv_second]).astype(jnp.bfloat16)
    return (dq_a, q_second.astype(jnp.bfloat16), kv_grads)
```

```python
import functools
import math

import jax
import jax.numpy as jnp
from jax import lax
from jax.experimental import pallas as pl
from jax.experimental.pallas import tpu as pltpu
from jax.sharding import PartitionSpec as P

KEY_VALUE_HEADS = 4
HEAD = 128
GROUP = 5
WIDE = GROUP * HEAD
ROWS = 128
NY = 4
NZ = 4
BLOCKS = NY * NZ
SCALE = 1.0 / math.sqrt(HEAD)
EXP2_SCALE = SCALE * math.log2(math.e)
NEG = -1e30
MESH = pl.DeviceIdType.MESH
BF16 = jnp.bfloat16
F32 = jnp.float32


def place():
    ctx = lax.axis_index("ctx")
    return ctx // NZ, ctx % NZ


def at_ctx(y, z):
    return {"ctx": lax.rem(y, NY) * NZ + lax.rem(z, NZ)}


def cols(index, width):
    return pl.ds(pl.multiple_of(index * width, width), width)


def greet(peers, extra_wait=0):
    barrier = pltpu.get_barrier_semaphore()
    for peer in peers:
        pl.semaphore_signal(barrier, inc=1, device_id=peer, device_id_type=MESH)
    pl.semaphore_wait(barrier, len(peers) + extra_wait)


def remote(src, dst, send, recv, peer):
    return pltpu.make_async_remote_copy(
        src_ref=src, dst_ref=dst, send_sem=send, recv_sem=recv, device_id=peer, device_id_type=MESH
    )


def gather_kernel(
    queries, keys, values, grad_a, grad_b,
    q_a, q_b, up_a, up_b, kv_a, kv_b,
    own_wide, own_kv, wide_send, wide_recv, kv_send, kv_recv, z_send, z_recv, local_in, local_out,
):
    y, z = place()
    greet([at_ctx(y + d, z) for d in range(1, NY)] + [at_ctx(y, z + 1), at_ctx(y, z + NZ - 1)])
    kv_out = (kv_a, kv_b)
    wide_src = (queries.at[0, 0], grad_a.at[0], queries.at[1, 0], grad_b.at[0])
    wide_dst = (q_a, up_a, q_b, up_b)

    kv_copies = {}
    kv_in = []
    for m in range(2):
        for part, source in enumerate((keys, values)):
            own = pltpu.make_async_copy(
                source.at[m, 0, :, cols(y, HEAD)], own_kv.at[2 * m + part], local_in.at[2 * m + part]
            )
            own.start()
            kv_in.append(own)
            for d in range(1, NY):
                there = lax.rem(y + d, NY)
                index = (m * 2 + part) * 3 + d - 1
                copy = remote(
                    source.at[m, 0, :, cols(there, HEAD)],
                    kv_out[m].at[z, part, y],
                    kv_send.at[index],
                    kv_recv.at[index],
                    at_ctx(y + d, z),
                )
                copy.start()
                kv_copies[m, part, d] = copy
    wide_in = []
    wide_copies = []
    for w in range(4):
        own = pltpu.make_async_copy(
            wide_src[w].at[:, cols(y, WIDE)], own_wide.at[w], local_in.at[4 + w]
        )
        own.start()
        wide_in.append(own)
        for d in range(1, NY):
            there = lax.rem(y + d, NY)
            index = w * 3 + d - 1
            copy = remote(
                wide_src[w].at[:, cols(there, WIDE)],
                wide_dst[w].at[y],
                wide_send.at[index],
                wide_recv.at[index],
                at_ctx(y + d, z),
            )
            copy.start()
            wide_copies.append(copy)
    outs = []
    for m in range(2):
        for part in range(2):
            kv_in[2 * m + part].wait()
            out = pltpu.make_async_copy(
                own_kv.at[2 * m + part], kv_out[m].at[z, part, y], local_out.at[2 * m + part]
            )
            out.start()
            outs.append(out)
    for w in range(4):
        wide_in[w].wait()
        out = pltpu.make_async_copy(own_wide.at[w], wide_dst[w].at[y], local_out.at[4 + w])
        out.start()
        outs.append(out)

    up, down = at_ctx(y, z + 1), at_ctx(y, z + NZ - 1)
    before, after = lax.rem(z + NZ - 1, NZ), lax.rem(z + 1, NZ)
    first = {}
    for m in range(2):
        for part in range(2):
            outs[2 * m + part].wait()
            for d in range(1, NY):
                kv_copies[m, part, d].wait_recv()
        for to_up, part in ((1, 0), (0, 1), (1, 1), (0, 0)):
            index = (m * 2 + to_up) * 3 + part
            ref = kv_out[m].at[z, part]
            copy = remote(ref, ref, z_send.at[index], z_recv.at[index], up if to_up else down)
            copy.start()
            first[m, to_up, part] = copy
    second = []
    for m in range(2):
        for to_up, part, owner in ((1, 0, before), (0, 1, after)):
            first[m, to_up, part].wait_recv()
            index = (m * 2 + to_up) * 3 + 2
            ref = kv_out[m].at[owner, part]
            copy = remote(ref, ref, z_send.at[index], z_recv.at[index], up if to_up else down)
            copy.start()
            second.append(copy)
    for m in range(2):
        first[m, 1, 1].wait_recv()
        first[m, 0, 0].wait_recv()
    for copy in second:
        copy.wait_recv()
    for copy in wide_copies:
        copy.wait_recv()
    for out in outs[4:]:
        out.wait()
    for copy in list(kv_copies.values()) + wide_copies + list(first.values()) + second:
        copy.wait_send()


def gather(queries, keys, values, grad_a, grad_b):
    wide = jax.ShapeDtypeStruct((NY, ROWS, WIDE), BF16)
    pair = jax.ShapeDtypeStruct((NZ, 2, NY, ROWS, HEAD), BF16)
    dma = pltpu.SemaphoreType.DMA
    return pl.pallas_call(
        gather_kernel,
        out_shape=(wide, wide, wide, wide, pair, pair),
        in_specs=[pl.BlockSpec(memory_space=pl.ANY)] * 5,
        out_specs=(pl.BlockSpec(memory_space=pl.ANY),) * 6,
        scratch_shapes=[
            pltpu.VMEM((4, ROWS, WIDE), BF16),
            pltpu.VMEM((4, ROWS, HEAD), BF16),
            dma((12,)), dma((12,)), dma((12,)), dma((12,)), dma((12,)), dma((12,)),
            dma((8,)), dma((8,)),
        ],
        compiler_params=pltpu.CompilerParams(collective_id=0, has_side_effects=True),
        name="gather",
    )(queries, keys, values, grad_a, grad_b)


def scatter_kernel(passes, *refs):
    if passes:
        dq_u, dkv, dq_out, kv_out, arrived = refs[:5]
        rest = refs[5:]
    else:
        dq_u, dkv, dq_out, kv_out = refs[:4]
        rest = refs[4:]
    relay, landed, total, q_send, q_recv, z_send, z_recv, k_send, k_recv, local, p_send, p_recv = rest
    y, z = place()
    pipe = lax.axis_index("pipe")
    last = lax.axis_size("pipe") - 1
    barrier = pltpu.get_barrier_semaphore()
    peers = [at_ctx(y + d, z) for d in range(1, NY)] + [at_ctx(y, z + 1), at_ctx(y, z + NZ - 1)]
    for peer in peers:
        pl.semaphore_signal(barrier, inc=1, device_id=peer, device_id_type=MESH)
    if passes:
        @pl.when(pipe < last)
        def _():
            pl.semaphore_signal(barrier, inc=1, device_id={"pipe": pipe + 1}, device_id_type=MESH)

        pl.semaphore_wait(barrier, len(peers) + jnp.where(pipe > 0, 1, 0))
        hand = remote(dq_u, arrived, p_send, p_recv, {"pipe": lax.rem(pipe + last, last + 1)})

        @pl.when(pipe > 0)
        def _():
            hand.start()
    else:
        pl.semaphore_wait(barrier, len(peers))

    up, down = at_ctx(y, z + 1), at_ctx(y, z + NZ - 1)
    before, after = lax.rem(z + NZ - 1, NZ), lax.rem(z + 1, NZ)
    across = lax.rem(z + 2, NZ)

    def z_copy(index, src, dst, peer):
        copy = remote(src, dst, z_send.at[index], z_recv.at[index], peer)
        copy.start()
        return copy

    relay_up = z_copy(0, dkv.at[across, 0], relay.at[0], up)
    relay_down = z_copy(1, dkv.at[across, 1], relay.at[1], down)
    straight_up = z_copy(2, dkv.at[after, 1], landed.at[0], up)
    straight_down = z_copy(3, dkv.at[before, 0], landed.at[1], down)

    q_copies = []
    for d in range(1, NY):
        there = lax.rem(y + d, NY)
        copy = remote(
            dq_u.at[there], dq_out.at[:, cols(y, WIDE)], q_send.at[d - 1], q_recv.at[d - 1],
            at_ctx(y + d, z),
        )
        copy.start()
        q_copies.append(copy)
    own_q = pltpu.make_async_copy(dq_u.at[y], dq_out.at[:, cols(y, WIDE)], local.at[0])
    own_q.start()

    relay_up.wait_recv()
    total[0] = (relay[0].astype(F32) + dkv[after, 0].astype(F32)).astype(BF16)
    sum_up = z_copy(4, total.at[0], landed.at[2], up)
    relay_down.wait_recv()
    total[1] = (relay[1].astype(F32) + dkv[before, 1].astype(F32)).astype(BF16)
    sum_down = z_copy(5, total.at[1], landed.at[3], down)

    straight_down.wait_recv()
    sum_up.wait_recv()
    total[2] = (
        dkv[z, 0].astype(F32) + landed[1].astype(F32) + landed[2].astype(F32)
    ).astype(BF16)
    straight_up.wait_recv()
    sum_down.wait_recv()
    total[3] = (
        dkv[z, 1].astype(F32) + landed[0].astype(F32) + landed[3].astype(F32)
    ).astype(BF16)
    k_copies = []
    own_k = []
    for part in range(2):
        columns = cols(KEY_VALUE_HEADS * part + y, HEAD)
        for d in range(1, NY):
            there = lax.rem(y + d, NY)
            index = part * 3 + d - 1
            copy = remote(
                total.at[2 + part, there], kv_out.at[:, columns], k_send.at[index],
                k_recv.at[index], at_ctx(y + d, z),
            )
            copy.start()
            k_copies.append(copy)
        own = pltpu.make_async_copy(
            total.at[2 + part, y], kv_out.at[:, columns], local.at[1 + part]
        )
        own.start()
        own_k.append(own)
    for copy in q_copies + k_copies:
        copy.wait_recv()
    for copy in [own_q] + own_k:
        copy.wait()
    for copy in q_copies + k_copies + [
        relay_up, relay_down, straight_up, straight_down, sum_up, sum_down
    ]:
        copy.wait_send()
    if passes:
        @pl.when(pipe > 0)
        def _():
            hand.wait_send()

        @pl.when(pipe < last)
        def _():
            hand.wait_recv()


def scatter(dq_u, dkv, passes):
    dma = pltpu.SemaphoreType.DMA
    shapes = [
        jax.ShapeDtypeStruct((ROWS, NY * WIDE), BF16),
        jax.ShapeDtypeStruct((ROWS, 2 * KEY_VALUE_HEADS * HEAD), BF16),
    ]
    if passes:
        shapes.append(jax.ShapeDtypeStruct((NY, ROWS, WIDE), BF16))
    return pl.pallas_call(
        functools.partial(scatter_kernel, passes),
        out_shape=tuple(shapes),
        in_specs=[pl.BlockSpec(memory_space=pltpu.VMEM)] * 2,
        out_specs=(pl.BlockSpec(memory_space=pl.ANY),) * len(shapes),
        scratch_shapes=[
            pltpu.VMEM((2, NY, ROWS, HEAD), BF16),
            pltpu.VMEM((4, NY, ROWS, HEAD), BF16),
            pltpu.VMEM((4, NY, ROWS, HEAD), BF16),
            dma((3,)), dma((3,)), dma((6,)), dma((6,)), dma((6,)), dma((6,)), dma((3,)),
            dma, dma,
        ],
        compiler_params=pltpu.CompilerParams(
            collective_id=1 if passes else 2, has_side_effects=True
        ),
        name="scatter_a" if passes else "scatter_b",
    )(dq_u, dkv)


def nt_dot(a, b):
    return lax.dot_general(a, b, (((1,), (1,)), ((), ())), preferred_element_type=F32)


def attend_kernel(micro, *refs):
    imports, ids, q, upstream = refs[:4]
    if micro:
        arrived, refs = refs[4], refs[5:]
    else:
        refs = refs[4:]
    kv, dq, dkv, scores, grads, sums, q_rows, up_rows, slots = refs
    z = lax.rem(lax.axis_index("ctx"), NZ)
    if micro:
        has_arrived = lax.axis_index("pipe") < lax.axis_size("pipe") - 1
    sums[...] = jnp.zeros_like(sums)
    key_place = lax.broadcasted_iota(jnp.int32, (ROWS, WIDE), 0)
    row_place = lax.rem(lax.broadcasted_iota(jnp.int32, (ROWS, WIDE), 1), ROWS)

    def per_block(i, nothing):
        mine = i * NZ + z
        block = ids[micro, 0, mine]
        slots[0] = mine

        def note(j, count):
            slots[count] = j
            seen = imports[micro, 0, block, ids[micro, 0, j]]
            return count + jnp.where((seen == 1) & (j != mine), 1, 0)

        count = lax.fori_loop(0, BLOCKS, note, jnp.int32(1))
        slots[count] = 0
        for g in range(GROUP):
            span = slice(g * HEAD, (g + 1) * HEAD)
            q_rows[span, :] = q[i, :, span]
            if micro:
                came = jnp.where(has_arrived, arrived[i, :, span].astype(F32), 0.0)
                up_rows[span, :] = (upstream[i, :, span].astype(F32) + came).astype(BF16)
            else:
                up_rows[span, :] = upstream[i, :, span]
        chunks = (count + 1) // 2

        def load(part, c):
            a, b = slots[2 * c], slots[2 * c + 1]
            return jnp.concatenate(
                [kv[lax.rem(a, NZ), part, a // NZ], kv[lax.rem(b, NZ), part, b // NZ]], axis=0
            )

        def first(c, row_max):
            s = nt_dot(load(0, c), q_rows[...]) * EXP2_SCALE
            limit = jnp.where(c == 0, row_place, ROWS)
            top = jnp.where(key_place <= limit, s[:ROWS], NEG)
            bottom = s[ROWS:] + jnp.where(2 * c + 1 < count, 0.0, NEG)
            scores[c, :ROWS] = top
            scores[c, ROWS:] = bottom
            grads[c] = nt_dot(load(1, c), up_rows[...])
            return jnp.maximum(
                row_max, jnp.max(jnp.maximum(top, bottom), axis=0, keepdims=True)
            )

        row_max = lax.fori_loop(0, chunks, first, jnp.full((1, WIDE), NEG, F32))

        def second(c, carry):
            row_sum, inner = carry
            p = jnp.exp2(scores[c] - row_max)
            scores[c] = p
            return (
                row_sum + jnp.sum(p, axis=0, keepdims=True),
                inner + jnp.sum(p * grads[c], axis=0, keepdims=True),
            )

        zero = jnp.zeros((1, WIDE), F32)
        row_sum, inner = lax.fori_loop(0, chunks, second, (zero, zero))
        inverse = 1.0 / row_sum
        delta = inner * inverse

        def third(c, dq_t):
            probs = scores[c] * inverse
            score_grad = (probs * (grads[c] - delta)).astype(BF16)
            dv = jnp.dot(probs.astype(BF16), up_rows[...], preferred_element_type=F32)
            dk = jnp.dot(score_grad, q_rows[...], preferred_element_type=F32) * SCALE
            for half in range(2):
                slot = slots[2 * c + half]
                span = slice(half * ROWS, (half + 1) * ROWS)
                sums[lax.rem(slot, NZ), 0, slot // NZ] += dk[span]
                sums[lax.rem(slot, NZ), 1, slot // NZ] += dv[span]
            return dq_t + lax.dot_general(
                load(0, c), score_grad, (((0,), (0,)), ((), ())), preferred_element_type=F32
            )

        dq_t = lax.fori_loop(0, chunks, third, jnp.zeros((HEAD, WIDE), F32)) * SCALE
        for g in range(GROUP):
            span = slice(g * HEAD, (g + 1) * HEAD)
            dq[i, :, span] = dq_t[:, span].T.astype(BF16)
        return nothing

    lax.fori_loop(0, NY, per_block, 0)
    dkv[...] = sums[...].astype(BF16)


def attend(micro, imports, ids, q, upstream, arrived, kv):
    smem = pl.BlockSpec(memory_space=pltpu.SMEM)
    vmem = pl.BlockSpec(memory_space=pltpu.VMEM)
    arrays = [q, upstream] + ([arrived] if micro else []) + [kv]
    return pl.pallas_call(
        functools.partial(attend_kernel, micro),
        out_shape=(
            jax.ShapeDtypeStruct((NY, ROWS, WIDE), BF16),
            jax.ShapeDtypeStruct((NZ, 2, NY, ROWS, HEAD), BF16),
        ),
        in_specs=[smem, smem] + [vmem] * len(arrays),
        out_specs=(vmem, vmem),
        scratch_shapes=[
            pltpu.VMEM((4, 2 * ROWS, WIDE), F32),
            pltpu.VMEM((4, 2 * ROWS, WIDE), F32),
            pltpu.VMEM((NZ, 2, NY, ROWS, HEAD), F32),
            pltpu.VMEM((WIDE, HEAD), BF16),
            pltpu.VMEM((WIDE, HEAD), BF16),
            pltpu.SMEM((BLOCKS + 2,), jnp.int32),
        ],
        name="attend_b" if micro else "attend_a",
    )(imports, ids, *arrays)


def on_device(queries, keys, values, grad_a, grad_b, imports, block_ids):
    q_a, q_b, up_a, up_b, kv_a, kv_b = gather(queries, keys, values, grad_a, grad_b)
    dq_u, dkv = attend(0, imports, block_ids, q_a, up_a, None, kv_a)
    dq_a, kv_out_a, arrived = scatter(dq_u, dkv, True)
    dq_u, dkv = attend(1, imports, block_ids, q_b, up_b, arrived, kv_b)
    dq_b, kv_out_b = scatter(dq_u, dkv, False)
    return (dq_a[None], dq_b[None], jnp.stack([kv_out_a, kv_out_b])[:, None])


def solution(mesh):
    return jax.shard_map(
        on_device,
        mesh=mesh,
        in_specs=(
            P(None, "pipe", "ctx", None),
            P(None, "pipe", "ctx", None),
            P(None, "pipe", "ctx", None),
            P("pipe", "ctx", None),
            P("pipe", "ctx", None),
            P(None, "pipe", None, None),
            P(None, "pipe", None),
        ),
        out_specs=(P("pipe", "ctx", None), P("pipe", "ctx", None), P(None, "pipe", "ctx", None)),
        check_vma=False,
    )
```

```python
import math

import jax
import jax.numpy as jnp
from jax import lax
from jax.experimental import pallas as pl
from jax.experimental.pallas import tpu as pltpu
from jax.sharding import PartitionSpec as P

KEY_VALUE_HEADS = 4
HEAD = 128
GROUP = 5
WIDE = GROUP * HEAD
ROWS = 128
NY = 4
NZ = 4
BLOCKS = NY * NZ
LISTED = 8
CHUNKS = LISTED // 2
FORWARD_AT = 2
RELAY_AT = 1
SCALE = 1.0 / math.sqrt(HEAD)
EXP2_SCALE = SCALE * math.log2(math.e)
NEG = -1e30
MESH = pl.DeviceIdType.MESH
BF16 = jnp.bfloat16
F32 = jnp.float32


def place():
    ctx = lax.axis_index("ctx")
    return ctx // NZ, ctx % NZ


def at_ctx(y, z):
    return {"ctx": lax.rem(y, NY) * NZ + lax.rem(z, NZ)}


def cols(index, width):
    return pl.ds(pl.multiple_of(index * width, width), width)


def remote(src, dst, send, recv, peer):
    return pltpu.make_async_remote_copy(
        src_ref=src, dst_ref=dst, send_sem=send, recv_sem=recv, device_id=peer, device_id_type=MESH
    )


def nt_dot(a, b):
    return lax.dot_general(a, b, (((1,), (1,)), ((), ())), preferred_element_type=F32)


def list_blocks(micro, z, imports, ids, slots, where_part, counts):
    for i in range(NY):
        mine = i * NZ + z
        block = ids[micro, 0, mine]

        def note(j, carry):
            count, found = carry[0], carry[1:]
            seen = imports[micro, 0, block, ids[micro, 0, j]]
            live = (seen == 1) & (j != mine)
            found = tuple(
                jnp.where(live & (count == p + 1), j, slot) for p, slot in enumerate(found)
            )
            position = jnp.where(live, i * LISTED + count, NY * LISTED)
            where_part[(micro * NY + i) * BLOCKS + j] = jnp.where(
                j == mine, i * LISTED, position
            )
            return (count + jnp.where(live, 1, 0),) + found

        start = (jnp.int32(1),) + (jnp.int32(0),) * (LISTED - 1)
        carry = lax.fori_loop(0, BLOCKS, note, start)
        base = (micro * NY + i) * LISTED
        counts[micro * NY + i] = carry[0]
        slots[base] = mine
        for p in range(LISTED - 1):
            slots[base + p + 1] = carry[p + 1]


def attend_block(micro, i, key_place, row_place, slots, counts, kv, q_rows, up_rows, scores,
                 grads, parts, dq_u):
    base = (micro * NY + i) * LISTED
    count = counts[micro * NY + i]

    def load(part, c):
        a, b = slots[base + 2 * c], slots[base + 2 * c + 1]
        return jnp.concatenate(
            [kv[lax.rem(a, NZ), part, a // NZ], kv[lax.rem(b, NZ), part, b // NZ]], axis=0
        )

    row_max = jnp.full((1, WIDE), NEG, F32)
    for c in range(CHUNKS):
        s = nt_dot(load(0, c), q_rows[...]) * EXP2_SCALE
        if c == 0:
            top = jnp.where(key_place <= row_place, s[:ROWS], NEG)
        else:
            top = s[:ROWS] + jnp.where(2 * c < count, 0.0, NEG)
        bottom = s[ROWS:] + jnp.where(2 * c + 1 < count, 0.0, NEG)
        scores[c, :ROWS] = top
        scores[c, ROWS:] = bottom
        grads[c] = nt_dot(load(1, c), up_rows[...])
        row_max = jnp.maximum(row_max, jnp.max(jnp.maximum(top, bottom), axis=0, keepdims=True))
    row_sum = jnp.zeros((1, WIDE), F32)
    inner = jnp.zeros((1, WIDE), F32)
    for c in range(CHUNKS):
        p = jnp.exp2(scores[c] - row_max)
        scores[c] = p
        row_sum = row_sum + jnp.sum(p, axis=0, keepdims=True)
        inner = inner + jnp.sum(p * grads[c], axis=0, keepdims=True)
    inverse = 1.0 / row_sum
    delta = inner * inverse
    dq_t = jnp.zeros((HEAD, WIDE), F32)
    for c in range(CHUNKS):
        probs = scores[c] * inverse
        score_grad = (probs * (grads[c] - delta)).astype(BF16)
        dv = jnp.dot(probs.astype(BF16), up_rows[...], preferred_element_type=F32)
        dk = jnp.dot(score_grad, q_rows[...], preferred_element_type=F32) * SCALE
        for half in range(2):
            span = slice(half * ROWS, (half + 1) * ROWS)
            parts[i * LISTED + 2 * c + half, 0] = dk[span]
            parts[i * LISTED + 2 * c + half, 1] = dv[span]
        dq_t = dq_t + lax.dot_general(
            load(0, c), score_grad, (((0,), (0,)), ((), ())), preferred_element_type=F32
        )
    dq_t = dq_t * SCALE
    for g in range(GROUP):
        span = slice(g * HEAD, (g + 1) * HEAD)
        dq_u[i, :, span] = dq_t[:, span].T.astype(BF16)


def step_kernel(
    queries, keys, values, grad_a, grad_b, imports, ids,
    dq_out_a, dq_out_b, kv_out,
    q_a, q_b, up_a, up_b, kv_a, kv_b, arrived, dq_u_a, dq_u_b, dkv_a, dkv_b,
    relay_a, relay_b, landed_a, landed_b, total_a, total_b,
    scores, grads, parts, q_rows, up_rows,
    slots, where_part, counts,
    wide_send, wide_recv, kv_send, kv_recv, z_send, z_recv, local_in,
    hand_send, hand_recv, dq_send, dq_recv, r_send, r_recv, o_send, o_recv, local_out,
):
    y, z = place()
    pipe = lax.axis_index("pipe")
    last = lax.axis_size("pipe") - 1
    up, down = at_ctx(y, z + 1), at_ctx(y, z + NZ - 1)
    before, after = lax.rem(z + NZ - 1, NZ), lax.rem(z + 1, NZ)
    across = lax.rem(z + 2, NZ)
    barrier = pltpu.get_barrier_semaphore()
    peers = [at_ctx(y + d, z) for d in range(1, NY)] + [up, down]
    for peer in peers:
        pl.semaphore_signal(barrier, inc=1, device_id=peer, device_id_type=MESH)

    @pl.when(pipe < last)
    def _():
        pl.semaphore_signal(barrier, inc=1, device_id={"pipe": pipe + 1}, device_id_type=MESH)

    pl.semaphore_wait(barrier, len(peers) + jnp.where(pipe > 0, 1, 0))

    kvs = (kv_a, kv_b)
    wide_src = (queries.at[0, 0], grad_a.at[0], queries.at[1, 0], grad_b.at[0])
    wide_dst = (q_a, up_a, q_b, up_b)
    kv_copies, kv_own, wide_copies, wide_own = {}, {}, {}, {}
    for m in range(2):
        for part, source in enumerate((keys, values)):
            for d in range(1, NY):
                there = lax.rem(y + d, NY)
                index = (m * 2 + part) * 3 + d - 1
                kv_copies[m, part, d] = remote(
                    source.at[m, 0, :, cols(there, HEAD)], kvs[m].at[z, part, y],
                    kv_send.at[index], kv_recv.at[index], at_ctx(y + d, z),
                )
                kv_copies[m, part, d].start()
            kv_own[m, part] = pltpu.make_async_copy(
                source.at[m, 0, :, cols(y, HEAD)], kvs[m].at[z, part, y],
                local_in.at[2 * m + part],
            )
            kv_own[m, part].start()
        for w in (2 * m, 2 * m + 1):
            for d in range(1, NY):
                there = lax.rem(y + d, NY)
                index = w * 3 + d - 1
                wide_copies[w, d] = remote(
                    wide_src[w].at[:, cols(there, WIDE)], wide_dst[w].at[y],
                    wide_send.at[index], wide_recv.at[index], at_ctx(y + d, z),
                )
                wide_copies[w, d].start()
            wide_own[w] = pltpu.make_async_copy(
                wide_src[w].at[:, cols(y, WIDE)], wide_dst[w].at[y], local_in.at[4 + w]
            )
            wide_own[w].start()

    def spread(m):
        for part in range(2):
            kv_own[m, part].wait()
            for d in range(1, NY):
                kv_copies[m, part, d].wait_recv()
        for to_up, part in ((1, 0), (0, 1), (1, 1), (0, 0)):
            z_copy(m, to_up, part, part, z).start()

    def z_copy(m, to_up, index, part, owner):
        ref = kvs[m].at[owner, part]
        where = (m * 2 + to_up) * 3 + index
        return remote(ref, ref, z_send.at[where], z_recv.at[where], up if to_up else down)

    def forward(m):
        for to_up, part, owner in ((1, 0, before), (0, 1, after)):
            z_copy(m, to_up, part, part, z).wait_recv()
            z_copy(m, to_up, 2, part, owner).start()

    def wait_spread(m):
        z_copy(m, 1, 1, 1, z).wait_recv()
        z_copy(m, 0, 0, 0, z).wait_recv()
        z_copy(m, 1, 2, 0, across).wait_recv()
        z_copy(m, 0, 2, 1, across).wait_recv()
        for w in (2 * m, 2 * m + 1):
            wide_own[w].wait()
            for d in range(1, NY):
                wide_copies[w, d].wait_recv()

    def hand(i):
        return remote(
            dq_u_a.at[i], arrived.at[i], hand_send.at[i], hand_recv.at[i],
            {"pipe": lax.rem(pipe + last, last + 1)},
        )

    def dq_copy(m, sender, target):
        return remote(
            (dq_u_a, dq_u_b)[m].at[target],
            (dq_out_a, dq_out_b)[m].at[0, :, cols(sender, WIDE)],
            dq_send.at[m * NY + target], dq_recv.at[m * NY + sender], at_ctx(target, z),
        )

    def dq_own(m):
        return pltpu.make_async_copy(
            (dq_u_a, dq_u_b)[m].at[y], (dq_out_a, dq_out_b)[m].at[0, :, cols(y, WIDE)],
            local_out.at[m],
        )

    def return_dq(m, i):
        @pl.when(i == y)
        def _():
            dq_own(m).start()

        @pl.when(i != y)
        def _():
            dq_copy(m, y, i).start()

    def combine(m, dkv):
        def one(slot, nothing):
            places = [where_part[(m * NY + i) * BLOCKS + slot] for i in range(NY)]
            for part in range(2):
                value = parts[places[0], part]
                for at in places[1:]:
                    value = value + parts[at, part]
                dkv[lax.rem(slot, NZ), part, slot // NZ] = value.astype(BF16)
            return nothing

        lax.fori_loop(0, BLOCKS, one, 0)

    relays, landeds, totals, dkvs = (
        (relay_a, relay_b), (landed_a, landed_b), (total_a, total_b), (dkv_a, dkv_b),
    )

    def r_copy(m, index):
        relay, landed, total, dkv = relays[m], landeds[m], totals[m], dkvs[m]
        src, dst, peer = (
            (dkv.at[across, 0], relay.at[0], up),
            (dkv.at[across, 1], relay.at[1], down),
            (dkv.at[after, 1], landed.at[0], up),
            (dkv.at[before, 0], landed.at[1], down),
            (total.at[0], landed.at[2], up),
            (total.at[1], landed.at[3], down),
        )[index]
        return remote(src, dst, r_send.at[m * 6 + index], r_recv.at[m * 6 + index], peer)

    def reduce_start(m):
        for index in range(4):
            r_copy(m, index).start()

    def reduce_relay(m):
        relay, total, dkv = relays[m], totals[m], dkvs[m]
        r_copy(m, 0).wait_recv()
        total[0] = (relay[0].astype(F32) + dkv[after, 0].astype(F32)).astype(BF16)
        r_copy(m, 4).start()
        r_copy(m, 1).wait_recv()
        total[1] = (relay[1].astype(F32) + dkv[before, 1].astype(F32)).astype(BF16)
        r_copy(m, 5).start()

    def o_copy(m, part, sender, target):
        return remote(
            totals[m].at[2 + part, target],
            kv_out.at[m, 0, :, cols(KEY_VALUE_HEADS * part + sender, HEAD)],
            o_send.at[(m * 2 + part) * NY + target], o_recv.at[(m * 2 + part) * NY + sender],
            at_ctx(target, z),
        )

    def o_own(m, part):
        return pltpu.make_async_copy(
            totals[m].at[2 + part, y],
            kv_out.at[m, 0, :, cols(KEY_VALUE_HEADS * part + y, HEAD)],
            local_out.at[2 + 2 * m + part],
        )

    def reduce_end(m):
        landed, total, dkv = landeds[m], totals[m], dkvs[m]
        for part, straight, summed in ((0, 3, 4), (1, 2, 5)):
            r_copy(m, straight).wait_recv()
            r_copy(m, summed).wait_recv()
            total[2 + part] = (
                dkv[z, part].astype(F32)
                + landed[1 - part].astype(F32)
                + landed[2 + part].astype(F32)
            ).astype(BF16)
            for d in range(1, NY):
                o_copy(m, part, y, lax.rem(y + d, NY)).start()
            o_own(m, part).start()

    key_place = lax.broadcasted_iota(jnp.int32, (ROWS, WIDE), 0)
    row_place = lax.rem(lax.broadcasted_iota(jnp.int32, (ROWS, WIDE), 1), ROWS)
    parts[NY * LISTED] = jnp.zeros_like(parts[NY * LISTED])
    for m in range(2):
        list_blocks(m, z, imports, ids, slots, where_part, counts)

    spread(0)
    forward(0)
    spread(1)
    wait_spread(0)

    def turn_a(i, nothing):
        for g in range(GROUP):
            span = slice(g * HEAD, (g + 1) * HEAD)
            q_rows[span, :] = q_a[i, :, span]
            up_rows[span, :] = up_a[i, :, span]
        attend_block(0, i, key_place, row_place, slots, counts, kv_a, q_rows, up_rows, scores,
                     grads, parts, dq_u_a)

        @pl.when(pipe > 0)
        def _():
            hand(i).start()

        return_dq(0, i)

        @pl.when(i == FORWARD_AT)
        def _():
            forward(1)

        return nothing

    lax.fori_loop(0, NY, turn_a, 0)
    combine(0, dkv_a)
    reduce_start(0)
    wait_spread(1)

    def turn_b(i, nothing):
        @pl.when(pipe < last)
        def _():
            hand(i).wait_recv()

        for g in range(GROUP):
            span = slice(g * HEAD, (g + 1) * HEAD)
            q_rows[span, :] = q_b[i, :, span]
            came = jnp.where(pipe < last, arrived[i, :, span].astype(F32), 0.0)
            up_rows[span, :] = (up_b[i, :, span].astype(F32) + came).astype(BF16)
        attend_block(1, i, key_place, row_place, slots, counts, kv_b, q_rows, up_rows, scores,
                     grads, parts, dq_u_b)
        return_dq(1, i)

        @pl.when(i == RELAY_AT)
        def _():
            reduce_relay(0)

        return nothing

    lax.fori_loop(0, NY, turn_b, 0)
    combine(1, dkv_b)
    reduce_start(1)
    reduce_end(0)
    reduce_relay(1)
    reduce_end(1)

    for m in range(2):
        dq_own(m).wait()
        for d in range(1, NY):
            other = lax.rem(y + d, NY)
            dq_copy(m, other, y).wait_recv()
            dq_copy(m, y, other).wait_send()
            for part in range(2):
                o_copy(m, part, other, y).wait_recv()
                o_copy(m, part, y, other).wait_send()
        for part in range(2):
            o_own(m, part).wait()
        for index in range(6):
            r_copy(m, index).wait_send()
        for to_up, part, owner in ((1, 0, before), (0, 1, after)):
            z_copy(m, to_up, 0, 0, z).wait_send()
            z_copy(m, to_up, 1, 1, z).wait_send()
            z_copy(m, to_up, 2, part, owner).wait_send()
    for copy in list(kv_copies.values()) + list(wide_copies.values()):
        copy.wait_send()

    @pl.when(pipe > 0)
    def _():
        for i in range(NY):
            hand(i).wait_send()


def on_device(queries, keys, values, grad_a, grad_b, imports, block_ids):
    wide = pltpu.VMEM((NY, ROWS, WIDE), BF16)
    pair = pltpu.VMEM((NZ, 2, NY, ROWS, HEAD), BF16)
    column = lambda n: pltpu.VMEM((n, NY, ROWS, HEAD), BF16)
    dma = lambda n: pltpu.SemaphoreType.DMA((n,))
    chunk = pltpu.VMEM((CHUNKS, 2 * ROWS, WIDE), F32)
    rows = pltpu.VMEM((WIDE, HEAD), BF16)
    whole = pl.BlockSpec(memory_space=pl.ANY)
    smem = pl.BlockSpec(memory_space=pltpu.SMEM)
    return pl.pallas_call(
        step_kernel,
        out_shape=(
            jax.ShapeDtypeStruct(grad_a.shape, BF16),
            jax.ShapeDtypeStruct(grad_b.shape, BF16),
            jax.ShapeDtypeStruct((2, 1, ROWS, 2 * KEY_VALUE_HEADS * HEAD), BF16),
        ),
        in_specs=[whole] * 5 + [smem, smem],
        out_specs=(whole,) * 3,
        scratch_shapes=[
            wide, wide, wide, wide, pair, pair, wide, wide, wide, pair, pair,
            column(2), column(2), column(4), column(4), column(4), column(4),
            chunk, chunk, pltpu.VMEM((NY * LISTED + 1, 2, ROWS, HEAD), F32), rows, rows,
            pltpu.SMEM((2 * NY * LISTED,), jnp.int32),
            pltpu.SMEM((2 * NY * BLOCKS,), jnp.int32),
            pltpu.SMEM((2 * NY,), jnp.int32),
            dma(12), dma(12), dma(12), dma(12), dma(12), dma(12), dma(8),
            dma(4), dma(4), dma(8), dma(8), dma(12), dma(12), dma(16), dma(16), dma(6),
        ],
        compiler_params=pltpu.CompilerParams(
            collective_id=0, has_side_effects=True, vmem_limit_bytes=60 * 1024 * 1024
        ),
        name="step",
    )(queries, keys, values, grad_a, grad_b, imports, block_ids)


def solution(mesh):
    return jax.shard_map(
        on_device,
        mesh=mesh,
        in_specs=(
            P(None, "pipe", "ctx", None),
            P(None, "pipe", "ctx", None),
            P(None, "pipe", "ctx", None),
            P("pipe", "ctx", None),
            P("pipe", "ctx", None),
            P(None, "pipe", None, None),
            P(None, "pipe", None),
        ),
        out_specs=(P("pipe", "ctx", None), P("pipe", "ctx", None), P(None, "pipe", "ctx", None)),
        check_vma=False,
    )
```

```python
import math

import jax
import jax.numpy as jnp
from jax import lax
from jax.experimental import pallas as pl
from jax.experimental.pallas import tpu as pltpu
from jax.sharding import PartitionSpec as P

KEY_VALUE_HEADS = 4
HEAD = 128
GROUP = 5
WIDE = GROUP * HEAD
ROWS = 128
HALF = ROWS // 2
NY = 4
NZ = 4
BLOCKS = NY * NZ
LISTED = 8
CHUNKS = LISTED // 2
FORWARD_AT = 2
RELAY_AT = 1
SCALE = 1.0 / math.sqrt(HEAD)
EXP2_SCALE = SCALE * math.log2(math.e)
NEG = -1e30
MESH = pl.DeviceIdType.MESH
BF16 = jnp.bfloat16
F32 = jnp.float32


def place():
    ctx = lax.axis_index("ctx")
    return ctx // NZ, ctx % NZ


def at_ctx(y, z):
    return {"ctx": lax.rem(y, NY) * NZ + lax.rem(z, NZ)}


def cols(index, width):
    return pl.ds(pl.multiple_of(index * width, width), width)


def remote(src, dst, send, recv, peer):
    return pltpu.make_async_remote_copy(
        src_ref=src, dst_ref=dst, send_sem=send, recv_sem=recv, device_id=peer, device_id_type=MESH
    )


def nt_dot(a, b):
    return lax.dot_general(a, b, (((1,), (1,)), ((), ())), preferred_element_type=F32)


def list_blocks(micro, z, imports, ids, slots, where_part, counts):
    for i in range(NY):
        mine = i * NZ + z
        block = ids[micro, 0, mine]

        def note(j, carry):
            count, found = carry[0], carry[1:]
            seen = imports[micro, 0, block, ids[micro, 0, j]]
            live = (seen == 1) & (j != mine)
            found = tuple(
                jnp.where(live & (count == p + 1), j, slot) for p, slot in enumerate(found)
            )
            position = jnp.where(live, i * LISTED + count, NY * LISTED)
            where_part[(micro * NY + i) * BLOCKS + j] = jnp.where(
                j == mine, i * LISTED, position
            )
            return (count + jnp.where(live, 1, 0),) + found

        start = (jnp.int32(1),) + (jnp.int32(0),) * (LISTED - 1)
        carry = lax.fori_loop(0, BLOCKS, note, start)
        base = (micro * NY + i) * LISTED
        counts[micro * NY + i] = carry[0]
        slots[base] = mine
        for p in range(LISTED - 1):
            slots[base + p + 1] = carry[p + 1]


def attend_block(micro, i, key_place, row_place, slots, counts, kv, q_rows, up_rows, scores,
                 grads, parts, dq_u):
    base = (micro * NY + i) * LISTED
    count = counts[micro * NY + i]

    def load(part, c):
        a, b = slots[base + 2 * c], slots[base + 2 * c + 1]
        return jnp.concatenate(
            [kv[lax.rem(a, NZ), part, a // NZ], kv[lax.rem(b, NZ), part, b // NZ]], axis=0
        )

    row_max = jnp.full((1, WIDE), NEG, F32)
    for c in range(CHUNKS):
        s = nt_dot(load(0, c), q_rows[...]) * EXP2_SCALE
        if c == 0:
            top = jnp.where(key_place <= row_place, s[:ROWS], NEG)
        else:
            top = s[:ROWS] + jnp.where(2 * c < count, 0.0, NEG)
        bottom = s[ROWS:] + jnp.where(2 * c + 1 < count, 0.0, NEG)
        scores[c, :ROWS] = top
        scores[c, ROWS:] = bottom
        grads[c] = nt_dot(load(1, c), up_rows[...])
        row_max = jnp.maximum(row_max, jnp.max(jnp.maximum(top, bottom), axis=0, keepdims=True))
    row_sum = jnp.zeros((1, WIDE), F32)
    inner = jnp.zeros((1, WIDE), F32)
    for c in range(CHUNKS):
        p = jnp.exp2(scores[c] - row_max)
        scores[c] = p
        row_sum = row_sum + jnp.sum(p, axis=0, keepdims=True)
        inner = inner + jnp.sum(p * grads[c], axis=0, keepdims=True)
    inverse = 1.0 / row_sum
    delta = inner * inverse
    dq_t = jnp.zeros((HEAD, WIDE), F32)
    for c in range(CHUNKS):
        probs = scores[c] * inverse
        score_grad = (probs * (grads[c] - delta)).astype(BF16)
        dv = jnp.dot(probs.astype(BF16), up_rows[...], preferred_element_type=F32)
        dk = jnp.dot(score_grad, q_rows[...], preferred_element_type=F32) * SCALE
        for half in range(2):
            span = slice(half * ROWS, (half + 1) * ROWS)
            parts[i * LISTED + 2 * c + half, 0] = dk[span]
            parts[i * LISTED + 2 * c + half, 1] = dv[span]
        dq_t = dq_t + lax.dot_general(
            load(0, c), score_grad, (((0,), (0,)), ((), ())), preferred_element_type=F32
        )
    dq_t = dq_t * SCALE
    for g in range(GROUP):
        span = slice(g * HEAD, (g + 1) * HEAD)
        dq_u[i, :, span] = dq_t[:, span].T.astype(BF16)


def step_kernel(
    queries, keys, values, grad_a, grad_b, imports, ids,
    dq_out_a, dq_out_b, kv_out,
    q_a, q_b, up_a, up_b, kv_a, kv_b, arrived, passing, dq_u_a, dq_u_b, dkv_a, dkv_b,
    relay_a, relay_b, landed_a, landed_b, total_a, total_b,
    scores, grads, parts, q_rows, up_rows,
    slots, where_part, counts,
    wide_send, wide_recv, kv_send, kv_recv, z_send, z_recv, local_in,
    hand_send, hand_recv, pass_recv, dq_send, dq_recv, r_send, r_recv, o_send, o_recv, local_out,
):
    y, z = place()
    pipe = lax.axis_index("pipe")
    last = lax.axis_size("pipe") - 1
    edge = (last + 1) // 2
    spread_hand = edge == 2 * NY
    up, down = at_ctx(y, z + 1), at_ctx(y, z + NZ - 1)
    before, after = lax.rem(z + NZ - 1, NZ), lax.rem(z + 1, NZ)
    across = lax.rem(z + 2, NZ)
    barrier = pltpu.get_barrier_semaphore()
    peers = [at_ctx(y + d, z) for d in range(1, NY)] + [up, down]
    for peer in peers:
        pl.semaphore_signal(barrier, inc=1, device_id=peer, device_id_type=MESH)

    @pl.when(pipe < last)
    def _():
        pl.semaphore_signal(barrier, inc=1, device_id={"pipe": pipe + 1}, device_id_type=MESH)

    callers = len(peers) + jnp.where(pipe > 0, 1, 0)
    if spread_hand:
        @pl.when(pipe == edge - 1)
        def _():
            for r in range(1, edge):
                pl.semaphore_signal(
                    barrier, inc=1, device_id={"pipe": edge + r}, device_id_type=MESH
                )

        @pl.when(pipe > edge)
        def _():
            pl.semaphore_signal(barrier, inc=1, device_id={"pipe": edge}, device_id_type=MESH)

        callers = callers + jnp.where(pipe > edge, 1, 0) + jnp.where(pipe == edge, edge - 1, 0)
    pl.semaphore_wait(barrier, callers)

    kvs = (kv_a, kv_b)
    wide_src = (queries.at[0, 0], grad_a.at[0], queries.at[1, 0], grad_b.at[0])
    wide_dst = (q_a, up_a, q_b, up_b)
    kv_copies, kv_own, wide_copies, wide_own = {}, {}, {}, {}
    for m in range(2):
        for part, source in enumerate((keys, values)):
            for d in range(1, NY):
                there = lax.rem(y + d, NY)
                index = (m * 2 + part) * 3 + d - 1
                kv_copies[m, part, d] = remote(
                    source.at[m, 0, :, cols(there, HEAD)], kvs[m].at[z, part, y],
                    kv_send.at[index], kv_recv.at[index], at_ctx(y + d, z),
                )
                kv_copies[m, part, d].start()
            kv_own[m, part] = pltpu.make_async_copy(
                source.at[m, 0, :, cols(y, HEAD)], kvs[m].at[z, part, y],
                local_in.at[2 * m + part],
            )
            kv_own[m, part].start()
        for w in (2 * m, 2 * m + 1):
            for d in range(1, NY):
                there = lax.rem(y + d, NY)
                index = w * 3 + d - 1
                wide_copies[w, d] = remote(
                    wide_src[w].at[:, cols(there, WIDE)], wide_dst[w].at[y],
                    wide_send.at[index], wide_recv.at[index], at_ctx(y + d, z),
                )
                wide_copies[w, d].start()
            wide_own[w] = pltpu.make_async_copy(
                wide_src[w].at[:, cols(y, WIDE)], wide_dst[w].at[y], local_in.at[4 + w]
            )
            wide_own[w].start()

    def spread(m):
        for part in range(2):
            kv_own[m, part].wait()
            for d in range(1, NY):
                kv_copies[m, part, d].wait_recv()
        for to_up, part in ((1, 0), (0, 1), (1, 1), (0, 0)):
            z_copy(m, to_up, part, part, z).start()

    def z_copy(m, to_up, index, part, owner):
        ref = kvs[m].at[owner, part]
        where = (m * 2 + to_up) * 3 + index
        return remote(ref, ref, z_send.at[where], z_recv.at[where], up if to_up else down)

    def forward(m):
        for to_up, part, owner in ((1, 0, before), (0, 1, after)):
            z_copy(m, to_up, part, part, z).wait_recv()
            z_copy(m, to_up, 2, part, owner).start()

    def wait_spread(m):
        z_copy(m, 1, 1, 1, z).wait_recv()
        z_copy(m, 0, 0, 0, z).wait_recv()
        z_copy(m, 1, 2, 0, across).wait_recv()
        z_copy(m, 0, 2, 1, across).wait_recv()
        for w in (2 * m, 2 * m + 1):
            wide_own[w].wait()
            for d in range(1, NY):
                wide_copies[w, d].wait_recv()

    def hand(i, h):
        span = pl.ds(h * HALF, HALF)
        return remote(
            dq_u_a.at[i, span], arrived.at[i, span], hand_send.at[2 * i + h],
            hand_recv.at[2 * i + h], {"pipe": lax.rem(pipe + last, last + 1)},
        )

    def to_relay(i, h):
        return remote(
            dq_u_a.at[i, pl.ds(h * HALF, HALF)], passing, hand_send.at[2 * i + h],
            pass_recv.at[0], {"pipe": lax.rem(edge + lax.rem(2 + 2 * i + h, edge), last + 1)},
        )

    piece = lax.rem(pipe + 2 * edge - 2, 2 * NY)

    def from_relay():
        i, h = piece // 2, lax.rem(piece, 2)
        return remote(
            passing, arrived.at[i, pl.ds(pl.multiple_of(h * HALF, HALF), HALF)],
            hand_send.at[2 * NY], hand_recv.at[piece], {"pipe": edge - 1},
        )

    def hand_over(i):
        direct = (pipe > 0) & (pipe != edge) if spread_hand else pipe > 0

        @pl.when(direct)
        def _():
            hand(i, 0).start()
            hand(i, 1).start()

        if spread_hand:
            @pl.when(pipe == edge)
            def _():
                @pl.when(i < NY - 1)
                def _():
                    to_relay(i, 0).start()

                @pl.when(i == NY - 1)
                def _():
                    hand(i, 0).start()

                to_relay(i, 1).start()

    def pass_on(i):
        if spread_hand:
            @pl.when((pipe > edge) & (piece // 2 + 1 == i))
            def _():
                to_relay(0, 0).wait_recv()
                from_relay().start()

    def hand_end():
        direct = (pipe > 0) & (pipe <= edge) if spread_hand else pipe > 0

        @pl.when(direct)
        def _():
            for i in range(NY):
                hand(i, 0).wait_send()
                hand(i, 1).wait_send()

        if spread_hand:
            @pl.when(pipe > edge)
            def _():
                for i in range(NY):
                    hand(i, 0).wait_send()
                    hand(i, 1).wait_send()
                from_relay().wait_send()

    def dq_copy(m, sender, target):
        return remote(
            (dq_u_a, dq_u_b)[m].at[target],
            (dq_out_a, dq_out_b)[m].at[0, :, cols(sender, WIDE)],
            dq_send.at[m * NY + target], dq_recv.at[m * NY + sender], at_ctx(target, z),
        )

    def dq_own(m):
        return pltpu.make_async_copy(
            (dq_u_a, dq_u_b)[m].at[y], (dq_out_a, dq_out_b)[m].at[0, :, cols(y, WIDE)],
            local_out.at[m],
        )

    def return_dq(m, i):
        @pl.when(i == y)
        def _():
            dq_own(m).start()

        @pl.when(i != y)
        def _():
            dq_copy(m, y, i).start()

    def combine(m, dkv):
        def one(slot, nothing):
            places = [where_part[(m * NY + i) * BLOCKS + slot] for i in range(NY)]
            for part in range(2):
                value = parts[places[0], part]
                for at in places[1:]:
                    value = value + parts[at, part]
                dkv[lax.rem(slot, NZ), part, slot // NZ] = value.astype(BF16)
            return nothing

        lax.fori_loop(0, BLOCKS, one, 0)

    relays, landeds, totals, dkvs = (
        (relay_a, relay_b), (landed_a, landed_b), (total_a, total_b), (dkv_a, dkv_b),
    )

    def r_copy(m, index):
        relay, landed, total, dkv = relays[m], landeds[m], totals[m], dkvs[m]
        src, dst, peer = (
            (dkv.at[across, 0], relay.at[0], up),
            (dkv.at[across, 1], relay.at[1], down),
            (dkv.at[after, 1], landed.at[0], up),
            (dkv.at[before, 0], landed.at[1], down),
            (total.at[0], landed.at[2], up),
            (total.at[1], landed.at[3], down),
        )[index]
        return remote(src, dst, r_send.at[m * 6 + index], r_recv.at[m * 6 + index], peer)

    def reduce_start(m):
        for index in range(4):
            r_copy(m, index).start()

    def reduce_relay(m):
        relay, total, dkv = relays[m], totals[m], dkvs[m]
        r_copy(m, 0).wait_recv()
        total[0] = (relay[0].astype(F32) + dkv[after, 0].astype(F32)).astype(BF16)
        r_copy(m, 4).start()
        r_copy(m, 1).wait_recv()
        total[1] = (relay[1].astype(F32) + dkv[before, 1].astype(F32)).astype(BF16)
        r_copy(m, 5).start()

    def o_copy(m, part, sender, target):
        return remote(
            totals[m].at[2 + part, target],
            kv_out.at[m, 0, :, cols(KEY_VALUE_HEADS * part + sender, HEAD)],
            o_send.at[(m * 2 + part) * NY + target], o_recv.at[(m * 2 + part) * NY + sender],
            at_ctx(target, z),
        )

    def o_own(m, part):
        return pltpu.make_async_copy(
            totals[m].at[2 + part, y],
            kv_out.at[m, 0, :, cols(KEY_VALUE_HEADS * part + y, HEAD)],
            local_out.at[2 + 2 * m + part],
        )

    def reduce_end(m):
        landed, total, dkv = landeds[m], totals[m], dkvs[m]
        for part, straight, summed in ((0, 3, 4), (1, 2, 5)):
            r_copy(m, straight).wait_recv()
            r_copy(m, summed).wait_recv()
            total[2 + part] = (
                dkv[z, part].astype(F32)
                + landed[1 - part].astype(F32)
                + landed[2 + part].astype(F32)
            ).astype(BF16)
            for d in range(1, NY):
                o_copy(m, part, y, lax.rem(y + d, NY)).start()
            o_own(m, part).start()

    key_place = lax.broadcasted_iota(jnp.int32, (ROWS, WIDE), 0)
    row_place = lax.rem(lax.broadcasted_iota(jnp.int32, (ROWS, WIDE), 1), ROWS)
    parts[NY * LISTED] = jnp.zeros_like(parts[NY * LISTED])
    for m in range(2):
        list_blocks(m, z, imports, ids, slots, where_part, counts)

    spread(0)
    forward(0)
    spread(1)
    wait_spread(0)

    def turn_a(i, nothing):
        for g in range(GROUP):
            span = slice(g * HEAD, (g + 1) * HEAD)
            q_rows[span, :] = q_a[i, :, span]
            up_rows[span, :] = up_a[i, :, span]
        attend_block(0, i, key_place, row_place, slots, counts, kv_a, q_rows, up_rows, scores,
                     grads, parts, dq_u_a)

        hand_over(i)
        return_dq(0, i)
        pass_on(i)

        @pl.when(i == FORWARD_AT)
        def _():
            forward(1)

        return nothing

    lax.fori_loop(0, NY, turn_a, 0)
    combine(0, dkv_a)
    pass_on(NY)
    reduce_start(0)
    wait_spread(1)

    def turn_b(i, nothing):
        @pl.when(pipe < last)
        def _():
            hand(i, 0).wait_recv()
            hand(i, 1).wait_recv()

        for g in range(GROUP):
            span = slice(g * HEAD, (g + 1) * HEAD)
            q_rows[span, :] = q_b[i, :, span]
            came = jnp.where(pipe < last, arrived[i, :, span].astype(F32), 0.0)
            up_rows[span, :] = (up_b[i, :, span].astype(F32) + came).astype(BF16)
        attend_block(1, i, key_place, row_place, slots, counts, kv_b, q_rows, up_rows, scores,
                     grads, parts, dq_u_b)
        return_dq(1, i)

        @pl.when(i == RELAY_AT)
        def _():
            reduce_relay(0)

        return nothing

    lax.fori_loop(0, NY, turn_b, 0)
    combine(1, dkv_b)
    reduce_start(1)
    reduce_end(0)
    reduce_relay(1)
    reduce_end(1)

    for m in range(2):
        dq_own(m).wait()
        for d in range(1, NY):
            other = lax.rem(y + d, NY)
            dq_copy(m, other, y).wait_recv()
            dq_copy(m, y, other).wait_send()
            for part in range(2):
                o_copy(m, part, other, y).wait_recv()
                o_copy(m, part, y, other).wait_send()
        for part in range(2):
            o_own(m, part).wait()
        for index in range(6):
            r_copy(m, index).wait_send()
        for to_up, part, owner in ((1, 0, before), (0, 1, after)):
            z_copy(m, to_up, 0, 0, z).wait_send()
            z_copy(m, to_up, 1, 1, z).wait_send()
            z_copy(m, to_up, 2, part, owner).wait_send()
    for copy in list(kv_copies.values()) + list(wide_copies.values()):
        copy.wait_send()

    hand_end()


def finish_kernel(*refs):
    sources, targets, held, sem_in, sem_out = refs[:3], refs[3:6], refs[6:9], refs[9], refs[10]
    incoming = [
        pltpu.make_async_copy(source, buffer, sem_in.at[k])
        for k, (source, buffer) in enumerate(zip(sources, held))
    ]
    outgoing = [
        pltpu.make_async_copy(buffer, target, sem_out.at[k])
        for k, (buffer, target) in enumerate(zip(held, targets))
    ]
    for copy in incoming:
        copy.start()
    for copy, later in zip(incoming, outgoing):
        copy.wait()
        later.start()
    for copy in outgoing:
        copy.wait()


def finish(*arrays):
    whole = pl.BlockSpec(memory_space=pl.ANY)
    return pl.pallas_call(
        finish_kernel,
        out_shape=tuple(jax.ShapeDtypeStruct(a.shape, a.dtype) for a in arrays),
        in_specs=[whole] * 3,
        out_specs=(whole,) * 3,
        scratch_shapes=[pltpu.VMEM(a.shape, a.dtype) for a in arrays]
        + [pltpu.SemaphoreType.DMA((3,)), pltpu.SemaphoreType.DMA((3,))],
        name="finish",
    )(*arrays)


def on_device(queries, keys, values, grad_a, grad_b, imports, block_ids):
    wide = pltpu.VMEM((NY, ROWS, WIDE), BF16)
    pair = pltpu.VMEM((NZ, 2, NY, ROWS, HEAD), BF16)
    column = lambda n: pltpu.VMEM((n, NY, ROWS, HEAD), BF16)
    dma = lambda n: pltpu.SemaphoreType.DMA((n,))
    chunk = pltpu.VMEM((CHUNKS, 2 * ROWS, WIDE), F32)
    rows = pltpu.VMEM((WIDE, HEAD), BF16)
    whole = pl.BlockSpec(memory_space=pl.ANY)
    smem = pl.BlockSpec(memory_space=pltpu.SMEM)
    outputs = pl.pallas_call(
        step_kernel,
        out_shape=(
            jax.ShapeDtypeStruct(grad_a.shape, BF16),
            jax.ShapeDtypeStruct(grad_b.shape, BF16),
            jax.ShapeDtypeStruct((2, 1, ROWS, 2 * KEY_VALUE_HEADS * HEAD), BF16),
        ),
        in_specs=[whole] * 5 + [smem, smem],
        out_specs=(whole,) * 3,
        scratch_shapes=[
            wide, wide, wide, wide, pair, pair, wide, pltpu.VMEM((HALF, WIDE), BF16),
            wide, wide, pair, pair,
            column(2), column(2), column(4), column(4), column(4), column(4),
            chunk, chunk, pltpu.VMEM((NY * LISTED + 1, 2, ROWS, HEAD), F32), rows, rows,
            pltpu.SMEM((2 * NY * LISTED,), jnp.int32),
            pltpu.SMEM((2 * NY * BLOCKS,), jnp.int32),
            pltpu.SMEM((2 * NY,), jnp.int32),
            dma(12), dma(12), dma(12), dma(12), dma(12), dma(12), dma(8),
            dma(9), dma(8), dma(1), dma(8), dma(8), dma(12), dma(12), dma(16), dma(16), dma(6),
        ],
        compiler_params=pltpu.CompilerParams(
            collective_id=0, has_side_effects=True, vmem_limit_bytes=60 * 1024 * 1024
        ),
        name="step",
    )(queries, keys, values, grad_a, grad_b, imports, block_ids)
    return finish(*outputs)


def solution(mesh):
    return jax.shard_map(
        on_device,
        mesh=mesh,
        in_specs=(
            P(None, "pipe", "ctx", None),
            P(None, "pipe", "ctx", None),
            P(None, "pipe", "ctx", None),
            P("pipe", "ctx", None),
            P("pipe", "ctx", None),
            P(None, "pipe", None, None),
            P(None, "pipe", None),
        ),
        out_specs=(P("pipe", "ctx", None), P("pipe", "ctx", None), P(None, "pipe", "ctx", None)),
        check_vma=False,
    )
```

```python
import math

import jax
import jax.numpy as jnp
from jax import lax
from jax.experimental import pallas as pl
from jax.experimental.pallas import tpu as pltpu
from jax.sharding import PartitionSpec as P

KEY_VALUE_HEADS = 4
HEAD = 128
GROUP = 5
WIDE = GROUP * HEAD
ROWS = 128
HALF = ROWS // 2
NY = 4
NZ = 4
BLOCKS = NY * NZ
LISTED = 8
CHUNKS = LISTED // 2
FORWARD_AT = 2
RELAY_AT = 1
SCALE = 1.0 / math.sqrt(HEAD)
EXP2_SCALE = SCALE * math.log2(math.e)
NEG = -1e30
MESH = pl.DeviceIdType.MESH
BF16 = jnp.bfloat16
F32 = jnp.float32


def place():
    ctx = lax.axis_index("ctx")
    return ctx // NZ, ctx % NZ


def at_ctx(y, z):
    return {"ctx": lax.rem(y, NY) * NZ + lax.rem(z, NZ)}


def cols(index, width):
    return pl.ds(pl.multiple_of(index * width, width), width)


def remote(src, dst, send, recv, peer):
    return pltpu.make_async_remote_copy(
        src_ref=src, dst_ref=dst, send_sem=send, recv_sem=recv, device_id=peer, device_id_type=MESH
    )


def nt_dot(a, b):
    return lax.dot_general(a, b, (((1,), (1,)), ((), ())), preferred_element_type=F32)


def list_blocks(micro, z, imports, ids, slots, where_part, counts):
    for i in range(NY):
        mine = i * NZ + z
        block = ids[micro, 0, mine]

        def note(j, carry):
            count, found = carry[0], carry[1:]
            seen = imports[micro, 0, block, ids[micro, 0, j]]
            live = (seen == 1) & (j != mine)
            found = tuple(
                jnp.where(live & (count == p + 1), j, slot) for p, slot in enumerate(found)
            )
            position = jnp.where(live, i * LISTED + count, NY * LISTED)
            where_part[(micro * NY + i) * BLOCKS + j] = jnp.where(
                j == mine, i * LISTED, position
            )
            return (count + jnp.where(live, 1, 0),) + found

        start = (jnp.int32(1),) + (jnp.int32(0),) * (LISTED - 1)
        carry = lax.fori_loop(0, BLOCKS, note, start)
        base = (micro * NY + i) * LISTED
        counts[micro * NY + i] = carry[0]
        slots[base] = mine
        for p in range(LISTED - 1):
            slots[base + p + 1] = carry[p + 1]


def attend_block(micro, i, key_place, row_place, slots, counts, kv, q_rows, up_rows, scores,
                 grads, parts, dq_u):
    base = (micro * NY + i) * LISTED
    count = counts[micro * NY + i]

    def load(part, c):
        a, b = slots[base + 2 * c], slots[base + 2 * c + 1]
        return jnp.concatenate(
            [kv[lax.rem(a, NZ), part, a // NZ], kv[lax.rem(b, NZ), part, b // NZ]], axis=0
        )

    row_max = jnp.full((1, WIDE), NEG, F32)
    for c in range(CHUNKS):
        s = nt_dot(load(0, c), q_rows[...]) * EXP2_SCALE
        if c == 0:
            top = jnp.where(key_place <= row_place, s[:ROWS], NEG)
        else:
            top = s[:ROWS] + jnp.where(2 * c < count, 0.0, NEG)
        bottom = s[ROWS:] + jnp.where(2 * c + 1 < count, 0.0, NEG)
        scores[c, :ROWS] = top
        scores[c, ROWS:] = bottom
        grads[c] = nt_dot(load(1, c), up_rows[...])
        row_max = jnp.maximum(row_max, jnp.max(jnp.maximum(top, bottom), axis=0, keepdims=True))
    row_sum = jnp.zeros((1, WIDE), F32)
    inner = jnp.zeros((1, WIDE), F32)
    for c in range(CHUNKS):
        p = jnp.exp2(scores[c] - row_max)
        scores[c] = p
        row_sum = row_sum + jnp.sum(p, axis=0, keepdims=True)
        inner = inner + jnp.sum(p * grads[c], axis=0, keepdims=True)
    inverse = 1.0 / row_sum
    delta = inner * inverse
    dq_t = jnp.zeros((HEAD, WIDE), F32)
    for c in range(CHUNKS):
        probs = scores[c] * inverse
        score_grad = (probs * (grads[c] - delta)).astype(BF16)
        dv = jnp.dot(probs.astype(BF16), up_rows[...], preferred_element_type=F32)
        dk = jnp.dot(score_grad, q_rows[...], preferred_element_type=F32) * SCALE
        for half in range(2):
            span = slice(half * ROWS, (half + 1) * ROWS)
            parts[i * LISTED + 2 * c + half, 0] = dk[span]
            parts[i * LISTED + 2 * c + half, 1] = dv[span]
        dq_t = dq_t + lax.dot_general(
            load(0, c), score_grad, (((0,), (0,)), ((), ())), preferred_element_type=F32
        )
    dq_t = dq_t * SCALE
    for g in range(GROUP):
        span = slice(g * HEAD, (g + 1) * HEAD)
        dq_u[i, :, span] = dq_t[:, span].T.astype(BF16)


def step_kernel(
    queries, keys, values, grad_a, grad_b, imports, ids,
    dq_out_a, dq_out_b, kv_out,
    q_a, q_b, up_a, up_b, kv_a, kv_b, arrived, passing, dq_u_a, dq_u_b, dkv_a, dkv_b,
    relay_a, relay_b, landed_a, landed_b, summed_a, summed_b, total_a, total_b,
    scores, grads, parts, q_rows, up_rows,
    slots, where_part, counts,
    wide_send, wide_recv, kv_send, kv_recv, z_send, z_recv, local_in,
    hand_send, hand_recv, pass_recv, dq_send, dq_recv, r_send, r_recv, s_send, s_recv, o_send, o_recv, local_out,
):
    y, z = place()
    pipe = lax.axis_index("pipe")
    last = lax.axis_size("pipe") - 1
    edge = (last + 1) // 2
    spread_hand = edge == 2 * NY
    up, down = at_ctx(y, z + 1), at_ctx(y, z + NZ - 1)
    before, after = lax.rem(z + NZ - 1, NZ), lax.rem(z + 1, NZ)
    across = lax.rem(z + 2, NZ)
    kvs = (kv_a, kv_b)
    wide_src = (queries.at[0, 0], grad_a.at[0], queries.at[1, 0], grad_b.at[0])
    wide_dst = (q_a, up_a, q_b, up_b)
    kv_copies, kv_own, wide_copies, wide_own = {}, {}, {}, {}
    for m in range(2):
        for part, source in enumerate((keys, values)):
            kv_own[m, part] = pltpu.make_async_copy(
                source.at[m, 0, :, cols(y, HEAD)], kvs[m].at[z, part, y],
                local_in.at[2 * m + part],
            )
            kv_own[m, part].start()
    for w in range(4):
        wide_own[w] = pltpu.make_async_copy(
            wide_src[w].at[:, cols(y, WIDE)], wide_dst[w].at[y], local_in.at[4 + w]
        )
        wide_own[w].start()

    def z_copy(m, to_up, index, part, owner, piece):
        ref = kvs[m].at[owner, part, piece]
        where = ((m * 2 + to_up) * 3 + index) * NY + piece
        return remote(ref, ref, z_send.at[where], z_recv.at[where], up if to_up else down)

    def spread_piece(m, piece):
        for to_up, part in ((1, 0), (0, 1), (1, 1), (0, 0)):
            z_copy(m, to_up, part, part, z, piece).start()

    barrier = pltpu.get_barrier_semaphore()
    peers = [at_ctx(y + d, z) for d in range(1, NY)] + [up, down]
    for peer in peers:
        pl.semaphore_signal(barrier, inc=1, device_id=peer, device_id_type=MESH)

    @pl.when(pipe < last)
    def _():
        pl.semaphore_signal(barrier, inc=1, device_id={"pipe": pipe + 1}, device_id_type=MESH)

    callers = len(peers) + jnp.where(pipe > 0, 1, 0)
    if spread_hand:
        @pl.when(pipe == edge - 1)
        def _():
            for r in range(1, edge):
                pl.semaphore_signal(
                    barrier, inc=1, device_id={"pipe": edge + r}, device_id_type=MESH
                )

        @pl.when(pipe > edge)
        def _():
            pl.semaphore_signal(barrier, inc=1, device_id={"pipe": edge}, device_id_type=MESH)

        callers = callers + jnp.where(pipe > edge, 1, 0) + jnp.where(pipe == edge, edge - 1, 0)
    pl.semaphore_wait(barrier, callers)

    for m in range(2):
        for part, source in enumerate((keys, values)):
            for d in range(1, NY):
                there = lax.rem(y + d, NY)
                index = (m * 2 + part) * 3 + d - 1
                kv_copies[m, part, d] = remote(
                    source.at[m, 0, :, cols(there, HEAD)], kvs[m].at[z, part, y],
                    kv_send.at[index], kv_recv.at[index], at_ctx(y + d, z),
                )
                kv_copies[m, part, d].start()
        for w in (2 * m, 2 * m + 1):
            for d in range(1, NY):
                there = lax.rem(y + d, NY)
                index = w * 3 + d - 1
                wide_copies[w, d] = remote(
                    wide_src[w].at[:, cols(there, WIDE)], wide_dst[w].at[y],
                    wide_send.at[index], wide_recv.at[index], at_ctx(y + d, z),
                )
                wide_copies[w, d].start()
        if m == 0:
            for part in range(2):
                kv_own[0, part].wait()
            spread_piece(0, y)

    def spread(m):
        for d in (1, 3, 2):
            for part in range(2):
                kv_copies[m, part, NY - d].wait_recv()
            spread_piece(m, lax.rem(y + d, NY))

    def forward(m):
        for d in (0, 1, 3, 2):
            piece = lax.rem(y + d, NY)
            for to_up, part, owner in ((1, 0, before), (0, 1, after)):
                z_copy(m, to_up, part, part, z, piece).wait_recv()
                z_copy(m, to_up, 2, part, owner, piece).start()

    def wait_spread(m):
        for b in range(NY):
            z_copy(m, 1, 1, 1, z, b).wait_recv()
            z_copy(m, 0, 0, 0, z, b).wait_recv()
            z_copy(m, 1, 2, 0, across, b).wait_recv()
            z_copy(m, 0, 2, 1, across, b).wait_recv()
        for w in (2 * m, 2 * m + 1):
            wide_own[w].wait()
            for d in range(1, NY):
                wide_copies[w, d].wait_recv()

    def hand(i, h):
        span = pl.ds(h * HALF, HALF)
        return remote(
            dq_u_a.at[i, span], arrived.at[i, span], hand_send.at[2 * i + h],
            hand_recv.at[2 * i + h], {"pipe": lax.rem(pipe + last, last + 1)},
        )

    def to_relay(i, h):
        return remote(
            dq_u_a.at[i, pl.ds(h * HALF, HALF)], passing, hand_send.at[2 * i + h],
            pass_recv.at[0], {"pipe": lax.rem(edge + lax.rem(2 + 2 * i + h, edge), last + 1)},
        )

    piece = lax.rem(pipe + 2 * edge - 2, 2 * NY)

    def from_relay():
        i, h = piece // 2, lax.rem(piece, 2)
        return remote(
            passing, arrived.at[i, pl.ds(pl.multiple_of(h * HALF, HALF), HALF)],
            hand_send.at[2 * NY], hand_recv.at[piece], {"pipe": edge - 1},
        )

    def hand_over(i):
        direct = (pipe > 0) & (pipe != edge) if spread_hand else pipe > 0

        @pl.when(direct)
        def _():
            hand(i, 0).start()
            hand(i, 1).start()

        if spread_hand:
            @pl.when(pipe == edge)
            def _():
                @pl.when(i < NY - 1)
                def _():
                    to_relay(i, 0).start()

                @pl.when(i == NY - 1)
                def _():
                    hand(i, 0).start()

                to_relay(i, 1).start()

    def pass_on(i):
        if spread_hand:
            @pl.when((pipe > edge) & (piece // 2 + 1 == i))
            def _():
                to_relay(0, 0).wait_recv()
                from_relay().start()

    def hand_end():
        direct = (pipe > 0) & (pipe <= edge) if spread_hand else pipe > 0

        @pl.when(direct)
        def _():
            for i in range(NY):
                hand(i, 0).wait_send()
                hand(i, 1).wait_send()

        if spread_hand:
            @pl.when(pipe > edge)
            def _():
                for i in range(NY):
                    hand(i, 0).wait_send()
                    hand(i, 1).wait_send()
                from_relay().wait_send()

    def dq_copy(m, sender, target):
        return remote(
            (dq_u_a, dq_u_b)[m].at[target],
            (dq_out_a, dq_out_b)[m].at[0, :, cols(sender, WIDE)],
            dq_send.at[m * NY + target], dq_recv.at[m * NY + sender], at_ctx(target, z),
        )

    def dq_own(m):
        return pltpu.make_async_copy(
            (dq_u_a, dq_u_b)[m].at[y], (dq_out_a, dq_out_b)[m].at[0, :, cols(y, WIDE)],
            local_out.at[m],
        )

    def return_dq(m, i):
        @pl.when(i == y)
        def _():
            dq_own(m).start()

        @pl.when(i != y)
        def _():
            dq_copy(m, y, i).start()

    def combine(m, dkv):
        def one(slot, nothing):
            places = [where_part[(m * NY + i) * BLOCKS + slot] for i in range(NY)]
            for part in range(2):
                value = parts[places[0], part]
                for at in places[1:]:
                    value = value + parts[at, part]
                dkv[lax.rem(slot, NZ), part, slot // NZ] = value.astype(BF16)
            return nothing

        lax.fori_loop(0, BLOCKS, one, 0)

    relays, landeds, totals, dkvs = (
        (relay_a, relay_b), (landed_a, landed_b), (total_a, total_b), (dkv_a, dkv_b),
    )

    def r_copy(m, index):
        relay, landed, dkv = relays[m], landeds[m], dkvs[m]
        src, dst, peer = (
            (dkv.at[across, 0], relay.at[0], up),
            (dkv.at[across, 1], relay.at[1], down),
            (dkv.at[after, 1], landed.at[0], up),
            (dkv.at[before, 0], landed.at[1], down),
        )[index]
        return remote(src, dst, r_send.at[m * 4 + index], r_recv.at[m * 4 + index], peer)

    def s_copy(m, part, turn):
        where = (m * 2 + part) * NY + turn
        return remote(
            totals[m].at[part, turn], (summed_a, summed_b)[m].at[part, turn],
            s_send.at[where], s_recv.at[where], (up, down)[part],
        )

    def reduce_start(m):
        for index in range(4):
            r_copy(m, index).start()

    def reduce_relay(m):
        relay, total, dkv = relays[m], totals[m], dkvs[m]
        r_copy(m, 0).wait_recv()
        r_copy(m, 1).wait_recv()
        for turn, d in enumerate((2, 1, 3, 0)):
            piece = lax.rem(y + d, NY)
            for part, owner in ((0, after), (1, before)):
                total[part, turn] = (
                    relay[part, piece].astype(F32) + dkv[owner, part, piece].astype(F32)
                ).astype(BF16)
                s_copy(m, part, turn).start()

    def o_copy(m, part, sender, target, turn=0):
        return remote(
            totals[m].at[2 + part, turn],
            kv_out.at[m, 0, :, cols(KEY_VALUE_HEADS * part + sender, HEAD)],
            o_send.at[(m * 2 + part) * NY + target], o_recv.at[(m * 2 + part) * NY + sender],
            at_ctx(target, z),
        )

    def o_own(m, part):
        return pltpu.make_async_copy(
            totals[m].at[2 + part, NY - 1],
            kv_out.at[m, 0, :, cols(KEY_VALUE_HEADS * part + y, HEAD)],
            local_out.at[2 + 2 * m + part],
        )

    def reduce_end(m):
        landed, total, dkv, summed = landeds[m], totals[m], dkvs[m], (summed_a, summed_b)[m]
        r_copy(m, 2).wait_recv()
        r_copy(m, 3).wait_recv()
        for turn, d in enumerate((2, 1, 3, 0)):
            piece = lax.rem(y + d, NY)
            for part in range(2):
                s_copy(m, part, turn).wait_recv()
                total[2 + part, turn] = (
                    dkv[z, part, piece].astype(F32)
                    + landed[1 - part, piece].astype(F32)
                    + summed[part, turn].astype(F32)
                ).astype(BF16)
                if d:
                    o_copy(m, part, y, piece, turn).start()
                else:
                    o_own(m, part).start()

    key_place = lax.broadcasted_iota(jnp.int32, (ROWS, WIDE), 0)
    row_place = lax.rem(lax.broadcasted_iota(jnp.int32, (ROWS, WIDE), 1), ROWS)
    parts[NY * LISTED] = jnp.zeros_like(parts[NY * LISTED])
    spread(0)
    list_blocks(0, z, imports, ids, slots, where_part, counts)
    forward(0)
    for part in range(2):
        kv_own[1, part].wait()
    spread_piece(1, y)
    spread(1)
    list_blocks(1, z, imports, ids, slots, where_part, counts)
    wait_spread(0)

    def turn_a(i, nothing):
        for g in range(GROUP):
            span = slice(g * HEAD, (g + 1) * HEAD)
            q_rows[span, :] = q_a[i, :, span]
            up_rows[span, :] = up_a[i, :, span]
        attend_block(0, i, key_place, row_place, slots, counts, kv_a, q_rows, up_rows, scores,
                     grads, parts, dq_u_a)

        hand_over(i)
        return_dq(0, i)
        pass_on(i)

        @pl.when(i == FORWARD_AT)
        def _():
            forward(1)

        return nothing

    lax.fori_loop(0, NY, turn_a, 0)
    combine(0, dkv_a)
    pass_on(NY)
    reduce_start(0)
    wait_spread(1)

    def turn_b(i, nothing):
        @pl.when(pipe < last)
        def _():
            hand(i, 0).wait_recv()
            hand(i, 1).wait_recv()

        for g in range(GROUP):
            span = slice(g * HEAD, (g + 1) * HEAD)
            q_rows[span, :] = q_b[i, :, span]
            came = jnp.where(pipe < last, arrived[i, :, span].astype(F32), 0.0)
            up_rows[span, :] = (up_b[i, :, span].astype(F32) + came).astype(BF16)
        attend_block(1, i, key_place, row_place, slots, counts, kv_b, q_rows, up_rows, scores,
                     grads, parts, dq_u_b)
        return_dq(1, i)

        @pl.when(i == RELAY_AT)
        def _():
            reduce_relay(0)

        return nothing

    lax.fori_loop(0, NY, turn_b, 0)
    combine(1, dkv_b)
    reduce_start(1)
    reduce_end(0)
    reduce_relay(1)
    reduce_end(1)

    for m in range(2):
        dq_own(m).wait()
        for d in range(1, NY):
            other = lax.rem(y + d, NY)
            dq_copy(m, other, y).wait_recv()
            dq_copy(m, y, other).wait_send()
            for part in range(2):
                o_copy(m, part, other, y).wait_recv()
                o_copy(m, part, y, other).wait_send()
        for part in range(2):
            o_own(m, part).wait()
        for index in range(4):
            r_copy(m, index).wait_send()
        for b in range(NY):
            for part in range(2):
                s_copy(m, part, b).wait_send()
            for to_up, part, owner in ((1, 0, before), (0, 1, after)):
                z_copy(m, to_up, 0, 0, z, b).wait_send()
                z_copy(m, to_up, 1, 1, z, b).wait_send()
                z_copy(m, to_up, 2, part, owner, b).wait_send()
    for copy in list(kv_copies.values()) + list(wide_copies.values()):
        copy.wait_send()

    hand_end()


def finish_kernel(*refs):
    sources, targets, held, sem_in, sem_out = refs[:3], refs[3:6], refs[6:9], refs[9], refs[10]
    incoming = [
        pltpu.make_async_copy(source, buffer, sem_in.at[k])
        for k, (source, buffer) in enumerate(zip(sources, held))
    ]
    outgoing = [
        pltpu.make_async_copy(buffer, target, sem_out.at[k])
        for k, (buffer, target) in enumerate(zip(held, targets))
    ]
    for copy in incoming:
        copy.start()
    for copy, later in zip(incoming, outgoing):
        copy.wait()
        later.start()
    for copy in outgoing:
        copy.wait()


def finish(*arrays):
    whole = pl.BlockSpec(memory_space=pl.ANY)
    return pl.pallas_call(
        finish_kernel,
        out_shape=tuple(jax.ShapeDtypeStruct(a.shape, a.dtype) for a in arrays),
        in_specs=[whole] * 3,
        out_specs=(whole,) * 3,
        scratch_shapes=[pltpu.VMEM(a.shape, a.dtype) for a in arrays]
        + [pltpu.SemaphoreType.DMA((3,)), pltpu.SemaphoreType.DMA((3,))],
        name="finish",
    )(*arrays)


def on_device(queries, keys, values, grad_a, grad_b, imports, block_ids):
    wide = pltpu.VMEM((NY, ROWS, WIDE), BF16)
    pair = pltpu.VMEM((NZ, 2, NY, ROWS, HEAD), BF16)
    column = lambda n: pltpu.VMEM((n, NY, ROWS, HEAD), BF16)
    dma = lambda n: pltpu.SemaphoreType.DMA((n,))
    chunk = pltpu.VMEM((CHUNKS, 2 * ROWS, WIDE), F32)
    rows = pltpu.VMEM((WIDE, HEAD), BF16)
    whole = pl.BlockSpec(memory_space=pl.ANY)
    smem = pl.BlockSpec(memory_space=pltpu.SMEM)
    outputs = pl.pallas_call(
        step_kernel,
        out_shape=(
            jax.ShapeDtypeStruct(grad_a.shape, BF16),
            jax.ShapeDtypeStruct(grad_b.shape, BF16),
            jax.ShapeDtypeStruct((2, 1, ROWS, 2 * KEY_VALUE_HEADS * HEAD), BF16),
        ),
        in_specs=[whole] * 5 + [smem, smem],
        out_specs=(whole,) * 3,
        scratch_shapes=[
            wide, wide, wide, wide, pair, pair, wide, pltpu.VMEM((HALF, WIDE), BF16),
            wide, wide, pair, pair,
            column(2), column(2), column(2), column(2), column(2), column(2), column(4), column(4),
            chunk, chunk, pltpu.VMEM((NY * LISTED + 1, 2, ROWS, HEAD), F32), rows, rows,
            pltpu.SMEM((2 * NY * LISTED,), jnp.int32),
            pltpu.SMEM((2 * NY * BLOCKS,), jnp.int32),
            pltpu.SMEM((2 * NY,), jnp.int32),
            dma(12), dma(12), dma(12), dma(12), dma(48), dma(48), dma(8),
            dma(9), dma(8), dma(1), dma(8), dma(8), dma(8), dma(8), dma(16), dma(16), dma(16), dma(16), dma(6),
        ],
        compiler_params=pltpu.CompilerParams(
            collective_id=0, has_side_effects=True, vmem_limit_bytes=60 * 1024 * 1024
        ),
        name="step",
    )(queries, keys, values, grad_a, grad_b, imports, block_ids)
    return finish(*outputs)


def solution(mesh):
    return jax.shard_map(
        on_device,
        mesh=mesh,
        in_specs=(
            P(None, "pipe", "ctx", None),
            P(None, "pipe", "ctx", None),
            P(None, "pipe", "ctx", None),
            P("pipe", "ctx", None),
            P("pipe", "ctx", None),
            P(None, "pipe", None, None),
            P(None, "pipe", None),
        ),
        out_specs=(P("pipe", "ctx", None), P("pipe", "ctx", None), P(None, "pipe", "ctx", None)),
        check_vma=False,
    )
```

```python
import math

import jax
import jax.numpy as jnp
from jax import lax
from jax.experimental import pallas as pl
from jax.experimental.pallas import tpu as pltpu
from jax.sharding import PartitionSpec as P

KEY_VALUE_HEADS = 4
HEAD = 128
GROUP = 5
WIDE = GROUP * HEAD
ROWS = 128
HALF = ROWS // 2
NY = 4
NZ = 4
BLOCKS = NY * NZ
LISTED = 8
CHUNKS = LISTED // 2
FORWARD_AT = 2
PIECES = 4
RELAY_AT = 1
SCALE = 1.0 / math.sqrt(HEAD)
EXP2_SCALE = SCALE * math.log2(math.e)
NEG = -1e30
MESH = pl.DeviceIdType.MESH
BF16 = jnp.bfloat16
F32 = jnp.float32


def place():
    ctx = lax.axis_index("ctx")
    return ctx // NZ, ctx % NZ


def at_ctx(y, z):
    return {"ctx": lax.rem(y, NY) * NZ + lax.rem(z, NZ)}


def cols(index, width):
    return pl.ds(pl.multiple_of(index * width, width), width)


def remote(src, dst, send, recv, peer):
    return pltpu.make_async_remote_copy(
        src_ref=src, dst_ref=dst, send_sem=send, recv_sem=recv, device_id=peer, device_id_type=MESH
    )


def nt_dot(a, b):
    return lax.dot_general(a, b, (((1,), (1,)), ((), ())), preferred_element_type=F32)


def list_blocks(micro, z, imports, ids, slots, where_part, counts):
    for i in range(NY):
        mine = i * NZ + z
        block = ids[micro, 0, mine]

        def note(j, carry):
            count, found = carry[0], carry[1:]
            seen = imports[micro, 0, block, ids[micro, 0, j]]
            live = (seen == 1) & (j != mine)
            found = tuple(
                jnp.where(live & (count == p + 1), j, slot) for p, slot in enumerate(found)
            )
            position = jnp.where(live, i * LISTED + count, NY * LISTED)
            where_part[(micro * NY + i) * BLOCKS + j] = jnp.where(
                j == mine, i * LISTED, position
            )
            return (count + jnp.where(live, 1, 0),) + found

        start = (jnp.int32(1),) + (jnp.int32(0),) * (LISTED - 1)
        carry = lax.fori_loop(0, BLOCKS, note, start)
        base = (micro * NY + i) * LISTED
        counts[micro * NY + i] = carry[0]
        slots[base] = mine
        for p in range(LISTED - 1):
            slots[base + p + 1] = carry[p + 1]


def attend_block(micro, i, key_place, row_place, slots, counts, kv, q_rows, up_rows, scores,
                 grads, parts, dq_u):
    base = (micro * NY + i) * LISTED
    count = counts[micro * NY + i]

    def load(part, c):
        a, b = slots[base + 2 * c], slots[base + 2 * c + 1]
        return jnp.concatenate(
            [kv[lax.rem(a, NZ), part, a // NZ], kv[lax.rem(b, NZ), part, b // NZ]], axis=0
        )

    row_max = jnp.full((1, WIDE), NEG, F32)
    for c in range(CHUNKS):
        s = nt_dot(load(0, c), q_rows[...]) * EXP2_SCALE
        if c == 0:
            top = jnp.where(key_place <= row_place, s[:ROWS], NEG)
        else:
            top = s[:ROWS] + jnp.where(2 * c < count, 0.0, NEG)
        bottom = s[ROWS:] + jnp.where(2 * c + 1 < count, 0.0, NEG)
        scores[c, :ROWS] = top
        scores[c, ROWS:] = bottom
        grads[c] = nt_dot(load(1, c), up_rows[...])
        row_max = jnp.maximum(row_max, jnp.max(jnp.maximum(top, bottom), axis=0, keepdims=True))
    row_sum = jnp.zeros((1, WIDE), F32)
    inner = jnp.zeros((1, WIDE), F32)
    for c in range(CHUNKS):
        p = jnp.exp2(scores[c] - row_max)
        scores[c] = p
        row_sum = row_sum + jnp.sum(p, axis=0, keepdims=True)
        inner = inner + jnp.sum(p * grads[c], axis=0, keepdims=True)
    inverse = 1.0 / row_sum
    delta = inner * inverse
    dq_t = jnp.zeros((HEAD, WIDE), F32)
    for c in range(CHUNKS):
        probs = scores[c] * inverse
        score_grad = (probs * (grads[c] - delta)).astype(BF16)
        dv = jnp.dot(probs.astype(BF16), up_rows[...], preferred_element_type=F32)
        dk = jnp.dot(score_grad, q_rows[...], preferred_element_type=F32) * SCALE
        for half in range(2):
            span = slice(half * ROWS, (half + 1) * ROWS)
            parts[i * LISTED + 2 * c + half, 0] = dk[span]
            parts[i * LISTED + 2 * c + half, 1] = dv[span]
        dq_t = dq_t + lax.dot_general(
            load(0, c), score_grad, (((0,), (0,)), ((), ())), preferred_element_type=F32
        )
    dq_t = dq_t * SCALE
    for g in range(GROUP):
        span = slice(g * HEAD, (g + 1) * HEAD)
        dq_u[i, :, span] = dq_t[:, span].T.astype(BF16)


def step_kernel(
    queries, keys, values, grad_a, grad_b, imports, ids,
    dq_out_a, dq_out_b, kv_out,
    q_a, q_b, up_a, up_b, kv_a, kv_b, arrived, passing, dq_u_a, dq_u_b, dkv_a, dkv_b,
    relay_a, relay_b, landed_a, landed_b, summed_a, summed_b, total_a, total_b,
    scores, grads, parts, q_rows, up_rows,
    slots, where_part, counts,
    wide_send, wide_recv, kv_send, kv_recv, z_send, z_recv, local_in,
    hand_send, hand_recv, pass_recv, dq_send, dq_recv, r_send, r_recv, s_send, s_recv, o_send, o_recv, local_out,
):
    y, z = place()
    pipe = lax.axis_index("pipe")
    last = lax.axis_size("pipe") - 1
    edge = (last + 1) // 2
    spread_hand = edge == 2 * NY
    up, down = at_ctx(y, z + 1), at_ctx(y, z + NZ - 1)
    before, after = lax.rem(z + NZ - 1, NZ), lax.rem(z + 1, NZ)
    across = lax.rem(z + 2, NZ)
    kvs = (kv_a, kv_b)
    wide_src = (queries.at[0, 0], grad_a.at[0], queries.at[1, 0], grad_b.at[0])
    wide_dst = (q_a, up_a, q_b, up_b)
    kv_copies, kv_own, wide_copies, wide_own = {}, {}, {}, {}
    for m in range(2):
        for part, source in enumerate((keys, values)):
            kv_own[m, part] = pltpu.make_async_copy(
                source.at[m, 0, :, cols(y, HEAD)], kvs[m].at[z, part, y],
                local_in.at[2 * m + part],
            )
            kv_own[m, part].start()
    for w in range(4):
        wide_own[w] = pltpu.make_async_copy(
            wide_src[w].at[:, cols(y, WIDE)], wide_dst[w].at[y], local_in.at[4 + w]
        )
        wide_own[w].start()

    def z_copy(m, to_up, index, part, owner, piece):
        ref = kvs[m].at[owner, part, piece]
        where = ((m * 2 + to_up) * 3 + index) * NY + piece
        return remote(ref, ref, z_send.at[where], z_recv.at[where], up if to_up else down)

    def spread_piece(m, piece):
        for to_up, part in ((1, 0), (0, 1), (1, 1), (0, 0)):
            z_copy(m, to_up, part, part, z, piece).start()

    barrier = pltpu.get_barrier_semaphore()
    peers = [at_ctx(y + d, z) for d in range(1, NY)] + [up, down]
    for peer in peers:
        pl.semaphore_signal(barrier, inc=1, device_id=peer, device_id_type=MESH)

    @pl.when(pipe < last)
    def _():
        pl.semaphore_signal(barrier, inc=1, device_id={"pipe": pipe + 1}, device_id_type=MESH)

    callers = len(peers) + jnp.where(pipe > 0, 1, 0)
    if spread_hand:
        @pl.when(pipe == edge - 1)
        def _():
            for r in range(1, edge):
                pl.semaphore_signal(
                    barrier, inc=1, device_id={"pipe": edge + r}, device_id_type=MESH
                )

        @pl.when(pipe > edge)
        def _():
            pl.semaphore_signal(barrier, inc=1, device_id={"pipe": edge}, device_id_type=MESH)

        callers = callers + jnp.where(pipe > edge, 1, 0) + jnp.where(pipe == edge, edge - 1, 0)
    pl.semaphore_wait(barrier, callers)

    def start_kv(m):
        for d in range(1, NY):
            there = lax.rem(y + d, NY)
            for part, source in enumerate((keys, values)):
                index = (m * 2 + part) * 3 + d - 1
                kv_copies[m, part, d] = remote(
                    source.at[m, 0, :, cols(there, HEAD)], kvs[m].at[z, part, y],
                    kv_send.at[index], kv_recv.at[index], at_ctx(y + d, z),
                )
                kv_copies[m, part, d].start()

    def start_wide(w):
        for d in range(1, NY):
            there = lax.rem(y + d, NY)
            index = w * 3 + d - 1
            wide_copies[w, d] = remote(
                wide_src[w].at[:, cols(there, WIDE)], wide_dst[w].at[y],
                wide_send.at[index], wide_recv.at[index], at_ctx(y + d, z),
            )
            wide_copies[w, d].start()

    start_kv(0)
    for part in range(2):
        kv_own[0, part].wait()
    spread_piece(0, y)
    start_kv(1)
    start_wide(0)
    start_wide(1)
    start_wide(2)
    start_wide(3)

    def spread(m):
        for d in (1, 3, 2):
            for part in range(2):
                kv_copies[m, part, NY - d].wait_recv()
            spread_piece(m, lax.rem(y + d, NY))

    def forward(m, order=(0, 1, 3, 2)):
        for d in order:
            piece = lax.rem(y + d, NY)
            for to_up, part, owner in ((1, 0, before), (0, 1, after)):
                z_copy(m, to_up, part, part, z, piece).wait_recv()
                z_copy(m, to_up, 2, part, owner, piece).start()

    def wait_spread(m):
        for b in range(NY):
            z_copy(m, 1, 1, 1, z, b).wait_recv()
            z_copy(m, 0, 0, 0, z, b).wait_recv()
            z_copy(m, 1, 2, 0, across, b).wait_recv()
            z_copy(m, 0, 2, 1, across, b).wait_recv()
        for w in (2 * m, 2 * m + 1):
            wide_own[w].wait()
            for d in range(1, NY):
                wide_copies[w, d].wait_recv()

    def hand(i, h):
        span = pl.ds(h * HALF, HALF)
        return remote(
            dq_u_a.at[i, span], arrived.at[i, span], hand_send.at[2 * i + h],
            hand_recv.at[2 * i + h], {"pipe": lax.rem(pipe + last, last + 1)},
        )

    def to_relay(i, h):
        return remote(
            dq_u_a.at[i, pl.ds(h * HALF, HALF)], passing, hand_send.at[2 * i + h],
            pass_recv.at[0], {"pipe": lax.rem(edge + lax.rem(2 + 2 * i + h, edge), last + 1)},
        )

    piece = lax.rem(pipe + 2 * edge - 2, 2 * NY)

    def from_relay():
        i, h = piece // 2, lax.rem(piece, 2)
        return remote(
            passing, arrived.at[i, pl.ds(pl.multiple_of(h * HALF, HALF), HALF)],
            hand_send.at[2 * NY], hand_recv.at[piece], {"pipe": edge - 1},
        )

    def hand_over(i):
        direct = (pipe > 0) & (pipe != edge) if spread_hand else pipe > 0

        @pl.when(direct)
        def _():
            hand(i, 0).start()
            hand(i, 1).start()

        if spread_hand:
            @pl.when(pipe == edge)
            def _():
                @pl.when(i < NY - 1)
                def _():
                    to_relay(i, 0).start()

                @pl.when(i == NY - 1)
                def _():
                    hand(i, 0).start()

                to_relay(i, 1).start()

    def pass_on(i):
        if spread_hand:
            @pl.when((pipe > edge) & (piece // 2 + 1 == i))
            def _():
                to_relay(0, 0).wait_recv()
                from_relay().start()

    def hand_end():
        direct = (pipe > 0) & (pipe <= edge) if spread_hand else pipe > 0

        @pl.when(direct)
        def _():
            for i in range(NY):
                hand(i, 0).wait_send()
                hand(i, 1).wait_send()

        if spread_hand:
            @pl.when(pipe > edge)
            def _():
                for i in range(NY):
                    hand(i, 0).wait_send()
                    hand(i, 1).wait_send()
                from_relay().wait_send()

    def dq_copy(m, sender, target):
        return remote(
            (dq_u_a, dq_u_b)[m].at[target],
            (dq_out_a, dq_out_b)[m].at[0, :, cols(sender, WIDE)],
            dq_send.at[m * NY + target], dq_recv.at[m * NY + sender], at_ctx(target, z),
        )

    def dq_own(m):
        return pltpu.make_async_copy(
            (dq_u_a, dq_u_b)[m].at[y], (dq_out_a, dq_out_b)[m].at[0, :, cols(y, WIDE)],
            local_out.at[m],
        )

    def return_dq(m, i):
        @pl.when(i == y)
        def _():
            dq_own(m).start()

        @pl.when(i != y)
        def _():
            dq_copy(m, y, i).start()

    def combine(m, dkv):
        def one(slot, nothing):
            places = [where_part[(m * NY + i) * BLOCKS + slot] for i in range(NY)]
            for part in range(2):
                value = parts[places[0], part]
                for at in places[1:]:
                    value = value + parts[at, part]
                dkv[lax.rem(slot, NZ), part, slot // NZ] = value.astype(BF16)
            return nothing

        lax.fori_loop(0, BLOCKS, one, 0)

    relays, landeds, totals, dkvs = (
        (relay_a, relay_b), (landed_a, landed_b), (total_a, total_b), (dkv_a, dkv_b),
    )

    def r_copy(m, index):
        relay, landed, dkv = relays[m], landeds[m], dkvs[m]
        src, dst, peer = (
            (dkv.at[across, 0], relay.at[0], up),
            (dkv.at[across, 1], relay.at[1], down),
            (dkv.at[after, 1], landed.at[0], up),
            (dkv.at[before, 0], landed.at[1], down),
        )[index]
        return remote(src, dst, r_send.at[m * 4 + index], r_recv.at[m * 4 + index], peer)

    def s_copy(m, part, turn):
        where = (m * 2 + part) * NY + turn
        return remote(
            totals[m].at[part, turn], (summed_a, summed_b)[m].at[part, turn],
            s_send.at[where], s_recv.at[where], (up, down)[part],
        )

    def reduce_start(m):
        for index in range(4):
            r_copy(m, index).start()

    def reduce_relay(m):
        relay, total, dkv = relays[m], totals[m], dkvs[m]
        r_copy(m, 0).wait_recv()
        r_copy(m, 1).wait_recv()
        for turn, d in enumerate((2, 1, 3, 0)):
            piece = lax.rem(y + d, NY)
            for part, owner in ((0, after), (1, before)):
                total[part, turn] = (
                    relay[part, piece].astype(F32) + dkv[owner, part, piece].astype(F32)
                ).astype(BF16)
                s_copy(m, part, turn).start()

    def o_copy(m, part, sender, target, turn=0):
        return remote(
            totals[m].at[2 + part, turn],
            kv_out.at[m, 0, :, cols(KEY_VALUE_HEADS * part + sender, HEAD)],
            o_send.at[(m * 2 + part) * NY + target], o_recv.at[(m * 2 + part) * NY + sender],
            at_ctx(target, z),
        )

    def o_own(m, part):
        return pltpu.make_async_copy(
            totals[m].at[2 + part, NY - 1],
            kv_out.at[m, 0, :, cols(KEY_VALUE_HEADS * part + y, HEAD)],
            local_out.at[2 + 2 * m + part],
        )

    def reduce_end(m):
        landed, total, dkv, summed = landeds[m], totals[m], dkvs[m], (summed_a, summed_b)[m]
        r_copy(m, 2).wait_recv()
        r_copy(m, 3).wait_recv()
        for turn, d in enumerate((2, 1, 3, 0)):
            piece = lax.rem(y + d, NY)
            for part in range(2):
                s_copy(m, part, turn).wait_recv()
                total[2 + part, turn] = (
                    dkv[z, part, piece].astype(F32)
                    + landed[1 - part, piece].astype(F32)
                    + summed[part, turn].astype(F32)
                ).astype(BF16)
                if d:
                    o_copy(m, part, y, piece, turn).start()
                else:
                    o_own(m, part).start()

    key_place = lax.broadcasted_iota(jnp.int32, (ROWS, WIDE), 0)
    row_place = lax.rem(lax.broadcasted_iota(jnp.int32, (ROWS, WIDE), 1), ROWS)
    parts[NY * LISTED] = jnp.zeros_like(parts[NY * LISTED])
    spread(0)
    list_blocks(0, z, imports, ids, slots, where_part, counts)
    forward(0)
    for part in range(2):
        kv_own[1, part].wait()
    spread_piece(1, y)
    spread(1)
    list_blocks(1, z, imports, ids, slots, where_part, counts)
    wait_spread(0)

    def turn_a(i, nothing):
        for g in range(GROUP):
            span = slice(g * HEAD, (g + 1) * HEAD)
            q_rows[span, :] = q_a[i, :, span]
            up_rows[span, :] = up_a[i, :, span]
        attend_block(0, i, key_place, row_place, slots, counts, kv_a, q_rows, up_rows, scores,
                     grads, parts, dq_u_a)

        hand_over(i)
        return_dq(0, i)
        pass_on(i)

        @pl.when(i == FORWARD_AT - 1)
        def _():
            forward(1, (0, 1))

        @pl.when(i == FORWARD_AT)
        def _():
            forward(1, (3, 2))

        return nothing

    lax.fori_loop(0, NY, turn_a, 0)
    combine(0, dkv_a)
    pass_on(NY)
    reduce_start(0)
    wait_spread(1)

    def turn_b(i, nothing):
        @pl.when(pipe < last)
        def _():
            hand(i, 0).wait_recv()
            hand(i, 1).wait_recv()

        for g in range(GROUP):
            span = slice(g * HEAD, (g + 1) * HEAD)
            q_rows[span, :] = q_b[i, :, span]
            came = jnp.where(pipe < last, arrived[i, :, span].astype(F32), 0.0)
            up_rows[span, :] = (up_b[i, :, span].astype(F32) + came).astype(BF16)
        attend_block(1, i, key_place, row_place, slots, counts, kv_b, q_rows, up_rows, scores,
                     grads, parts, dq_u_b)
        return_dq(1, i)

        @pl.when(i == RELAY_AT)
        def _():
            reduce_relay(0)

        return nothing

    lax.fori_loop(0, NY, turn_b, 0)
    combine(1, dkv_b)
    reduce_start(1)
    reduce_end(0)
    reduce_relay(1)
    reduce_end(1)

    for m in range(2):
        dq_own(m).wait()
        for d in range(1, NY):
            other = lax.rem(y + d, NY)
            dq_copy(m, other, y).wait_recv()
            dq_copy(m, y, other).wait_send()
            for part in range(2):
                o_copy(m, part, other, y).wait_recv()
                o_copy(m, part, y, other).wait_send()
        for part in range(2):
            o_own(m, part).wait()
        for index in range(4):
            r_copy(m, index).wait_send()
        for b in range(NY):
            for part in range(2):
                s_copy(m, part, b).wait_send()
            for to_up, part, owner in ((1, 0, before), (0, 1, after)):
                z_copy(m, to_up, 0, 0, z, b).wait_send()
                z_copy(m, to_up, 1, 1, z, b).wait_send()
                z_copy(m, to_up, 2, part, owner, b).wait_send()
    for copy in list(kv_copies.values()) + list(wide_copies.values()):
        copy.wait_send()

    hand_end()


def finish_kernel(*refs):
    sources, targets, held, sem_in, sem_out = refs[:3], refs[3:6], refs[6:9], refs[9], refs[10]
    incoming, outgoing = [], []
    for k, (source, target, buffer) in enumerate(zip(sources, targets, held)):
        rows = ROWS // PIECES
        for lead in range(source.shape[0]):
            for p in range(PIECES):
                middle = (0,) * (len(source.shape) - 3)
                at = (lead,) + middle + (pl.ds(p * rows, rows),)
                n = len(incoming)
                incoming.append(
                    pltpu.make_async_copy(source.at[at], buffer.at[at], sem_in.at[n])
                )
                outgoing.append(
                    pltpu.make_async_copy(buffer.at[at], target.at[at], sem_out.at[n])
                )
    for copy in incoming:
        copy.start()
    for copy, later in zip(incoming, outgoing):
        copy.wait()
        later.start()
    for copy in outgoing:
        copy.wait()


def finish(*arrays):
    whole = pl.BlockSpec(memory_space=pl.ANY)
    return pl.pallas_call(
        finish_kernel,
        out_shape=tuple(jax.ShapeDtypeStruct(a.shape, a.dtype) for a in arrays),
        in_specs=[whole] * 3,
        out_specs=(whole,) * 3,
        scratch_shapes=[pltpu.VMEM(a.shape, a.dtype) for a in arrays]
        + [pltpu.SemaphoreType.DMA((4 * PIECES,)), pltpu.SemaphoreType.DMA((4 * PIECES,))],
        name="finish",
    )(*arrays)


def on_device(queries, keys, values, grad_a, grad_b, imports, block_ids):
    wide = pltpu.VMEM((NY, ROWS, WIDE), BF16)
    pair = pltpu.VMEM((NZ, 2, NY, ROWS, HEAD), BF16)
    column = lambda n: pltpu.VMEM((n, NY, ROWS, HEAD), BF16)
    dma = lambda n: pltpu.SemaphoreType.DMA((n,))
    chunk = pltpu.VMEM((CHUNKS, 2 * ROWS, WIDE), F32)
    rows = pltpu.VMEM((WIDE, HEAD), BF16)
    whole = pl.BlockSpec(memory_space=pl.ANY)
    smem = pl.BlockSpec(memory_space=pltpu.SMEM)
    outputs = pl.pallas_call(
        step_kernel,
        out_shape=(
            jax.ShapeDtypeStruct(grad_a.shape, BF16),
            jax.ShapeDtypeStruct(grad_b.shape, BF16),
            jax.ShapeDtypeStruct((2, 1, ROWS, 2 * KEY_VALUE_HEADS * HEAD), BF16),
        ),
        in_specs=[whole] * 5 + [smem, smem],
        out_specs=(whole,) * 3,
        scratch_shapes=[
            wide, wide, wide, wide, pair, pair, wide, pltpu.VMEM((HALF, WIDE), BF16),
            wide, wide, pair, pair,
            column(2), column(2), column(2), column(2), column(2), column(2), column(4), column(4),
            chunk, chunk, pltpu.VMEM((NY * LISTED + 1, 2, ROWS, HEAD), F32), rows, rows,
            pltpu.SMEM((2 * NY * LISTED,), jnp.int32),
            pltpu.SMEM((2 * NY * BLOCKS,), jnp.int32),
            pltpu.SMEM((2 * NY,), jnp.int32),
            dma(12), dma(12), dma(12), dma(12), dma(48), dma(48), dma(8),
            dma(9), dma(8), dma(1), dma(8), dma(8), dma(8), dma(8), dma(16), dma(16), dma(16), dma(16), dma(6),
        ],
        compiler_params=pltpu.CompilerParams(
            collective_id=0, has_side_effects=True, vmem_limit_bytes=60 * 1024 * 1024
        ),
        name="step",
    )(queries, keys, values, grad_a, grad_b, imports, block_ids)
    return finish(*outputs)


def solution(mesh):
    return jax.shard_map(
        on_device,
        mesh=mesh,
        in_specs=(
            P(None, "pipe", "ctx", None),
            P(None, "pipe", "ctx", None),
            P(None, "pipe", "ctx", None),
            P("pipe", "ctx", None),
            P("pipe", "ctx", None),
            P(None, "pipe", None, None),
            P(None, "pipe", None),
        ),
        out_specs=(P("pipe", "ctx", None), P("pipe", "ctx", None), P(None, "pipe", "ctx", None)),
        check_vma=False,
    )
```

```python
import math

import jax
import jax.numpy as jnp
from jax import lax
from jax.experimental import pallas as pl
from jax.experimental.pallas import tpu as pltpu
from jax.sharding import PartitionSpec as P

KEY_VALUE_HEADS = 4
HEAD = 128
GROUP = 5
WIDE = GROUP * HEAD
ROWS = 128
HALF = ROWS // 2
NY = 4
NZ = 4
BLOCKS = NY * NZ
LISTED = 8
CHUNKS = LISTED // 2
FORWARD_AT = 2
RELAY_AT = 1
SCALE = 1.0 / math.sqrt(HEAD)
EXP2_SCALE = SCALE * math.log2(math.e)
NEG = -1e30
MESH = pl.DeviceIdType.MESH
BF16 = jnp.bfloat16
F32 = jnp.float32


def place():
    ctx = lax.axis_index("ctx")
    return ctx // NZ, ctx % NZ


def at_ctx(y, z):
    return {"ctx": lax.rem(y, NY) * NZ + lax.rem(z, NZ)}


def cols(index, width):
    return pl.ds(pl.multiple_of(index * width, width), width)


def remote(src, dst, send, recv, peer):
    return pltpu.make_async_remote_copy(
        src_ref=src, dst_ref=dst, send_sem=send, recv_sem=recv, device_id=peer, device_id_type=MESH
    )


def nt_dot(a, b):
    return lax.dot_general(a, b, (((1,), (1,)), ((), ())), preferred_element_type=F32)


def list_blocks(micro, z, imports, ids, slots, where_part, counts):
    for i in range(NY):
        mine = i * NZ + z
        block = ids[micro, 0, mine]

        def note(j, carry):
            count, found = carry[0], carry[1:]
            seen = imports[micro, 0, block, ids[micro, 0, j]]
            live = (seen == 1) & (j != mine)
            found = tuple(
                jnp.where(live & (count == p + 1), j, slot) for p, slot in enumerate(found)
            )
            position = jnp.where(live, i * LISTED + count, NY * LISTED)
            where_part[(micro * NY + i) * BLOCKS + j] = jnp.where(
                j == mine, i * LISTED, position
            )
            return (count + jnp.where(live, 1, 0),) + found

        start = (jnp.int32(1),) + (jnp.int32(0),) * (LISTED - 1)
        carry = lax.fori_loop(0, BLOCKS, note, start)
        base = (micro * NY + i) * LISTED
        counts[micro * NY + i] = carry[0]
        slots[base] = mine
        for p in range(LISTED - 1):
            slots[base + p + 1] = carry[p + 1]


def attend_block(micro, i, key_place, row_place, slots, counts, kv, q_rows, up_rows, scores,
                 grads, parts, dq_u):
    base = (micro * NY + i) * LISTED
    count = counts[micro * NY + i]

    def load(part, c):
        a, b = slots[base + 2 * c], slots[base + 2 * c + 1]
        return jnp.concatenate(
            [kv[lax.rem(a, NZ), part, a // NZ], kv[lax.rem(b, NZ), part, b // NZ]], axis=0
        )

    row_max = jnp.full((1, WIDE), NEG, F32)
    for c in range(CHUNKS):
        s = nt_dot(load(0, c), q_rows[...]) * EXP2_SCALE
        if c == 0:
            top = jnp.where(key_place <= row_place, s[:ROWS], NEG)
        else:
            top = s[:ROWS] + jnp.where(2 * c < count, 0.0, NEG)
        bottom = s[ROWS:] + jnp.where(2 * c + 1 < count, 0.0, NEG)
        scores[c, :ROWS] = top
        scores[c, ROWS:] = bottom
        grads[c] = nt_dot(load(1, c), up_rows[...])
        row_max = jnp.maximum(row_max, jnp.max(jnp.maximum(top, bottom), axis=0, keepdims=True))
    row_sum = jnp.zeros((1, WIDE), F32)
    inner = jnp.zeros((1, WIDE), F32)
    for c in range(CHUNKS):
        p = jnp.exp2(scores[c] - row_max)
        scores[c] = p
        row_sum = row_sum + jnp.sum(p, axis=0, keepdims=True)
        inner = inner + jnp.sum(p * grads[c], axis=0, keepdims=True)
    inverse = 1.0 / row_sum
    delta = inner * inverse
    dq_t = jnp.zeros((HEAD, WIDE), F32)
    for c in range(CHUNKS):
        probs = scores[c] * inverse
        score_grad = (probs * (grads[c] - delta)).astype(BF16)
        dv = jnp.dot(probs.astype(BF16), up_rows[...], preferred_element_type=F32)
        dk = jnp.dot(score_grad, q_rows[...], preferred_element_type=F32) * SCALE
        for half in range(2):
            span = slice(half * ROWS, (half + 1) * ROWS)
            parts[i * LISTED + 2 * c + half, 0] = dk[span]
            parts[i * LISTED + 2 * c + half, 1] = dv[span]
        dq_t = dq_t + lax.dot_general(
            load(0, c), score_grad, (((0,), (0,)), ((), ())), preferred_element_type=F32
        )
    dq_t = dq_t * SCALE
    for g in range(GROUP):
        span = slice(g * HEAD, (g + 1) * HEAD)
        dq_u[i, :, span] = dq_t[:, span].T.astype(BF16)


def step_kernel(
    queries, keys, values, grad_a, grad_b, imports, ids,
    dq_out_a, dq_out_b, kv_out,
    q_a, q_b, up_a, up_b, kv_a, kv_b, arrived, passing, dq_u_a, dq_u_b, dkv_a, dkv_b,
    relay_a, relay_b, landed_a, landed_b, summed_a, summed_b, total_a, total_b,
    scores, grads, parts, q_rows, up_rows,
    slots, where_part, counts,
    wide_send, wide_recv, kv_send, kv_recv, z_send, z_recv, local_in,
    hand_send, hand_recv, pass_recv, dq_send, dq_recv, r_send, r_recv, s_send, s_recv, o_send, o_recv, local_out,
):
    y, z = place()
    pipe = lax.axis_index("pipe")
    last = lax.axis_size("pipe") - 1
    edge = (last + 1) // 2
    spread_hand = edge == 2 * NY
    up, down = at_ctx(y, z + 1), at_ctx(y, z + NZ - 1)
    before, after = lax.rem(z + NZ - 1, NZ), lax.rem(z + 1, NZ)
    across = lax.rem(z + 2, NZ)
    kvs = (kv_a, kv_b)
    wide_src = (queries.at[0, 0], grad_a.at[0], queries.at[1, 0], grad_b.at[0])
    wide_dst = (q_a, up_a, q_b, up_b)
    kv_copies, kv_own, wide_copies, wide_own = {}, {}, {}, {}
    for m in range(2):
        for part, source in enumerate((keys, values)):
            kv_own[m, part] = pltpu.make_async_copy(
                source.at[m, 0, :, cols(y, HEAD)], kvs[m].at[z, part, y],
                local_in.at[2 * m + part],
            )
            kv_own[m, part].start()
    for w in range(4):
        wide_own[w] = pltpu.make_async_copy(
            wide_src[w].at[:, cols(y, WIDE)], wide_dst[w].at[y], local_in.at[4 + w]
        )
        wide_own[w].start()

    def z_copy(m, to_up, index, part, owner, piece):
        ref = kvs[m].at[owner, part, piece]
        where = ((m * 2 + to_up) * 3 + index) * NY + piece
        return remote(ref, ref, z_send.at[where], z_recv.at[where], up if to_up else down)

    def spread_piece(m, piece):
        for to_up, part in ((1, 0), (0, 1), (1, 1), (0, 0)):
            z_copy(m, to_up, part, part, z, piece).start()

    barrier = pltpu.get_barrier_semaphore()
    peers = [at_ctx(y + d, z) for d in range(1, NY)] + [up, down]
    for peer in peers:
        pl.semaphore_signal(barrier, inc=1, device_id=peer, device_id_type=MESH)

    @pl.when(pipe < last)
    def _():
        pl.semaphore_signal(barrier, inc=1, device_id={"pipe": pipe + 1}, device_id_type=MESH)

    callers = len(peers) + jnp.where(pipe > 0, 1, 0)
    if spread_hand:
        @pl.when(pipe == edge - 1)
        def _():
            for r in range(1, edge):
                pl.semaphore_signal(
                    barrier, inc=1, device_id={"pipe": edge + r}, device_id_type=MESH
                )

        @pl.when(pipe > edge)
        def _():
            pl.semaphore_signal(barrier, inc=1, device_id={"pipe": edge}, device_id_type=MESH)

        callers = callers + jnp.where(pipe > edge, 1, 0) + jnp.where(pipe == edge, edge - 1, 0)
    pl.semaphore_wait(barrier, callers)

    def start_kv(m):
        for d in range(1, NY):
            there = lax.rem(y + d, NY)
            for part, source in enumerate((keys, values)):
                index = (m * 2 + part) * 3 + d - 1
                kv_copies[m, part, d] = remote(
                    source.at[m, 0, :, cols(there, HEAD)], kvs[m].at[z, part, y],
                    kv_send.at[index], kv_recv.at[index], at_ctx(y + d, z),
                )
                kv_copies[m, part, d].start()

    def start_wide(w):
        for d in range(1, NY):
            there = lax.rem(y + d, NY)
            index = w * 3 + d - 1
            wide_copies[w, d] = remote(
                wide_src[w].at[:, cols(there, WIDE)], wide_dst[w].at[y],
                wide_send.at[index], wide_recv.at[index], at_ctx(y + d, z),
            )
            wide_copies[w, d].start()

    start_kv(0)
    for part in range(2):
        kv_own[0, part].wait()
    spread_piece(0, y)
    start_kv(1)
    start_wide(0)
    start_wide(1)
    start_wide(2)
    start_wide(3)

    def spread(m):
        for d in (1, 3, 2):
            for part in range(2):
                kv_copies[m, part, NY - d].wait_recv()
            spread_piece(m, lax.rem(y + d, NY))

    def forward(m, order=(0, 1, 3, 2)):
        for d in order:
            piece = lax.rem(y + d, NY)
            for to_up, part, owner in ((1, 0, before), (0, 1, after)):
                z_copy(m, to_up, part, part, z, piece).wait_recv()
                z_copy(m, to_up, 2, part, owner, piece).start()

    def wait_spread(m):
        for b in range(NY):
            z_copy(m, 1, 1, 1, z, b).wait_recv()
            z_copy(m, 0, 0, 0, z, b).wait_recv()
            z_copy(m, 1, 2, 0, across, b).wait_recv()
            z_copy(m, 0, 2, 1, across, b).wait_recv()
        for w in (2 * m, 2 * m + 1):
            wide_own[w].wait()
            for d in range(1, NY):
                wide_copies[w, d].wait_recv()

    def hand(i, h):
        span = pl.ds(h * HALF, HALF)
        return remote(
            dq_u_a.at[i, span], arrived.at[i, span], hand_send.at[2 * i + h],
            hand_recv.at[2 * i + h], {"pipe": lax.rem(pipe + last, last + 1)},
        )

    def to_relay(i, h):
        return remote(
            dq_u_a.at[i, pl.ds(h * HALF, HALF)], passing, hand_send.at[2 * i + h],
            pass_recv.at[0], {"pipe": lax.rem(edge + lax.rem(2 + 2 * i + h, edge), last + 1)},
        )

    piece = lax.rem(pipe + 2 * edge - 2, 2 * NY)

    def from_relay():
        i, h = piece // 2, lax.rem(piece, 2)
        return remote(
            passing, arrived.at[i, pl.ds(pl.multiple_of(h * HALF, HALF), HALF)],
            hand_send.at[2 * NY], hand_recv.at[piece], {"pipe": edge - 1},
        )

    def hand_over(i):
        direct = (pipe > 0) & (pipe != edge) if spread_hand else pipe > 0

        @pl.when(direct)
        def _():
            hand(i, 0).start()
            hand(i, 1).start()

        if spread_hand:
            @pl.when(pipe == edge)
            def _():
                @pl.when(i < NY - 1)
                def _():
                    to_relay(i, 0).start()

                @pl.when(i == NY - 1)
                def _():
                    hand(i, 0).start()

                to_relay(i, 1).start()

    def pass_on(i):
        if spread_hand:
            @pl.when((pipe > edge) & (piece // 2 + 1 == i))
            def _():
                to_relay(0, 0).wait_recv()
                from_relay().start()

    def hand_end():
        direct = (pipe > 0) & (pipe <= edge) if spread_hand else pipe > 0

        @pl.when(direct)
        def _():
            for i in range(NY):
                hand(i, 0).wait_send()
                hand(i, 1).wait_send()

        if spread_hand:
            @pl.when(pipe > edge)
            def _():
                for i in range(NY):
                    hand(i, 0).wait_send()
                    hand(i, 1).wait_send()
                from_relay().wait_send()

    def dq_copy(m, sender, target):
        return remote(
            (dq_u_a, dq_u_b)[m].at[target],
            (dq_out_a, dq_out_b)[m].at[0, :, cols(sender, WIDE)],
            dq_send.at[m * NY + target], dq_recv.at[m * NY + sender], at_ctx(target, z),
        )

    def dq_own(m):
        return pltpu.make_async_copy(
            (dq_u_a, dq_u_b)[m].at[y], (dq_out_a, dq_out_b)[m].at[0, :, cols(y, WIDE)],
            local_out.at[m],
        )

    def return_dq(m, i):
        @pl.when(i == y)
        def _():
            dq_own(m).start()

        @pl.when(i != y)
        def _():
            dq_copy(m, y, i).start()

    def combine(m, dkv):
        def one(slot, nothing):
            places = [where_part[(m * NY + i) * BLOCKS + slot] for i in range(NY)]
            for part in range(2):
                value = parts[places[0], part]
                for at in places[1:]:
                    value = value + parts[at, part]
                dkv[lax.rem(slot, NZ), part, slot // NZ] = value.astype(BF16)
            return nothing

        lax.fori_loop(0, BLOCKS, one, 0)

    relays, landeds, totals, dkvs = (
        (relay_a, relay_b), (landed_a, landed_b), (total_a, total_b), (dkv_a, dkv_b),
    )

    def r_copy(m, index):
        relay, landed, dkv = relays[m], landeds[m], dkvs[m]
        src, dst, peer = (
            (dkv.at[across, 0], relay.at[0], up),
            (dkv.at[across, 1], relay.at[1], down),
            (dkv.at[after, 1], landed.at[0], up),
            (dkv.at[before, 0], landed.at[1], down),
        )[index]
        return remote(src, dst, r_send.at[m * 4 + index], r_recv.at[m * 4 + index], peer)

    def s_copy(m, part, turn):
        where = (m * 2 + part) * NY + turn
        return remote(
            totals[m].at[part, turn], (summed_a, summed_b)[m].at[part, turn],
            s_send.at[where], s_recv.at[where], (up, down)[part],
        )

    def reduce_start(m):
        for index in range(4):
            r_copy(m, index).start()

    def reduce_relay(m):
        relay, total, dkv = relays[m], totals[m], dkvs[m]
        r_copy(m, 0).wait_recv()
        r_copy(m, 1).wait_recv()
        for turn, d in enumerate((2, 1, 3, 0)):
            piece = lax.rem(y + d, NY)
            for part, owner in ((0, after), (1, before)):
                total[part, turn] = (
                    relay[part, piece].astype(F32) + dkv[owner, part, piece].astype(F32)
                ).astype(BF16)
                s_copy(m, part, turn).start()

    def o_copy(m, part, sender, target, turn=0):
        return remote(
            totals[m].at[2 + part, turn],
            kv_out.at[m, 0, :, cols(KEY_VALUE_HEADS * part + sender, HEAD)],
            o_send.at[(m * 2 + part) * NY + target], o_recv.at[(m * 2 + part) * NY + sender],
            at_ctx(target, z),
        )

    def o_own(m, part):
        return pltpu.make_async_copy(
            totals[m].at[2 + part, NY - 1],
            kv_out.at[m, 0, :, cols(KEY_VALUE_HEADS * part + y, HEAD)],
            local_out.at[2 + 2 * m + part],
        )

    def reduce_end(m):
        landed, total, dkv, summed = landeds[m], totals[m], dkvs[m], (summed_a, summed_b)[m]
        r_copy(m, 2).wait_recv()
        r_copy(m, 3).wait_recv()
        for turn, d in enumerate((2, 1, 3, 0)):
            piece = lax.rem(y + d, NY)
            for part in range(2):
                s_copy(m, part, turn).wait_recv()
                total[2 + part, turn] = (
                    dkv[z, part, piece].astype(F32)
                    + landed[1 - part, piece].astype(F32)
                    + summed[part, turn].astype(F32)
                ).astype(BF16)
                if d:
                    o_copy(m, part, y, piece, turn).start()
                else:
                    o_own(m, part).start()

    key_place = lax.broadcasted_iota(jnp.int32, (ROWS, WIDE), 0)
    row_place = lax.rem(lax.broadcasted_iota(jnp.int32, (ROWS, WIDE), 1), ROWS)
    parts[NY * LISTED] = jnp.zeros_like(parts[NY * LISTED])
    spread(0)
    list_blocks(0, z, imports, ids, slots, where_part, counts)
    forward(0)
    for part in range(2):
        kv_own[1, part].wait()
    spread_piece(1, y)
    spread(1)
    list_blocks(1, z, imports, ids, slots, where_part, counts)
    wait_spread(0)

    def turn_a(i, nothing):
        for g in range(GROUP):
            span = slice(g * HEAD, (g + 1) * HEAD)
            q_rows[span, :] = q_a[i, :, span]
            up_rows[span, :] = up_a[i, :, span]
        attend_block(0, i, key_place, row_place, slots, counts, kv_a, q_rows, up_rows, scores,
                     grads, parts, dq_u_a)

        hand_over(i)
        return_dq(0, i)
        pass_on(i)

        @pl.when(i == FORWARD_AT - 1)
        def _():
            forward(1, (0, 1))

        @pl.when(i == FORWARD_AT)
        def _():
            forward(1, (3, 2))

        return nothing

    lax.fori_loop(0, NY, turn_a, 0)
    combine(0, dkv_a)
    pass_on(NY)
    reduce_start(0)
    wait_spread(1)

    def turn_b(i, nothing):
        @pl.when(pipe < last)
        def _():
            hand(i, 0).wait_recv()
            hand(i, 1).wait_recv()

        for g in range(GROUP):
            span = slice(g * HEAD, (g + 1) * HEAD)
            q_rows[span, :] = q_b[i, :, span]
            came = jnp.where(pipe < last, arrived[i, :, span].astype(F32), 0.0)
            up_rows[span, :] = (up_b[i, :, span].astype(F32) + came).astype(BF16)
        attend_block(1, i, key_place, row_place, slots, counts, kv_b, q_rows, up_rows, scores,
                     grads, parts, dq_u_b)
        return_dq(1, i)

        @pl.when(i == RELAY_AT)
        def _():
            reduce_relay(0)

        return nothing

    lax.fori_loop(0, NY, turn_b, 0)
    combine(1, dkv_b)
    reduce_start(1)
    reduce_end(0)
    reduce_relay(1)
    reduce_end(1)

    for m in range(2):
        dq_own(m).wait()
        for d in range(1, NY):
            other = lax.rem(y + d, NY)
            dq_copy(m, other, y).wait_recv()
            dq_copy(m, y, other).wait_send()
            for part in range(2):
                o_copy(m, part, other, y).wait_recv()
                o_copy(m, part, y, other).wait_send()
        for part in range(2):
            o_own(m, part).wait()
        for index in range(4):
            r_copy(m, index).wait_send()
        for b in range(NY):
            for part in range(2):
                s_copy(m, part, b).wait_send()
            for to_up, part, owner in ((1, 0, before), (0, 1, after)):
                z_copy(m, to_up, 0, 0, z, b).wait_send()
                z_copy(m, to_up, 1, 1, z, b).wait_send()
                z_copy(m, to_up, 2, part, owner, b).wait_send()
    for copy in list(kv_copies.values()) + list(wide_copies.values()):
        copy.wait_send()

    hand_end()


def on_device(queries, keys, values, grad_a, grad_b, imports, block_ids):
    wide = pltpu.VMEM((NY, ROWS, WIDE), BF16)
    pair = pltpu.VMEM((NZ, 2, NY, ROWS, HEAD), BF16)
    column = lambda n: pltpu.VMEM((n, NY, ROWS, HEAD), BF16)
    dma = lambda n: pltpu.SemaphoreType.DMA((n,))
    chunk = pltpu.VMEM((CHUNKS, 2 * ROWS, WIDE), F32)
    rows = pltpu.VMEM((WIDE, HEAD), BF16)
    whole = pl.BlockSpec(memory_space=pl.ANY)
    smem = pl.BlockSpec(memory_space=pltpu.SMEM)
    return pl.pallas_call(
        step_kernel,
        out_shape=(
            jax.ShapeDtypeStruct(grad_a.shape, BF16),
            jax.ShapeDtypeStruct(grad_b.shape, BF16),
            jax.ShapeDtypeStruct((2, 1, ROWS, 2 * KEY_VALUE_HEADS * HEAD), BF16),
        ),
        in_specs=[pl.BlockSpec(memory_space=pltpu.HBM)] * 5 + [smem, smem],
        out_specs=(whole,) * 3,
        scratch_shapes=[
            wide, wide, wide, wide, pair, pair, wide, pltpu.VMEM((HALF, WIDE), BF16),
            wide, wide, pair, pair,
            column(2), column(2), column(2), column(2), column(2), column(2), column(4), column(4),
            chunk, chunk, pltpu.VMEM((NY * LISTED + 1, 2, ROWS, HEAD), F32), rows, rows,
            pltpu.SMEM((2 * NY * LISTED,), jnp.int32),
            pltpu.SMEM((2 * NY * BLOCKS,), jnp.int32),
            pltpu.SMEM((2 * NY,), jnp.int32),
            dma(12), dma(12), dma(12), dma(12), dma(48), dma(48), dma(8),
            dma(9), dma(8), dma(1), dma(8), dma(8), dma(8), dma(8), dma(16), dma(16), dma(16), dma(16), dma(6),
        ],
        compiler_params=pltpu.CompilerParams(
            collective_id=0, has_side_effects=True, vmem_limit_bytes=40 * 1024 * 1024
        ),
        name="step",
    )(queries, keys, values, grad_a, grad_b, imports, block_ids)


def solution(mesh):
    return jax.shard_map(
        on_device,
        mesh=mesh,
        in_specs=(
            P(None, "pipe", "ctx", None),
            P(None, "pipe", "ctx", None),
            P(None, "pipe", "ctx", None),
            P("pipe", "ctx", None),
            P("pipe", "ctx", None),
            P(None, "pipe", None, None),
            P(None, "pipe", None),
        ),
        out_specs=(P("pipe", "ctx", None), P("pipe", "ctx", None), P(None, "pipe", "ctx", None)),
        check_vma=False,
    )
```

```python
import math

import jax
import jax.numpy as jnp
from jax import lax
from jax.experimental import pallas as pl
from jax.experimental.pallas import tpu as pltpu
from jax.sharding import PartitionSpec as P

KEY_VALUE_HEADS = 4
HEAD = 128
GROUP = 5
WIDE = GROUP * HEAD
ROWS = 128
HALF = ROWS // 2
NY = 4
NZ = 4
BLOCKS = NY * NZ
LISTED = 8
CHUNKS = LISTED // 2
FORWARD_AT = 2
RELAY_AT = 1
SCALE = 1.0 / math.sqrt(HEAD)
EXP2_SCALE = SCALE * math.log2(math.e)
NEG = -1e30
MESH = pl.DeviceIdType.MESH
BF16 = jnp.bfloat16
F32 = jnp.float32


def place():
    ctx = lax.axis_index("ctx")
    return ctx // NZ, ctx % NZ


def at_ctx(y, z):
    return {"ctx": lax.rem(y, NY) * NZ + lax.rem(z, NZ)}


def cols(index, width):
    return pl.ds(pl.multiple_of(index * width, width), width)


def remote(src, dst, send, recv, peer):
    return pltpu.make_async_remote_copy(
        src_ref=src, dst_ref=dst, send_sem=send, recv_sem=recv, device_id=peer, device_id_type=MESH
    )


def nt_dot(a, b):
    return lax.dot_general(a, b, (((1,), (1,)), ((), ())), preferred_element_type=F32)


def list_blocks(micro, z, imports, ids, slots, where_part, counts):
    for i in range(NY):
        mine = i * NZ + z
        block = ids[micro, 0, mine]

        def note(j, carry):
            count, found = carry[0], carry[1:]
            seen = imports[micro, 0, block, ids[micro, 0, j]]
            live = (seen == 1) & (j != mine)
            found = tuple(
                jnp.where(live & (count == p + 1), j, slot) for p, slot in enumerate(found)
            )
            position = jnp.where(live, i * LISTED + count, NY * LISTED)
            where_part[(micro * NY + i) * BLOCKS + j] = jnp.where(
                j == mine, i * LISTED, position
            )
            return (count + jnp.where(live, 1, 0),) + found

        start = (jnp.int32(1),) + (jnp.int32(0),) * (LISTED - 1)
        carry = lax.fori_loop(0, BLOCKS, note, start)
        base = (micro * NY + i) * LISTED
        counts[micro * NY + i] = carry[0]
        slots[base] = mine
        for p in range(LISTED - 1):
            slots[base + p + 1] = carry[p + 1]


def attend_block(micro, i, key_place, row_place, slots, counts, kv, q_rows, up_rows, scores,
                 grads, parts, dq_u):
    base = (micro * NY + i) * LISTED
    count = counts[micro * NY + i]

    def load(part, c):
        a, b = slots[base + 2 * c], slots[base + 2 * c + 1]
        return jnp.concatenate(
            [kv[lax.rem(a, NZ), part, a // NZ], kv[lax.rem(b, NZ), part, b // NZ]], axis=0
        )

    row_max = jnp.full((1, WIDE), NEG, F32)
    for c in range(CHUNKS):
        s = nt_dot(load(0, c), q_rows[...]) * EXP2_SCALE
        if c == 0:
            top = jnp.where(key_place <= row_place, s[:ROWS], NEG)
        else:
            top = s[:ROWS] + jnp.where(2 * c < count, 0.0, NEG)
        bottom = s[ROWS:] + jnp.where(2 * c + 1 < count, 0.0, NEG)
        scores[c, :ROWS] = top
        scores[c, ROWS:] = bottom
        grads[c] = nt_dot(load(1, c), up_rows[...])
        row_max = jnp.maximum(row_max, jnp.max(jnp.maximum(top, bottom), axis=0, keepdims=True))
    row_sum = jnp.zeros((1, WIDE), F32)
    inner = jnp.zeros((1, WIDE), F32)
    for c in range(CHUNKS):
        p = jnp.exp2(scores[c] - row_max)
        scores[c] = p
        row_sum = row_sum + jnp.sum(p, axis=0, keepdims=True)
        inner = inner + jnp.sum(p * grads[c], axis=0, keepdims=True)
    inverse = 1.0 / row_sum
    delta = inner * inverse
    dq_t = jnp.zeros((HEAD, WIDE), F32)
    for c in range(CHUNKS):
        probs = scores[c] * inverse
        score_grad = (probs * (grads[c] - delta)).astype(BF16)
        dv = jnp.dot(probs.astype(BF16), up_rows[...], preferred_element_type=F32)
        dk = jnp.dot(score_grad, q_rows[...], preferred_element_type=F32) * SCALE
        for half in range(2):
            span = slice(half * ROWS, (half + 1) * ROWS)
            parts[i * LISTED + 2 * c + half, 0] = dk[span]
            parts[i * LISTED + 2 * c + half, 1] = dv[span]
        dq_t = dq_t + lax.dot_general(
            load(0, c), score_grad, (((0,), (0,)), ((), ())), preferred_element_type=F32
        )
    dq_t = dq_t * SCALE
    for g in range(GROUP):
        span = slice(g * HEAD, (g + 1) * HEAD)
        dq_u[i, :, span] = dq_t[:, span].T.astype(BF16)


def step_kernel(
    queries, keys, values, grad_a, grad_b, imports, ids,
    dq_out_a, dq_out_b, kv_out,
    q_a, q_b, up_a, up_b, kv_a, kv_b, arrived, passing, dq_u_a, dq_u_b, dkv_a, dkv_b,
    relay_a, relay_b, landed_a, landed_b, summed_a, summed_b, total_a, total_b,
    scores, grads, parts, q_rows, up_rows,
    slots, where_part, counts,
    wide_send, wide_recv, kv_send, kv_recv, z_send, z_recv, local_in,
    hand_send, hand_recv, pass_recv, dq_send, dq_recv, r_send, r_recv, s_send, s_recv, o_send, o_recv, local_out,
):
    y, z = place()
    pipe = lax.axis_index("pipe")
    last = lax.axis_size("pipe") - 1
    edge = (last + 1) // 2
    spread_hand = edge == 2 * NY
    up, down = at_ctx(y, z + 1), at_ctx(y, z + NZ - 1)
    before, after = lax.rem(z + NZ - 1, NZ), lax.rem(z + 1, NZ)
    across = lax.rem(z + 2, NZ)
    kvs = (kv_a, kv_b)
    wide_src = (queries.at[0, 0], grad_a.at[0], queries.at[1, 0], grad_b.at[0])
    wide_dst = (q_a, up_a, q_b, up_b)
    kv_copies, kv_own, wide_copies, wide_own = {}, {}, {}, {}
    for m in range(2):
        for part, source in enumerate((keys, values)):
            kv_own[m, part] = pltpu.make_async_copy(
                source.at[m, 0, :, cols(y, HEAD)], kvs[m].at[z, part, y],
                local_in.at[2 * m + part],
            )
            kv_own[m, part].start()
    for w in range(4):
        wide_own[w] = pltpu.make_async_copy(
            wide_src[w].at[:, cols(y, WIDE)], wide_dst[w].at[y], local_in.at[4 + w]
        )
        wide_own[w].start()

    def z_copy(m, to_up, index, part, owner, piece):
        ref = kvs[m].at[owner, part, piece]
        where = ((m * 2 + to_up) * 3 + index) * NY + piece
        return remote(ref, ref, z_send.at[where], z_recv.at[where], up if to_up else down)

    def z_first(to_up, part):
        where = (to_up * 3 + part) * NY + y
        return remote(
            (keys, values)[part].at[0, 0, :, cols(y, HEAD)], kv_a.at[z, part, y],
            z_send.at[where], z_recv.at[where], up if to_up else down,
        )

    def spread_piece(m, piece):
        for to_up, part in ((1, 0), (0, 1), (1, 1), (0, 0)):
            z_copy(m, to_up, part, part, z, piece).start()

    barrier = pltpu.get_barrier_semaphore()
    peers = [at_ctx(y + d, z) for d in range(1, NY)] + [up, down]
    for peer in peers:
        pl.semaphore_signal(barrier, inc=1, device_id=peer, device_id_type=MESH)

    @pl.when(pipe < last)
    def _():
        pl.semaphore_signal(barrier, inc=1, device_id={"pipe": pipe + 1}, device_id_type=MESH)

    callers = len(peers) + jnp.where(pipe > 0, 1, 0)
    if spread_hand:
        @pl.when(pipe == edge - 1)
        def _():
            for r in range(1, edge):
                pl.semaphore_signal(
                    barrier, inc=1, device_id={"pipe": edge + r}, device_id_type=MESH
                )

        @pl.when(pipe > edge)
        def _():
            pl.semaphore_signal(barrier, inc=1, device_id={"pipe": edge}, device_id_type=MESH)

        callers = callers + jnp.where(pipe > edge, 1, 0) + jnp.where(pipe == edge, edge - 1, 0)
    pl.semaphore_wait(barrier, callers)

    def start_kv(m):
        for d in range(1, NY):
            there = lax.rem(y + d, NY)
            for part, source in enumerate((keys, values)):
                index = (m * 2 + part) * 3 + d - 1
                kv_copies[m, part, d] = remote(
                    source.at[m, 0, :, cols(there, HEAD)], kvs[m].at[z, part, y],
                    kv_send.at[index], kv_recv.at[index], at_ctx(y + d, z),
                )
                kv_copies[m, part, d].start()

    def start_wide(w):
        for d in range(1, NY):
            there = lax.rem(y + d, NY)
            index = w * 3 + d - 1
            wide_copies[w, d] = remote(
                wide_src[w].at[:, cols(there, WIDE)], wide_dst[w].at[y],
                wide_send.at[index], wide_recv.at[index], at_ctx(y + d, z),
            )
            wide_copies[w, d].start()

    for to_up, part in ((1, 0), (0, 1), (1, 1), (0, 0)):
        z_first(to_up, part).start()
    start_kv(0)
    start_kv(1)
    start_wide(0)
    start_wide(1)
    start_wide(2)
    start_wide(3)

    def spread(m):
        for d in (1, 3, 2):
            for part in range(2):
                kv_copies[m, part, NY - d].wait_recv()
            spread_piece(m, lax.rem(y + d, NY))

    def forward(m, order=(0, 1, 3, 2)):
        for d in order:
            piece = lax.rem(y + d, NY)
            for to_up, part, owner in ((1, 0, before), (0, 1, after)):
                z_copy(m, to_up, part, part, z, piece).wait_recv()
                z_copy(m, to_up, 2, part, owner, piece).start()

    def wait_spread(m):
        if m == 0:
            for part in range(2):
                kv_own[0, part].wait()
        for b in range(NY):
            z_copy(m, 1, 1, 1, z, b).wait_recv()
            z_copy(m, 0, 0, 0, z, b).wait_recv()
            z_copy(m, 1, 2, 0, across, b).wait_recv()
            z_copy(m, 0, 2, 1, across, b).wait_recv()
        for w in (2 * m, 2 * m + 1):
            wide_own[w].wait()
            for d in range(1, NY):
                wide_copies[w, d].wait_recv()

    def hand(i, h):
        span = pl.ds(h * HALF, HALF)
        return remote(
            dq_u_a.at[i, span], arrived.at[i, span], hand_send.at[2 * i + h],
            hand_recv.at[2 * i + h], {"pipe": lax.rem(pipe + last, last + 1)},
        )

    def to_relay(i, h):
        return remote(
            dq_u_a.at[i, pl.ds(h * HALF, HALF)], passing, hand_send.at[2 * i + h],
            pass_recv.at[0], {"pipe": lax.rem(edge + lax.rem(2 + 2 * i + h, edge), last + 1)},
        )

    piece = lax.rem(pipe + 2 * edge - 2, 2 * NY)

    def from_relay():
        i, h = piece // 2, lax.rem(piece, 2)
        return remote(
            passing, arrived.at[i, pl.ds(pl.multiple_of(h * HALF, HALF), HALF)],
            hand_send.at[2 * NY], hand_recv.at[piece], {"pipe": edge - 1},
        )

    def hand_over(i):
        direct = (pipe > 0) & (pipe != edge) if spread_hand else pipe > 0

        @pl.when(direct)
        def _():
            hand(i, 0).start()
            hand(i, 1).start()

        if spread_hand:
            @pl.when(pipe == edge)
            def _():
                @pl.when(i < NY - 1)
                def _():
                    to_relay(i, 0).start()

                @pl.when(i == NY - 1)
                def _():
                    hand(i, 0).start()

                to_relay(i, 1).start()

    def pass_on(i):
        if spread_hand:
            @pl.when((pipe > edge) & (piece // 2 + 1 == i))
            def _():
                to_relay(0, 0).wait_recv()
                from_relay().start()

    def hand_end():
        direct = (pipe > 0) & (pipe <= edge) if spread_hand else pipe > 0

        @pl.when(direct)
        def _():
            for i in range(NY):
                hand(i, 0).wait_send()
                hand(i, 1).wait_send()

        if spread_hand:
            @pl.when(pipe > edge)
            def _():
                for i in range(NY):
                    hand(i, 0).wait_send()
                    hand(i, 1).wait_send()
                from_relay().wait_send()

    def dq_copy(m, sender, target):
        return remote(
            (dq_u_a, dq_u_b)[m].at[target],
            (dq_out_a, dq_out_b)[m].at[0, :, cols(sender, WIDE)],
            dq_send.at[m * NY + target], dq_recv.at[m * NY + sender], at_ctx(target, z),
        )

    def dq_own(m):
        return pltpu.make_async_copy(
            (dq_u_a, dq_u_b)[m].at[y], (dq_out_a, dq_out_b)[m].at[0, :, cols(y, WIDE)],
            local_out.at[m],
        )

    def return_dq(m, i):
        @pl.when(i == y)
        def _():
            dq_own(m).start()

        @pl.when(i != y)
        def _():
            dq_copy(m, y, i).start()

    def combine(m, dkv):
        def one(slot, nothing):
            places = [where_part[(m * NY + i) * BLOCKS + slot] for i in range(NY)]
            for part in range(2):
                value = parts[places[0], part]
                for at in places[1:]:
                    value = value + parts[at, part]
                dkv[lax.rem(slot, NZ), part, slot // NZ] = value.astype(BF16)
            return nothing

        lax.fori_loop(0, BLOCKS, one, 0)

    relays, landeds, totals, dkvs = (
        (relay_a, relay_b), (landed_a, landed_b), (total_a, total_b), (dkv_a, dkv_b),
    )

    def r_copy(m, index):
        relay, landed, dkv = relays[m], landeds[m], dkvs[m]
        src, dst, peer = (
            (dkv.at[across, 0], relay.at[0], up),
            (dkv.at[across, 1], relay.at[1], down),
            (dkv.at[after, 1], landed.at[0], up),
            (dkv.at[before, 0], landed.at[1], down),
        )[index]
        return remote(src, dst, r_send.at[m * 4 + index], r_recv.at[m * 4 + index], peer)

    def s_copy(m, part, turn):
        where = (m * 2 + part) * NY + turn
        return remote(
            totals[m].at[part, turn], (summed_a, summed_b)[m].at[part, turn],
            s_send.at[where], s_recv.at[where], (up, down)[part],
        )

    def reduce_start(m):
        for index in range(4):
            r_copy(m, index).start()

    def reduce_relay(m):
        relay, total, dkv = relays[m], totals[m], dkvs[m]
        r_copy(m, 0).wait_recv()
        r_copy(m, 1).wait_recv()
        for turn, d in enumerate((2, 1, 3, 0)):
            piece = lax.rem(y + d, NY)
            for part, owner in ((0, after), (1, before)):
                total[part, turn] = (
                    relay[part, piece].astype(F32) + dkv[owner, part, piece].astype(F32)
                ).astype(BF16)
                s_copy(m, part, turn).start()

    def o_copy(m, part, sender, target, turn=0):
        return remote(
            totals[m].at[2 + part, turn],
            kv_out.at[m, 0, :, cols(KEY_VALUE_HEADS * part + sender, HEAD)],
            o_send.at[(m * 2 + part) * NY + target], o_recv.at[(m * 2 + part) * NY + sender],
            at_ctx(target, z),
        )

    def o_own(m, part):
        return pltpu.make_async_copy(
            totals[m].at[2 + part, NY - 1],
            kv_out.at[m, 0, :, cols(KEY_VALUE_HEADS * part + y, HEAD)],
            local_out.at[2 + 2 * m + part],
        )

    def reduce_end(m):
        landed, total, dkv, summed = landeds[m], totals[m], dkvs[m], (summed_a, summed_b)[m]
        r_copy(m, 2).wait_recv()
        r_copy(m, 3).wait_recv()
        for turn, d in enumerate((2, 1, 3, 0)):
            piece = lax.rem(y + d, NY)
            for part in range(2):
                s_copy(m, part, turn).wait_recv()
                total[2 + part, turn] = (
                    dkv[z, part, piece].astype(F32)
                    + landed[1 - part, piece].astype(F32)
                    + summed[part, turn].astype(F32)
                ).astype(BF16)
                if d:
                    o_copy(m, part, y, piece, turn).start()
                else:
                    o_own(m, part).start()

    key_place = lax.broadcasted_iota(jnp.int32, (ROWS, WIDE), 0)
    row_place = lax.rem(lax.broadcasted_iota(jnp.int32, (ROWS, WIDE), 1), ROWS)
    parts[NY * LISTED] = jnp.zeros_like(parts[NY * LISTED])
    spread(0)
    list_blocks(0, z, imports, ids, slots, where_part, counts)
    forward(0)
    for part in range(2):
        kv_own[1, part].wait()
    spread_piece(1, y)
    spread(1)
    list_blocks(1, z, imports, ids, slots, where_part, counts)
    wait_spread(0)

    def turn_a(i, nothing):
        for g in range(GROUP):
            span = slice(g * HEAD, (g + 1) * HEAD)
            q_rows[span, :] = q_a[i, :, span]
            up_rows[span, :] = up_a[i, :, span]
        attend_block(0, i, key_place, row_place, slots, counts, kv_a, q_rows, up_rows, scores,
                     grads, parts, dq_u_a)

        hand_over(i)
        return_dq(0, i)
        pass_on(i)

        @pl.when(i == FORWARD_AT - 1)
        def _():
            forward(1, (0, 1))

        @pl.when(i == FORWARD_AT)
        def _():
            forward(1, (3, 2))

        return nothing

    lax.fori_loop(0, NY, turn_a, 0)
    combine(0, dkv_a)
    pass_on(NY)
    reduce_start(0)
    wait_spread(1)

    def turn_b(i, nothing):
        @pl.when(pipe < last)
        def _():
            hand(i, 0).wait_recv()
            hand(i, 1).wait_recv()

        for g in range(GROUP):
            span = slice(g * HEAD, (g + 1) * HEAD)
            q_rows[span, :] = q_b[i, :, span]
            came = jnp.where(pipe < last, arrived[i, :, span].astype(F32), 0.0)
            up_rows[span, :] = (up_b[i, :, span].astype(F32) + came).astype(BF16)
        attend_block(1, i, key_place, row_place, slots, counts, kv_b, q_rows, up_rows, scores,
                     grads, parts, dq_u_b)
        return_dq(1, i)

        @pl.when(i == RELAY_AT)
        def _():
            reduce_relay(0)

        return nothing

    lax.fori_loop(0, NY, turn_b, 0)
    combine(1, dkv_b)
    reduce_start(1)
    reduce_end(0)
    reduce_relay(1)
    reduce_end(1)

    for m in range(2):
        dq_own(m).wait()
        for d in range(1, NY):
            other = lax.rem(y + d, NY)
            dq_copy(m, other, y).wait_recv()
            dq_copy(m, y, other).wait_send()
            for part in range(2):
                o_copy(m, part, other, y).wait_recv()
                o_copy(m, part, y, other).wait_send()
        for part in range(2):
            o_own(m, part).wait()
        for index in range(4):
            r_copy(m, index).wait_send()
        for b in range(NY):
            for part in range(2):
                s_copy(m, part, b).wait_send()
            for to_up, part, owner in ((1, 0, before), (0, 1, after)):
                z_copy(m, to_up, 0, 0, z, b).wait_send()
                z_copy(m, to_up, 1, 1, z, b).wait_send()
                z_copy(m, to_up, 2, part, owner, b).wait_send()
    for copy in list(kv_copies.values()) + list(wide_copies.values()):
        copy.wait_send()

    hand_end()


def finish_kernel(*refs):
    sources, targets, held, sem_in, sem_out = refs[:3], refs[3:6], refs[6:9], refs[9], refs[10]
    incoming = [
        pltpu.make_async_copy(source, buffer, sem_in.at[k])
        for k, (source, buffer) in enumerate(zip(sources, held))
    ]
    outgoing = [
        pltpu.make_async_copy(buffer, target, sem_out.at[k])
        for k, (buffer, target) in enumerate(zip(held, targets))
    ]
    for copy in incoming:
        copy.start()
    for copy, later in zip(incoming, outgoing):
        copy.wait()
        later.start()
    for copy in outgoing:
        copy.wait()


def finish(*arrays):
    whole = pl.BlockSpec(memory_space=pl.ANY)
    return pl.pallas_call(
        finish_kernel,
        out_shape=tuple(jax.ShapeDtypeStruct(a.shape, a.dtype) for a in arrays),
        in_specs=[whole] * 3,
        out_specs=(whole,) * 3,
        scratch_shapes=[pltpu.VMEM(a.shape, a.dtype) for a in arrays]
        + [pltpu.SemaphoreType.DMA((3,)), pltpu.SemaphoreType.DMA((3,))],
        name="finish",
    )(*arrays)


def on_device(queries, keys, values, grad_a, grad_b, imports, block_ids):
    wide = pltpu.VMEM((NY, ROWS, WIDE), BF16)
    pair = pltpu.VMEM((NZ, 2, NY, ROWS, HEAD), BF16)
    column = lambda n: pltpu.VMEM((n, NY, ROWS, HEAD), BF16)
    dma = lambda n: pltpu.SemaphoreType.DMA((n,))
    chunk = pltpu.VMEM((CHUNKS, 2 * ROWS, WIDE), F32)
    rows = pltpu.VMEM((WIDE, HEAD), BF16)
    whole = pl.BlockSpec(memory_space=pl.ANY)
    smem = pl.BlockSpec(memory_space=pltpu.SMEM)
    outputs = pl.pallas_call(
        step_kernel,
        out_shape=(
            jax.ShapeDtypeStruct(grad_a.shape, BF16),
            jax.ShapeDtypeStruct(grad_b.shape, BF16),
            jax.ShapeDtypeStruct((2, 1, ROWS, 2 * KEY_VALUE_HEADS * HEAD), BF16),
        ),
        in_specs=[whole] * 5 + [smem, smem],
        out_specs=(whole,) * 3,
        scratch_shapes=[
            wide, wide, wide, wide, pair, pair, wide, pltpu.VMEM((HALF, WIDE), BF16),
            wide, wide, pair, pair,
            column(2), column(2), column(2), column(2), column(2), column(2), column(4), column(4),
            chunk, chunk, pltpu.VMEM((NY * LISTED + 1, 2, ROWS, HEAD), F32), rows, rows,
            pltpu.SMEM((2 * NY * LISTED,), jnp.int32),
            pltpu.SMEM((2 * NY * BLOCKS,), jnp.int32),
            pltpu.SMEM((2 * NY,), jnp.int32),
            dma(12), dma(12), dma(12), dma(12), dma(48), dma(48), dma(8),
            dma(9), dma(8), dma(1), dma(8), dma(8), dma(8), dma(8), dma(16), dma(16), dma(16), dma(16), dma(6),
        ],
        compiler_params=pltpu.CompilerParams(
            collective_id=0, has_side_effects=True, vmem_limit_bytes=60 * 1024 * 1024
        ),
        name="step",
    )(queries, keys, values, grad_a, grad_b, imports, block_ids)
    return finish(*outputs)


def solution(mesh):
    return jax.shard_map(
        on_device,
        mesh=mesh,
        in_specs=(
            P(None, "pipe", "ctx", None),
            P(None, "pipe", "ctx", None),
            P(None, "pipe", "ctx", None),
            P("pipe", "ctx", None),
            P("pipe", "ctx", None),
            P(None, "pipe", None, None),
            P(None, "pipe", None),
        ),
        out_specs=(P("pipe", "ctx", None), P("pipe", "ctx", None), P(None, "pipe", "ctx", None)),
        check_vma=False,
    )
```

```python
import math

import jax
import jax.numpy as jnp
from jax import lax
from jax.experimental import pallas as pl
from jax.experimental.pallas import tpu as pltpu
from jax.sharding import PartitionSpec as P

KEY_VALUE_HEADS = 4
HEAD = 128
GROUP = 5
WIDE = GROUP * HEAD
ROWS = 128
HALF = ROWS // 2
NY = 4
NZ = 4
BLOCKS = NY * NZ
LISTED = 8
CHUNKS = LISTED // 2
FORWARD_AT = 2
RELAY_AT = 2
SCALE = 1.0 / math.sqrt(HEAD)
EXP2_SCALE = SCALE * math.log2(math.e)
NEG = -1e30
MESH = pl.DeviceIdType.MESH
BF16 = jnp.bfloat16
F32 = jnp.float32


def place():
    ctx = lax.axis_index("ctx")
    return ctx // NZ, ctx % NZ


def at_ctx(y, z):
    return {"ctx": lax.rem(y, NY) * NZ + lax.rem(z, NZ)}


def cols(index, width):
    return pl.ds(pl.multiple_of(index * width, width), width)


def remote(src, dst, send, recv, peer):
    return pltpu.make_async_remote_copy(
        src_ref=src, dst_ref=dst, send_sem=send, recv_sem=recv, device_id=peer, device_id_type=MESH
    )


def nt_dot(a, b):
    return lax.dot_general(a, b, (((1,), (1,)), ((), ())), preferred_element_type=F32)


def list_blocks(micro, z, imports, ids, slots, where_part, counts):
    for i in range(NY):
        mine = i * NZ + z
        block = ids[micro, 0, mine]

        def note(j, carry):
            count, found = carry[0], carry[1:]
            seen = imports[micro, 0, block, ids[micro, 0, j]]
            live = (seen == 1) & (j != mine)
            found = tuple(
                jnp.where(live & (count == p + 1), j, slot) for p, slot in enumerate(found)
            )
            position = jnp.where(live, i * LISTED + count, NY * LISTED)
            where_part[(micro * NY + i) * BLOCKS + j] = jnp.where(
                j == mine, i * LISTED, position
            )
            return (count + jnp.where(live, 1, 0),) + found

        start = (jnp.int32(1),) + (jnp.int32(0),) * (LISTED - 1)
        carry = lax.fori_loop(0, BLOCKS, note, start)
        base = (micro * NY + i) * LISTED
        counts[micro * NY + i] = carry[0]
        slots[base] = mine
        for p in range(LISTED - 1):
            slots[base + p + 1] = carry[p + 1]


def attend_block(micro, i, key_place, row_place, slots, counts, kv, q_rows, up_rows, scores,
                 grads, parts, dq_u):
    base = (micro * NY + i) * LISTED
    count = counts[micro * NY + i]

    def load(part, c):
        a, b = slots[base + 2 * c], slots[base + 2 * c + 1]
        return jnp.concatenate(
            [kv[lax.rem(a, NZ), part, a // NZ], kv[lax.rem(b, NZ), part, b // NZ]], axis=0
        )

    row_max = jnp.full((1, WIDE), NEG, F32)
    for c in range(CHUNKS):
        s = nt_dot(load(0, c), q_rows[...]) * EXP2_SCALE
        if c == 0:
            top = jnp.where(key_place <= row_place, s[:ROWS], NEG)
        else:
            top = s[:ROWS] + jnp.where(2 * c < count, 0.0, NEG)
        bottom = s[ROWS:] + jnp.where(2 * c + 1 < count, 0.0, NEG)
        scores[c, :ROWS] = top
        scores[c, ROWS:] = bottom
        grads[c] = nt_dot(load(1, c), up_rows[...])
        row_max = jnp.maximum(row_max, jnp.max(jnp.maximum(top, bottom), axis=0, keepdims=True))
    row_sum = jnp.zeros((1, WIDE), F32)
    inner = jnp.zeros((1, WIDE), F32)
    for c in range(CHUNKS):
        p = jnp.exp2(scores[c] - row_max)
        scores[c] = p
        row_sum = row_sum + jnp.sum(p, axis=0, keepdims=True)
        inner = inner + jnp.sum(p * grads[c], axis=0, keepdims=True)
    inverse = 1.0 / row_sum
    delta = inner * inverse
    dq_t = jnp.zeros((HEAD, WIDE), F32)
    for c in range(CHUNKS):
        probs = scores[c] * inverse
        score_grad = (probs * (grads[c] - delta)).astype(BF16)
        dv = jnp.dot(probs.astype(BF16), up_rows[...], preferred_element_type=F32)
        dk = jnp.dot(score_grad, q_rows[...], preferred_element_type=F32) * SCALE
        for half in range(2):
            span = slice(half * ROWS, (half + 1) * ROWS)
            parts[i * LISTED + 2 * c + half, 0] = dk[span]
            parts[i * LISTED + 2 * c + half, 1] = dv[span]
        dq_t = dq_t + lax.dot_general(
            load(0, c), score_grad, (((0,), (0,)), ((), ())), preferred_element_type=F32
        )
    dq_t = dq_t * SCALE
    for g in range(GROUP):
        span = slice(g * HEAD, (g + 1) * HEAD)
        dq_u[i, :, span] = dq_t[:, span].T.astype(BF16)


def step_kernel(
    queries, keys, values, grad_a, grad_b, imports, ids,
    dq_out_a, dq_out_b, kv_out,
    q_a, q_b, up_a, up_b, kv_a, kv_b, arrived, passing, dq_u_a, dq_u_b, dkv_a, dkv_b,
    relay_a, relay_b, landed_a, landed_b, summed_a, summed_b, total_a, total_b,
    scores, grads, parts, q_rows, up_rows,
    slots, where_part, counts,
    wide_send, wide_recv, kv_send, kv_recv, z_send, z_recv, local_in,
    hand_send, hand_recv, pass_recv, dq_send, dq_recv, r_send, r_recv, s_send, s_recv, o_send, o_recv, local_out,
):
    y, z = place()
    pipe = lax.axis_index("pipe")
    last = lax.axis_size("pipe") - 1
    edge = (last + 1) // 2
    spread_hand = edge == 2 * NY
    up, down = at_ctx(y, z + 1), at_ctx(y, z + NZ - 1)
    before, after = lax.rem(z + NZ - 1, NZ), lax.rem(z + 1, NZ)
    across = lax.rem(z + 2, NZ)
    kvs = (kv_a, kv_b)
    wide_src = (queries.at[0, 0], grad_a.at[0], queries.at[1, 0], grad_b.at[0])
    wide_dst = (q_a, up_a, q_b, up_b)
    kv_copies, kv_own, wide_copies, wide_own = {}, {}, {}, {}
    for m in range(2):
        for part, source in enumerate((keys, values)):
            kv_own[m, part] = pltpu.make_async_copy(
                source.at[m, 0, :, cols(y, HEAD)], kvs[m].at[z, part, y],
                local_in.at[2 * m + part],
            )
            kv_own[m, part].start()
    for w in range(4):
        wide_own[w] = pltpu.make_async_copy(
            wide_src[w].at[:, cols(y, WIDE)], wide_dst[w].at[y], local_in.at[4 + w]
        )
        wide_own[w].start()

    def z_copy(m, to_up, index, part, owner, piece):
        ref = kvs[m].at[owner, part, piece]
        where = ((m * 2 + to_up) * 3 + index) * NY + piece
        return remote(ref, ref, z_send.at[where], z_recv.at[where], up if to_up else down)

    def z_first(to_up, part):
        where = (to_up * 3 + part) * NY + y
        return remote(
            (keys, values)[part].at[0, 0, :, cols(y, HEAD)], kv_a.at[z, part, y],
            z_send.at[where], z_recv.at[where], up if to_up else down,
        )

    def spread_piece(m, piece):
        for to_up, part in ((1, 0), (0, 1), (1, 1), (0, 0)):
            z_copy(m, to_up, part, part, z, piece).start()

    barrier = pltpu.get_barrier_semaphore()
    peers = [at_ctx(y + d, z) for d in range(1, NY)] + [up, down]
    for peer in peers:
        pl.semaphore_signal(barrier, inc=1, device_id=peer, device_id_type=MESH)

    @pl.when(pipe < last)
    def _():
        pl.semaphore_signal(barrier, inc=1, device_id={"pipe": pipe + 1}, device_id_type=MESH)

    callers = len(peers) + jnp.where(pipe > 0, 1, 0)
    if spread_hand:
        @pl.when(pipe == edge - 1)
        def _():
            for r in range(1, edge):
                pl.semaphore_signal(
                    barrier, inc=1, device_id={"pipe": edge + r}, device_id_type=MESH
                )

        @pl.when(pipe > edge)
        def _():
            pl.semaphore_signal(barrier, inc=1, device_id={"pipe": edge}, device_id_type=MESH)

        callers = callers + jnp.where(pipe > edge, 1, 0) + jnp.where(pipe == edge, edge - 1, 0)
    pl.semaphore_wait(barrier, callers)

    def start_kv(m):
        for d in range(1, NY):
            there = lax.rem(y + d, NY)
            for part, source in enumerate((keys, values)):
                index = (m * 2 + part) * 3 + d - 1
                kv_copies[m, part, d] = remote(
                    source.at[m, 0, :, cols(there, HEAD)], kvs[m].at[z, part, y],
                    kv_send.at[index], kv_recv.at[index], at_ctx(y + d, z),
                )
                kv_copies[m, part, d].start()

    def start_wide(w):
        for d in range(1, NY):
            there = lax.rem(y + d, NY)
            index = w * 3 + d - 1
            wide_copies[w, d] = remote(
                wide_src[w].at[:, cols(there, WIDE)], wide_dst[w].at[y],
                wide_send.at[index], wide_recv.at[index], at_ctx(y + d, z),
            )
            wide_copies[w, d].start()

    for to_up, part in ((1, 0), (0, 1), (1, 1), (0, 0)):
        z_first(to_up, part).start()
    start_kv(0)
    start_kv(1)
    start_wide(0)
    start_wide(1)
    start_wide(2)
    start_wide(3)

    def spread(m):
        for d in (1, 3, 2):
            for part in range(2):
                kv_copies[m, part, NY - d].wait_recv()
            spread_piece(m, lax.rem(y + d, NY))

    def forward(m, order=(0, 1, 3, 2)):
        for d in order:
            piece = lax.rem(y + d, NY)
            for to_up, part, owner in ((1, 0, before), (0, 1, after)):
                z_copy(m, to_up, part, part, z, piece).wait_recv()
                z_copy(m, to_up, 2, part, owner, piece).start()

    def wait_spread(m):
        if m == 0:
            for part in range(2):
                kv_own[0, part].wait()
        for b in range(NY):
            z_copy(m, 1, 1, 1, z, b).wait_recv()
            z_copy(m, 0, 0, 0, z, b).wait_recv()
            z_copy(m, 1, 2, 0, across, b).wait_recv()
            z_copy(m, 0, 2, 1, across, b).wait_recv()
        for w in (2 * m, 2 * m + 1):
            wide_own[w].wait()
            for d in range(1, NY):
                wide_copies[w, d].wait_recv()

    def hand(i, h):
        span = pl.ds(h * HALF, HALF)
        return remote(
            dq_u_a.at[i, span], arrived.at[i, span], hand_send.at[2 * i + h],
            hand_recv.at[2 * i + h], {"pipe": lax.rem(pipe + last, last + 1)},
        )

    def to_relay(i, h):
        return remote(
            dq_u_a.at[i, pl.ds(h * HALF, HALF)], passing, hand_send.at[2 * i + h],
            pass_recv.at[0], {"pipe": lax.rem(edge + lax.rem(2 + 2 * i + h, edge), last + 1)},
        )

    piece = lax.rem(pipe + 2 * edge - 2, 2 * NY)

    def from_relay():
        i, h = piece // 2, lax.rem(piece, 2)
        return remote(
            passing, arrived.at[i, pl.ds(pl.multiple_of(h * HALF, HALF), HALF)],
            hand_send.at[2 * NY], hand_recv.at[piece], {"pipe": edge - 1},
        )

    def hand_over(i):
        direct = (pipe > 0) & (pipe != edge) if spread_hand else pipe > 0

        @pl.when(direct)
        def _():
            hand(i, 0).start()
            hand(i, 1).start()

        if spread_hand:
            @pl.when(pipe == edge)
            def _():
                @pl.when(i < NY - 1)
                def _():
                    to_relay(i, 0).start()

                @pl.when(i == NY - 1)
                def _():
                    hand(i, 0).start()

                to_relay(i, 1).start()

    def pass_on(i):
        if spread_hand:
            @pl.when((pipe > edge) & (piece // 2 + 1 == i))
            def _():
                to_relay(0, 0).wait_recv()
                from_relay().start()

    def hand_end():
        direct = (pipe > 0) & (pipe <= edge) if spread_hand else pipe > 0

        @pl.when(direct)
        def _():
            for i in range(NY):
                hand(i, 0).wait_send()
                hand(i, 1).wait_send()

        if spread_hand:
            @pl.when(pipe > edge)
            def _():
                for i in range(NY):
                    hand(i, 0).wait_send()
                    hand(i, 1).wait_send()
                from_relay().wait_send()

    def dq_copy(m, sender, target):
        return remote(
            (dq_u_a, dq_u_b)[m].at[target],
            (dq_out_a, dq_out_b)[m].at[0, :, cols(sender, WIDE)],
            dq_send.at[m * NY + target], dq_recv.at[m * NY + sender], at_ctx(target, z),
        )

    def dq_own(m):
        return pltpu.make_async_copy(
            (dq_u_a, dq_u_b)[m].at[y], (dq_out_a, dq_out_b)[m].at[0, :, cols(y, WIDE)],
            local_out.at[m],
        )

    def return_dq(m, i):
        @pl.when(i == y)
        def _():
            dq_own(m).start()

        @pl.when(i != y)
        def _():
            dq_copy(m, y, i).start()

    def combine(m, dkv):
        def one(slot, nothing):
            places = [where_part[(m * NY + i) * BLOCKS + slot] for i in range(NY)]
            for part in range(2):
                value = parts[places[0], part]
                for at in places[1:]:
                    value = value + parts[at, part]
                dkv[lax.rem(slot, NZ), part, slot // NZ] = value.astype(BF16)
            return nothing

        lax.fori_loop(0, BLOCKS, one, 0)

    relays, landeds, totals, dkvs = (
        (relay_a, relay_b), (landed_a, landed_b), (total_a, total_b), (dkv_a, dkv_b),
    )

    def r_copy(m, index):
        relay, landed, dkv = relays[m], landeds[m], dkvs[m]
        src, dst, peer = (
            (dkv.at[across, 0], relay.at[0], up),
            (dkv.at[across, 1], relay.at[1], down),
            (dkv.at[after, 1], landed.at[0], up),
            (dkv.at[before, 0], landed.at[1], down),
        )[index]
        return remote(src, dst, r_send.at[m * 4 + index], r_recv.at[m * 4 + index], peer)

    def s_copy(m, part, turn):
        where = (m * 2 + part) * NY + turn
        return remote(
            totals[m].at[part, turn], (summed_a, summed_b)[m].at[part, turn],
            s_send.at[where], s_recv.at[where], (up, down)[part],
        )

    def reduce_start(m):
        for index in range(4):
            r_copy(m, index).start()

    def reduce_relay(m):
        relay, total, dkv = relays[m], totals[m], dkvs[m]
        r_copy(m, 0).wait_recv()
        r_copy(m, 1).wait_recv()
        for turn, d in enumerate((2, 1, 3, 0)):
            piece = lax.rem(y + d, NY)
            for part, owner in ((0, after), (1, before)):
                total[part, turn] = (
                    relay[part, piece].astype(F32) + dkv[owner, part, piece].astype(F32)
                ).astype(BF16)
                s_copy(m, part, turn).start()

    def o_copy(m, part, sender, target, turn=0):
        return remote(
            totals[m].at[2 + part, turn],
            kv_out.at[m, 0, :, cols(KEY_VALUE_HEADS * part + sender, HEAD)],
            o_send.at[(m * 2 + part) * NY + target], o_recv.at[(m * 2 + part) * NY + sender],
            at_ctx(target, z),
        )

    def o_own(m, part):
        return pltpu.make_async_copy(
            totals[m].at[2 + part, NY - 1],
            kv_out.at[m, 0, :, cols(KEY_VALUE_HEADS * part + y, HEAD)],
            local_out.at[2 + 2 * m + part],
        )

    def reduce_end(m):
        landed, total, dkv, summed = landeds[m], totals[m], dkvs[m], (summed_a, summed_b)[m]
        r_copy(m, 2).wait_recv()
        r_copy(m, 3).wait_recv()
        for turn, d in enumerate((2, 1, 3, 0)):
            piece = lax.rem(y + d, NY)
            for part in range(2):
                s_copy(m, part, turn).wait_recv()
                total[2 + part, turn] = (
                    dkv[z, part, piece].astype(F32)
                    + landed[1 - part, piece].astype(F32)
                    + summed[part, turn].astype(F32)
                ).astype(BF16)
                if d:
                    o_copy(m, part, y, piece, turn).start()
                else:
                    o_own(m, part).start()

    key_place = lax.broadcasted_iota(jnp.int32, (ROWS, WIDE), 0)
    row_place = lax.rem(lax.broadcasted_iota(jnp.int32, (ROWS, WIDE), 1), ROWS)
    parts[NY * LISTED] = jnp.zeros_like(parts[NY * LISTED])
    spread(0)
    list_blocks(0, z, imports, ids, slots, where_part, counts)
    forward(0)
    for part in range(2):
        kv_own[1, part].wait()
    spread_piece(1, y)
    spread(1)
    list_blocks(1, z, imports, ids, slots, where_part, counts)
    wait_spread(0)

    def turn_a(i, nothing):
        for g in range(GROUP):
            span = slice(g * HEAD, (g + 1) * HEAD)
            q_rows[span, :] = q_a[i, :, span]
            up_rows[span, :] = up_a[i, :, span]
        attend_block(0, i, key_place, row_place, slots, counts, kv_a, q_rows, up_rows, scores,
                     grads, parts, dq_u_a)

        hand_over(i)
        return_dq(0, i)
        pass_on(i)

        @pl.when(i == FORWARD_AT - 1)
        def _():
            forward(1, (0, 1))

        @pl.when(i == FORWARD_AT)
        def _():
            forward(1, (3, 2))

        return nothing

    lax.fori_loop(0, NY, turn_a, 0)
    combine(0, dkv_a)
    pass_on(NY)
    reduce_start(0)
    wait_spread(1)

    def turn_b(i, nothing):
        @pl.when(pipe < last)
        def _():
            hand(i, 0).wait_recv()
            hand(i, 1).wait_recv()

        for g in range(GROUP):
            span = slice(g * HEAD, (g + 1) * HEAD)
            q_rows[span, :] = q_b[i, :, span]
            came = jnp.where(pipe < last, arrived[i, :, span].astype(F32), 0.0)
            up_rows[span, :] = (up_b[i, :, span].astype(F32) + came).astype(BF16)
        attend_block(1, i, key_place, row_place, slots, counts, kv_b, q_rows, up_rows, scores,
                     grads, parts, dq_u_b)
        return_dq(1, i)

        @pl.when(i == RELAY_AT)
        def _():
            reduce_relay(0)

        return nothing

    lax.fori_loop(0, NY, turn_b, 0)
    combine(1, dkv_b)
    reduce_start(1)
    reduce_end(0)
    reduce_relay(1)
    reduce_end(1)

    for m in range(2):
        dq_own(m).wait()
        for d in range(1, NY):
            other = lax.rem(y + d, NY)
            dq_copy(m, other, y).wait_recv()
            dq_copy(m, y, other).wait_send()
            for part in range(2):
                o_copy(m, part, other, y).wait_recv()
                o_copy(m, part, y, other).wait_send()
        for part in range(2):
            o_own(m, part).wait()
        for index in range(4):
            r_copy(m, index).wait_send()
        for b in range(NY):
            for part in range(2):
                s_copy(m, part, b).wait_send()
            for to_up, part, owner in ((1, 0, before), (0, 1, after)):
                z_copy(m, to_up, 0, 0, z, b).wait_send()
                z_copy(m, to_up, 1, 1, z, b).wait_send()
                z_copy(m, to_up, 2, part, owner, b).wait_send()
    for copy in list(kv_copies.values()) + list(wide_copies.values()):
        copy.wait_send()

    hand_end()


def finish_kernel(*refs):
    sources, targets, held, sem_in, sem_out = refs[:3], refs[3:6], refs[6:9], refs[9], refs[10]
    incoming = [
        pltpu.make_async_copy(source, buffer, sem_in.at[k])
        for k, (source, buffer) in enumerate(zip(sources, held))
    ]
    outgoing = [
        pltpu.make_async_copy(buffer, target, sem_out.at[k])
        for k, (buffer, target) in enumerate(zip(held, targets))
    ]
    for copy in incoming:
        copy.start()
    for copy, later in zip(incoming, outgoing):
        copy.wait()
        later.start()
    for copy in outgoing:
        copy.wait()


def finish(*arrays):
    whole = pl.BlockSpec(memory_space=pl.ANY)
    return pl.pallas_call(
        finish_kernel,
        out_shape=tuple(jax.ShapeDtypeStruct(a.shape, a.dtype) for a in arrays),
        in_specs=[whole] * 3,
        out_specs=(whole,) * 3,
        scratch_shapes=[pltpu.VMEM(a.shape, a.dtype) for a in arrays]
        + [pltpu.SemaphoreType.DMA((3,)), pltpu.SemaphoreType.DMA((3,))],
        name="finish",
    )(*arrays)


def on_device(queries, keys, values, grad_a, grad_b, imports, block_ids):
    wide = pltpu.VMEM((NY, ROWS, WIDE), BF16)
    pair = pltpu.VMEM((NZ, 2, NY, ROWS, HEAD), BF16)
    column = lambda n: pltpu.VMEM((n, NY, ROWS, HEAD), BF16)
    dma = lambda n: pltpu.SemaphoreType.DMA((n,))
    chunk = pltpu.VMEM((CHUNKS, 2 * ROWS, WIDE), F32)
    rows = pltpu.VMEM((WIDE, HEAD), BF16)
    whole = pl.BlockSpec(memory_space=pl.ANY)
    smem = pl.BlockSpec(memory_space=pltpu.SMEM)
    outputs = pl.pallas_call(
        step_kernel,
        out_shape=(
            jax.ShapeDtypeStruct(grad_a.shape, BF16),
            jax.ShapeDtypeStruct(grad_b.shape, BF16),
            jax.ShapeDtypeStruct((2, 1, ROWS, 2 * KEY_VALUE_HEADS * HEAD), BF16),
        ),
        in_specs=[whole] * 5 + [smem, smem],
        out_specs=(whole,) * 3,
        scratch_shapes=[
            wide, wide, wide, wide, pair, pair, wide, pltpu.VMEM((HALF, WIDE), BF16),
            wide, wide, pair, pair,
            column(2), column(2), column(2), column(2), column(2), column(2), column(4), column(4),
            chunk, chunk, pltpu.VMEM((NY * LISTED + 1, 2, ROWS, HEAD), F32), rows, rows,
            pltpu.SMEM((2 * NY * LISTED,), jnp.int32),
            pltpu.SMEM((2 * NY * BLOCKS,), jnp.int32),
            pltpu.SMEM((2 * NY,), jnp.int32),
            dma(12), dma(12), dma(12), dma(12), dma(48), dma(48), dma(8),
            dma(9), dma(8), dma(1), dma(8), dma(8), dma(8), dma(8), dma(16), dma(16), dma(16), dma(16), dma(6),
        ],
        compiler_params=pltpu.CompilerParams(
            collective_id=0, has_side_effects=True, vmem_limit_bytes=60 * 1024 * 1024
        ),
        name="step",
    )(queries, keys, values, grad_a, grad_b, imports, block_ids)
    return finish(*outputs)


def solution(mesh):
    return jax.shard_map(
        on_device,
        mesh=mesh,
        in_specs=(
            P(None, "pipe", "ctx", None),
            P(None, "pipe", "ctx", None),
            P(None, "pipe", "ctx", None),
            P("pipe", "ctx", None),
            P("pipe", "ctx", None),
            P(None, "pipe", None, None),
            P(None, "pipe", None),
        ),
        out_specs=(P("pipe", "ctx", None), P("pipe", "ctx", None), P(None, "pipe", "ctx", None)),
        check_vma=False,
    )
```

```python
import math

import jax
import jax.numpy as jnp
from jax import lax
from jax.experimental import pallas as pl
from jax.experimental.pallas import tpu as pltpu
from jax.sharding import PartitionSpec as P

KEY_VALUE_HEADS = 4
HEAD = 128
GROUP = 5
WIDE = GROUP * HEAD
ROWS = 128
HALF = ROWS // 2
NY = 4
NZ = 4
BLOCKS = NY * NZ
LISTED = 8
CHUNKS = LISTED // 2
FORWARD_AT = 2
RELAY_AT = 1
SCALE = 1.0 / math.sqrt(HEAD)
EXP2_SCALE = SCALE * math.log2(math.e)
NEG = -1e30
MESH = pl.DeviceIdType.MESH
BF16 = jnp.bfloat16
F32 = jnp.float32


def place():
    ctx = lax.axis_index("ctx")
    return ctx // NZ, ctx % NZ


def at_ctx(y, z):
    return {"ctx": lax.rem(y, NY) * NZ + lax.rem(z, NZ)}


def cols(index, width):
    return pl.ds(pl.multiple_of(index * width, width), width)


def remote(src, dst, send, recv, peer):
    return pltpu.make_async_remote_copy(
        src_ref=src, dst_ref=dst, send_sem=send, recv_sem=recv, device_id=peer, device_id_type=MESH
    )


def nt_dot(a, b):
    return lax.dot_general(a, b, (((1,), (1,)), ((), ())), preferred_element_type=F32)


def list_blocks(micro, z, imports, ids, slots, where_part, counts):
    for i in range(NY):
        mine = i * NZ + z
        block = ids[micro, 0, mine]

        def note(j, carry):
            count, found = carry[0], carry[1:]
            seen = imports[micro, 0, block, ids[micro, 0, j]]
            live = (seen == 1) & (j != mine)
            found = tuple(
                jnp.where(live & (count == p + 1), j, slot) for p, slot in enumerate(found)
            )
            position = jnp.where(live, i * LISTED + count, NY * LISTED)
            where_part[(micro * NY + i) * BLOCKS + j] = jnp.where(
                j == mine, i * LISTED, position
            )
            return (count + jnp.where(live, 1, 0),) + found

        start = (jnp.int32(1),) + (jnp.int32(0),) * (LISTED - 1)
        carry = lax.fori_loop(0, BLOCKS, note, start)
        base = (micro * NY + i) * LISTED
        counts[micro * NY + i] = carry[0]
        slots[base] = mine
        for p in range(LISTED - 1):
            slots[base + p + 1] = carry[p + 1]


def attend_block(micro, i, key_place, row_place, slots, counts, kv, q_rows, up_rows, scores,
                 grads, parts, dq_u):
    base = (micro * NY + i) * LISTED
    count = counts[micro * NY + i]

    def load(part, c):
        a, b = slots[base + 2 * c], slots[base + 2 * c + 1]
        return jnp.concatenate(
            [kv[lax.rem(a, NZ), part, a // NZ], kv[lax.rem(b, NZ), part, b // NZ]], axis=0
        )

    row_max = jnp.full((1, WIDE), NEG, F32)
    for c in range(CHUNKS):
        s = nt_dot(load(0, c), q_rows[...]) * EXP2_SCALE
        if c == 0:
            top = jnp.where(key_place <= row_place, s[:ROWS], NEG)
        else:
            top = s[:ROWS] + jnp.where(2 * c < count, 0.0, NEG)
        bottom = s[ROWS:] + jnp.where(2 * c + 1 < count, 0.0, NEG)
        scores[c, :ROWS] = top
        scores[c, ROWS:] = bottom
        grads[c] = nt_dot(load(1, c), up_rows[...])
        row_max = jnp.maximum(row_max, jnp.max(jnp.maximum(top, bottom), axis=0, keepdims=True))
    row_sum = jnp.zeros((1, WIDE), F32)
    inner = jnp.zeros((1, WIDE), F32)
    for c in range(CHUNKS):
        p = jnp.exp2(scores[c] - row_max)
        scores[c] = p
        row_sum = row_sum + jnp.sum(p, axis=0, keepdims=True)
        inner = inner + jnp.sum(p * grads[c], axis=0, keepdims=True)
    inverse = 1.0 / row_sum
    delta = inner * inverse
    dq_t = jnp.zeros((HEAD, WIDE), F32)
    for c in range(CHUNKS):
        probs = scores[c] * inverse
        score_grad = (probs * (grads[c] - delta)).astype(BF16)
        dv = jnp.dot(probs.astype(BF16), up_rows[...], preferred_element_type=F32)
        dk = jnp.dot(score_grad, q_rows[...], preferred_element_type=F32) * SCALE
        for half in range(2):
            span = slice(half * ROWS, (half + 1) * ROWS)
            parts[i * LISTED + 2 * c + half, 0] = dk[span]
            parts[i * LISTED + 2 * c + half, 1] = dv[span]
        dq_t = dq_t + lax.dot_general(
            load(0, c), score_grad, (((0,), (0,)), ((), ())), preferred_element_type=F32
        )
    dq_t = dq_t * SCALE
    for g in range(GROUP):
        span = slice(g * HEAD, (g + 1) * HEAD)
        dq_u[i, :, span] = dq_t[:, span].T.astype(BF16)


def step_kernel(
    queries, keys, values, grad_a, grad_b, imports, ids,
    dq_out_a, dq_out_b, kv_out,
    q_a, q_b, up_a, up_b, kv_a, kv_b, arrived, passing, dq_u_a, dq_u_b, dkv_a, dkv_b,
    relay_a, relay_b, landed_a, landed_b, summed_a, summed_b, total_a, total_b,
    scores, grads, parts, q_rows, up_rows,
    slots, where_part, counts,
    wide_send, wide_recv, kv_send, kv_recv, z_send, z_recv, local_in,
    hand_send, hand_recv, pass_recv, dq_send, dq_recv, r_send, r_recv, s_send, s_recv, o_send, o_recv, local_out,
):
    y, z = place()
    pipe = lax.axis_index("pipe")
    last = lax.axis_size("pipe") - 1
    edge = (last + 1) // 2
    spread_hand = edge == 2 * NY
    up, down = at_ctx(y, z + 1), at_ctx(y, z + NZ - 1)
    before, after = lax.rem(z + NZ - 1, NZ), lax.rem(z + 1, NZ)
    across = lax.rem(z + 2, NZ)
    kvs = (kv_a, kv_b)
    wide_src = (queries.at[0, 0], grad_a.at[0], queries.at[1, 0], grad_b.at[0])
    wide_dst = (q_a, up_a, q_b, up_b)
    kv_copies, kv_own, wide_copies, wide_own = {}, {}, {}, {}
    for m in range(2):
        for part, source in enumerate((keys, values)):
            kv_own[m, part] = pltpu.make_async_copy(
                source.at[m, 0, :, cols(y, HEAD)], kvs[m].at[z, part, y],
                local_in.at[2 * m + part],
            )
            kv_own[m, part].start()
    for w in range(4):
        wide_own[w] = pltpu.make_async_copy(
            wide_src[w].at[:, cols(y, WIDE)], wide_dst[w].at[y], local_in.at[4 + w]
        )
        wide_own[w].start()

    def z_copy(m, to_up, index, part, owner, piece):
        ref = kvs[m].at[owner, part, piece]
        where = ((m * 2 + to_up) * 3 + index) * NY + piece
        return remote(ref, ref, z_send.at[where], z_recv.at[where], up if to_up else down)

    def z_first(to_up, part):
        where = (to_up * 3 + part) * NY + y
        return remote(
            (keys, values)[part].at[0, 0, :, cols(y, HEAD)], kv_a.at[z, part, y],
            z_send.at[where], z_recv.at[where], up if to_up else down,
        )

    def spread_piece(m, piece):
        for to_up, part in ((1, 0), (0, 1), (1, 1), (0, 0)):
            z_copy(m, to_up, part, part, z, piece).start()

    barrier = pltpu.get_barrier_semaphore()
    peers = [at_ctx(y + d, z) for d in range(1, NY)] + [up, down]
    for peer in peers:
        pl.semaphore_signal(barrier, inc=1, device_id=peer, device_id_type=MESH)

    @pl.when(pipe < last)
    def _():
        pl.semaphore_signal(barrier, inc=1, device_id={"pipe": pipe + 1}, device_id_type=MESH)

    callers = len(peers) + jnp.where(pipe > 0, 1, 0)
    if spread_hand:
        @pl.when(pipe == edge - 1)
        def _():
            for r in range(1, edge):
                pl.semaphore_signal(
                    barrier, inc=1, device_id={"pipe": edge + r}, device_id_type=MESH
                )

        @pl.when(pipe > edge)
        def _():
            pl.semaphore_signal(barrier, inc=1, device_id={"pipe": edge}, device_id_type=MESH)

        callers = callers + jnp.where(pipe > edge, 1, 0) + jnp.where(pipe == edge, edge - 1, 0)
    pl.semaphore_wait(barrier, callers)

    def start_kv(m):
        for d in range(1, NY):
            there = lax.rem(y + d, NY)
            for part, source in enumerate((keys, values)):
                index = (m * 2 + part) * 3 + d - 1
                kv_copies[m, part, d] = remote(
                    source.at[m, 0, :, cols(there, HEAD)], kvs[m].at[z, part, y],
                    kv_send.at[index], kv_recv.at[index], at_ctx(y + d, z),
                )
                kv_copies[m, part, d].start()

    def start_wide(w):
        for d in range(1, NY):
            there = lax.rem(y + d, NY)
            index = w * 3 + d - 1
            wide_copies[w, d] = remote(
                wide_src[w].at[:, cols(there, WIDE)], wide_dst[w].at[y],
                wide_send.at[index], wide_recv.at[index], at_ctx(y + d, z),
            )
            wide_copies[w, d].start()

    for to_up, part in ((1, 0), (0, 1), (1, 1), (0, 0)):
        z_first(to_up, part).start()
    start_kv(0)
    start_kv(1)
    start_wide(0)
    start_wide(1)
    start_wide(2)
    start_wide(3)

    def spread(m):
        for d in (1, 3, 2):
            for part in range(2):
                kv_copies[m, part, NY - d].wait_recv()
            spread_piece(m, lax.rem(y + d, NY))

    def forward(m, order=(0, 1, 3, 2)):
        for d in order:
            piece = lax.rem(y + d, NY)
            for to_up, part, owner in ((1, 0, before), (0, 1, after)):
                z_copy(m, to_up, part, part, z, piece).wait_recv()
                z_copy(m, to_up, 2, part, owner, piece).start()

    def wait_spread(m):
        if m == 0:
            for part in range(2):
                kv_own[0, part].wait()
        for b in range(NY):
            z_copy(m, 1, 1, 1, z, b).wait_recv()
            z_copy(m, 0, 0, 0, z, b).wait_recv()
            z_copy(m, 1, 2, 0, across, b).wait_recv()
            z_copy(m, 0, 2, 1, across, b).wait_recv()
        for w in (2 * m, 2 * m + 1):
            wide_own[w].wait()
            for d in range(1, NY):
                wide_copies[w, d].wait_recv()

    def hand(i, h):
        span = pl.ds(h * HALF, HALF)
        return remote(
            dq_u_a.at[i, span], arrived.at[i, span], hand_send.at[2 * i + h],
            hand_recv.at[2 * i + h], {"pipe": lax.rem(pipe + last, last + 1)},
        )

    def to_relay(i, h):
        return remote(
            dq_u_a.at[i, pl.ds(h * HALF, HALF)], passing, hand_send.at[2 * i + h],
            pass_recv.at[0], {"pipe": lax.rem(edge + lax.rem(2 + 2 * i + h, edge), last + 1)},
        )

    piece = lax.rem(pipe + 2 * edge - 2, 2 * NY)

    def from_relay():
        i, h = piece // 2, lax.rem(piece, 2)
        return remote(
            passing, arrived.at[i, pl.ds(pl.multiple_of(h * HALF, HALF), HALF)],
            hand_send.at[2 * NY], hand_recv.at[piece], {"pipe": edge - 1},
        )

    def hand_over(i):
        direct = (pipe > 0) & (pipe != edge) if spread_hand else pipe > 0

        @pl.when(direct)
        def _():
            hand(i, 0).start()
            hand(i, 1).start()

        if spread_hand:
            @pl.when(pipe == edge)
            def _():
                @pl.when(i < NY - 1)
                def _():
                    to_relay(i, 0).start()

                @pl.when(i == NY - 1)
                def _():
                    hand(i, 0).start()

                to_relay(i, 1).start()

    def pass_on(i):
        if spread_hand:
            @pl.when((pipe > edge) & (piece // 2 + 1 == i))
            def _():
                to_relay(0, 0).wait_recv()
                from_relay().start()

    def hand_end():
        direct = (pipe > 0) & (pipe <= edge) if spread_hand else pipe > 0

        @pl.when(direct)
        def _():
            for i in range(NY):
                hand(i, 0).wait_send()
                hand(i, 1).wait_send()

        if spread_hand:
            @pl.when(pipe > edge)
            def _():
                for i in range(NY):
                    hand(i, 0).wait_send()
                    hand(i, 1).wait_send()
                from_relay().wait_send()

    def dq_copy(m, sender, target):
        return remote(
            (dq_u_a, dq_u_b)[m].at[target],
            (dq_out_a, dq_out_b)[m].at[0, :, cols(sender, WIDE)],
            dq_send.at[m * NY + target], dq_recv.at[m * NY + sender], at_ctx(target, z),
        )

    def dq_own(m):
        return pltpu.make_async_copy(
            (dq_u_a, dq_u_b)[m].at[y], (dq_out_a, dq_out_b)[m].at[0, :, cols(y, WIDE)],
            local_out.at[m],
        )

    def return_dq(m, i):
        @pl.when(i == y)
        def _():
            dq_own(m).start()

        @pl.when(i != y)
        def _():
            dq_copy(m, y, i).start()

    def combine(m, dkv, part):
        def one(slot, nothing):
            places = [where_part[(m * NY + i) * BLOCKS + slot] for i in range(NY)]
            value = parts[places[0], part]
            for at in places[1:]:
                value = value + parts[at, part]
            dkv[lax.rem(slot, NZ), part, slot // NZ] = value.astype(BF16)
            return nothing

        lax.fori_loop(0, BLOCKS, one, 0)

    relays, landeds, totals, dkvs = (
        (relay_a, relay_b), (landed_a, landed_b), (total_a, total_b), (dkv_a, dkv_b),
    )

    def r_copy(m, index):
        relay, landed, dkv = relays[m], landeds[m], dkvs[m]
        src, dst, peer = (
            (dkv.at[across, 0], relay.at[0], up),
            (dkv.at[across, 1], relay.at[1], down),
            (dkv.at[after, 1], landed.at[0], up),
            (dkv.at[before, 0], landed.at[1], down),
        )[index]
        return remote(src, dst, r_send.at[m * 4 + index], r_recv.at[m * 4 + index], peer)

    def s_copy(m, part, turn):
        where = (m * 2 + part) * NY + turn
        return remote(
            totals[m].at[part, turn], (summed_a, summed_b)[m].at[part, turn],
            s_send.at[where], s_recv.at[where], (up, down)[part],
        )

    def reduce_start(m):
        combine(m, dkvs[m], 1)
        r_copy(m, 1).start()
        r_copy(m, 2).start()
        combine(m, dkvs[m], 0)
        r_copy(m, 0).start()
        r_copy(m, 3).start()

    def reduce_relay(m):
        relay, total, dkv = relays[m], totals[m], dkvs[m]
        r_copy(m, 0).wait_recv()
        r_copy(m, 1).wait_recv()
        for turn, d in enumerate((2, 1, 3, 0)):
            piece = lax.rem(y + d, NY)
            for part, owner in ((0, after), (1, before)):
                total[part, turn] = (
                    relay[part, piece].astype(F32) + dkv[owner, part, piece].astype(F32)
                ).astype(BF16)
                s_copy(m, part, turn).start()

    def o_copy(m, part, sender, target, turn=0):
        return remote(
            totals[m].at[2 + part, turn],
            kv_out.at[m, 0, :, cols(KEY_VALUE_HEADS * part + sender, HEAD)],
            o_send.at[(m * 2 + part) * NY + target], o_recv.at[(m * 2 + part) * NY + sender],
            at_ctx(target, z),
        )

    def o_own(m, part):
        return pltpu.make_async_copy(
            totals[m].at[2 + part, NY - 1],
            kv_out.at[m, 0, :, cols(KEY_VALUE_HEADS * part + y, HEAD)],
            local_out.at[2 + 2 * m + part],
        )

    def reduce_end(m):
        landed, total, dkv, summed = landeds[m], totals[m], dkvs[m], (summed_a, summed_b)[m]
        r_copy(m, 2).wait_recv()
        r_copy(m, 3).wait_recv()
        for turn, d in enumerate((2, 1, 3, 0)):
            piece = lax.rem(y + d, NY)
            for part in range(2):
                s_copy(m, part, turn).wait_recv()
                total[2 + part, turn] = (
                    dkv[z, part, piece].astype(F32)
                    + landed[1 - part, piece].astype(F32)
                    + summed[part, turn].astype(F32)
                ).astype(BF16)
                if d:
                    o_copy(m, part, y, piece, turn).start()
                else:
                    o_own(m, part).start()

    key_place = lax.broadcasted_iota(jnp.int32, (ROWS, WIDE), 0)
    row_place = lax.rem(lax.broadcasted_iota(jnp.int32, (ROWS, WIDE), 1), ROWS)
    parts[NY * LISTED] = jnp.zeros_like(parts[NY * LISTED])
    spread(0)
    list_blocks(0, z, imports, ids, slots, where_part, counts)
    forward(0)
    for part in range(2):
        kv_own[1, part].wait()
    spread_piece(1, y)
    spread(1)
    list_blocks(1, z, imports, ids, slots, where_part, counts)
    wait_spread(0)

    def turn_a(i, nothing):
        for g in range(GROUP):
            span = slice(g * HEAD, (g + 1) * HEAD)
            q_rows[span, :] = q_a[i, :, span]
            up_rows[span, :] = up_a[i, :, span]
        attend_block(0, i, key_place, row_place, slots, counts, kv_a, q_rows, up_rows, scores,
                     grads, parts, dq_u_a)

        hand_over(i)
        return_dq(0, i)
        pass_on(i)

        @pl.when(i == FORWARD_AT - 1)
        def _():
            forward(1, (0, 1))

        @pl.when(i == FORWARD_AT)
        def _():
            forward(1, (3, 2))

        return nothing

    lax.fori_loop(0, NY, turn_a, 0)
    pass_on(NY)
    reduce_start(0)
    wait_spread(1)

    def turn_b(i, nothing):
        @pl.when(pipe < last)
        def _():
            hand(i, 0).wait_recv()
            hand(i, 1).wait_recv()

        for g in range(GROUP):
            span = slice(g * HEAD, (g + 1) * HEAD)
            q_rows[span, :] = q_b[i, :, span]
            came = jnp.where(pipe < last, arrived[i, :, span].astype(F32), 0.0)
            up_rows[span, :] = (up_b[i, :, span].astype(F32) + came).astype(BF16)
        attend_block(1, i, key_place, row_place, slots, counts, kv_b, q_rows, up_rows, scores,
                     grads, parts, dq_u_b)
        return_dq(1, i)

        @pl.when(i == RELAY_AT)
        def _():
            reduce_relay(0)

        return nothing

    lax.fori_loop(0, NY, turn_b, 0)
    reduce_start(1)
    reduce_end(0)
    reduce_relay(1)
    reduce_end(1)

    for m in range(2):
        dq_own(m).wait()
        for d in range(1, NY):
            other = lax.rem(y + d, NY)
            dq_copy(m, other, y).wait_recv()
            dq_copy(m, y, other).wait_send()
            for part in range(2):
                o_copy(m, part, other, y).wait_recv()
                o_copy(m, part, y, other).wait_send()
        for part in range(2):
            o_own(m, part).wait()
        for index in range(4):
            r_copy(m, index).wait_send()
        for b in range(NY):
            for part in range(2):
                s_copy(m, part, b).wait_send()
            for to_up, part, owner in ((1, 0, before), (0, 1, after)):
                z_copy(m, to_up, 0, 0, z, b).wait_send()
                z_copy(m, to_up, 1, 1, z, b).wait_send()
                z_copy(m, to_up, 2, part, owner, b).wait_send()
    for copy in list(kv_copies.values()) + list(wide_copies.values()):
        copy.wait_send()

    hand_end()


def finish_kernel(*refs):
    sources, targets, held, sem_in, sem_out = refs[:3], refs[3:6], refs[6:9], refs[9], refs[10]
    incoming = [
        pltpu.make_async_copy(source, buffer, sem_in.at[k])
        for k, (source, buffer) in enumerate(zip(sources, held))
    ]
    outgoing = [
        pltpu.make_async_copy(buffer, target, sem_out.at[k])
        for k, (buffer, target) in enumerate(zip(held, targets))
    ]
    for copy in incoming:
        copy.start()
    for copy, later in zip(incoming, outgoing):
        copy.wait()
        later.start()
    for copy in outgoing:
        copy.wait()


def finish(*arrays):
    whole = pl.BlockSpec(memory_space=pl.ANY)
    return pl.pallas_call(
        finish_kernel,
        out_shape=tuple(jax.ShapeDtypeStruct(a.shape, a.dtype) for a in arrays),
        in_specs=[whole] * 3,
        out_specs=(whole,) * 3,
        scratch_shapes=[pltpu.VMEM(a.shape, a.dtype) for a in arrays]
        + [pltpu.SemaphoreType.DMA((3,)), pltpu.SemaphoreType.DMA((3,))],
        name="finish",
    )(*arrays)


def on_device(queries, keys, values, grad_a, grad_b, imports, block_ids):
    wide = pltpu.VMEM((NY, ROWS, WIDE), BF16)
    pair = pltpu.VMEM((NZ, 2, NY, ROWS, HEAD), BF16)
    column = lambda n: pltpu.VMEM((n, NY, ROWS, HEAD), BF16)
    dma = lambda n: pltpu.SemaphoreType.DMA((n,))
    chunk = pltpu.VMEM((CHUNKS, 2 * ROWS, WIDE), F32)
    rows = pltpu.VMEM((WIDE, HEAD), BF16)
    whole = pl.BlockSpec(memory_space=pl.ANY)
    smem = pl.BlockSpec(memory_space=pltpu.SMEM)
    outputs = pl.pallas_call(
        step_kernel,
        out_shape=(
            jax.ShapeDtypeStruct(grad_a.shape, BF16),
            jax.ShapeDtypeStruct(grad_b.shape, BF16),
            jax.ShapeDtypeStruct((2, 1, ROWS, 2 * KEY_VALUE_HEADS * HEAD), BF16),
        ),
        in_specs=[whole] * 5 + [smem, smem],
        out_specs=(whole,) * 3,
        scratch_shapes=[
            wide, wide, wide, wide, pair, pair, wide, pltpu.VMEM((HALF, WIDE), BF16),
            wide, wide, pair, pair,
            column(2), column(2), column(2), column(2), column(2), column(2), column(4), column(4),
            chunk, chunk, pltpu.VMEM((NY * LISTED + 1, 2, ROWS, HEAD), F32), rows, rows,
            pltpu.SMEM((2 * NY * LISTED,), jnp.int32),
            pltpu.SMEM((2 * NY * BLOCKS,), jnp.int32),
            pltpu.SMEM((2 * NY,), jnp.int32),
            dma(12), dma(12), dma(12), dma(12), dma(48), dma(48), dma(8),
            dma(9), dma(8), dma(1), dma(8), dma(8), dma(8), dma(8), dma(16), dma(16), dma(16), dma(16), dma(6),
        ],
        compiler_params=pltpu.CompilerParams(
            collective_id=0, has_side_effects=True, vmem_limit_bytes=60 * 1024 * 1024
        ),
        name="step",
    )(queries, keys, values, grad_a, grad_b, imports, block_ids)
    return finish(*outputs)


def solution(mesh):
    return jax.shard_map(
        on_device,
        mesh=mesh,
        in_specs=(
            P(None, "pipe", "ctx", None),
            P(None, "pipe", "ctx", None),
            P(None, "pipe", "ctx", None),
            P("pipe", "ctx", None),
            P("pipe", "ctx", None),
            P(None, "pipe", None, None),
            P(None, "pipe", None),
        ),
        out_specs=(P("pipe", "ctx", None), P("pipe", "ctx", None), P(None, "pipe", "ctx", None)),
        check_vma=False,
    )
```
